256 devices in a mesh: batch: 4 (over z_lo, core), row: 4 (over x), col: 16 (over y, z_hi).
Axes of the slice: x: 4, y: 4, z: 8 (z_hi: 4, z_lo: 2; z = z_hi * 2 + z_lo), core: 2. Of those that a mesh axis runs over, the one named last changes fastest.
Arguments:
- embeddings: bfloat16 [512, 128, 512], P('batch', 'col', 'row'), may hold values from -170 to 170
- projection: bfloat16 [512, 32], replicated, may hold values from -0.25 to 0.25
- w_in: bfloat16 [16384, 2048], P('row', 'col'), may hold values from -0.046875 to 0.046875
- bias: float32 [2048], P('col'), may hold values from -3 to 3
- w_out: bfloat16 [2048, 128, 512], P(None, 'col', 'row'), may hold values from -0.125 to 0.125
- cotangent: bfloat16 [512, 128, 512], P('batch', 'col', 'row'), may hold values from -0.1796875 to 0.1796875
Outputs:
- mixed: bfloat16 [512, 128, 512], P('batch', 'col', 'row')
- grad_out: float32 [2048, 128, 512], P('batch', 'col', 'row')
- grad_in: float32 [16384, 2048], P('row', 'col')
- grad_bias: float32 [2048], P('col')
- grad_proj: float32 [512, 32], P('row')
The draws below stay inside these ranges and needn't reach their ends.
All inputs are finite; a program needn't handle non-finite values.
Results may differ from the reference program's by a relative error of at most 0.006.
Values may be sent and summed in bfloat16 or wider, within the bound.
A program may use at most 128 MiB of HBM per device.

```python
import jax
import jax.numpy as jnp
from jax import lax

N_EMB = 512
D = 128
RANK = 32
HID = 2048
TOKENS = 512


def draw_embeddings(key, part):
    key = jax.random.fold_in(key, 7)
    key_vals, key_emb, key_tok = jax.random.split(key, 3)
    rising = 3.0 ** (jnp.arange(N_EMB, dtype=jnp.float32) / N_EMB)
    values = jnp.clip(jax.random.normal(key_vals, (TOKENS, D, N_EMB), jnp.float32), -4.0, 4.0)
    emb_scale = rising * jnp.exp(jax.random.uniform(key_emb, (N_EMB,), jnp.float32, 0.0, jnp.log(10.0 / 3.0)))
    tok_scale = jnp.exp(jax.random.uniform(key_tok, (TOKENS,), jnp.float32, 0.0, jnp.log(3.0)))
    return (values * emb_scale[None, None, :] * tok_scale[:, None, None]).astype(jnp.bfloat16)


def steps_of(stream_key, shape, shards, smallest, top_value):
    loudness = 1.0
    for axis_at, blocks in shards:
        draws = jax.random.uniform(jax.random.fold_in(jax.random.fold_in(stream_key, 6), axis_at), (blocks,), jnp.float32, smallest / len(shards), top_value / len(shards))
        loudness = loudness * jnp.repeat(jnp.exp(draws), shape[axis_at] // blocks).reshape((-1,) + (1,) * (len(shape) - 1 - axis_at))
    return loudness


def normal_values(stream_key, extent, spread, limit, pieces=(), held_as=jnp.bfloat16):
    drawn = spread * jax.random.normal(stream_key, extent, jnp.float32)
    if pieces:
        drawn = drawn * steps_of(stream_key, extent, pieces, -0.22, 0.18)
    return jnp.clip(drawn, -limit, limit).astype(held_as)


def setup_inputs(seed: int = 0) -> dict:
    key_list = jax.random.split(jax.random.key(seed), 7)
    embeddings = draw_embeddings(jax.random.fold_in(key_list[6], 71), 0)
    projection = normal_values(key_list[1], (N_EMB, RANK), N_EMB ** -0.5, 0.25)
    w_in = normal_values(key_list[2], (N_EMB * RANK, HID), (N_EMB * RANK) ** -0.5, 0.046875, ((0, 4), (1, 16)))
    bias = normal_values(key_list[3], (HID,), 0.5, 3.0, ((0, 16),), jnp.float32)
    w_out = normal_values(key_list[4], (HID, D, N_EMB), HID ** -0.5, 0.125, ((1, 16), (2, 4)))
    cotangent = normal_values(key_list[5], (TOKENS, D, N_EMB), 0.03, 0.1796875, ((0, 4), (1, 16), (2, 4)))
    return {"embeddings": embeddings, "projection": projection, "w_in": w_in, "bias": bias, "w_out": w_out, "cotangent": cotangent}


epsilon = 1e-06

def reference(embeddings, projection, w_in, bias, w_out, cotangent):
    highest = lax.Precision.HIGHEST
    emb_float = embeddings.astype(jnp.float32)
    folded = jnp.einsum('bde,ek->bdk', emb_float, projection.astype(jnp.float32), precision=highest)
    interact = jnp.einsum('bde,bdk->bek', emb_float, folded, precision=highest)
    inv_rms = lax.rsqrt(lax.optimization_barrier(jnp.mean(interact * interact, axis=(1, 2))) + epsilon)[:, None, None]
    normed = interact * inv_rms
    activated = normed.astype(jnp.bfloat16).reshape(TOKENS, N_EMB * RANK)
    preact = jnp.dot(activated, w_in, preferred_element_type=jnp.float32) + bias
    hidden = jax.nn.silu(preact).astype(jnp.bfloat16)
    flat_out = w_out.reshape(HID, D * N_EMB)
    mixed = jnp.dot(hidden, flat_out, preferred_element_type=jnp.float32).astype(jnp.bfloat16).reshape(TOKENS, D, N_EMB)
    cot_rows = cotangent.reshape(TOKENS, D * N_EMB)
    d_hidden = lax.dot_general(cot_rows, flat_out, (((1,), (1,)), ((), ())), preferred_element_type=jnp.float32)
    sigmoid_pre = jax.nn.sigmoid(preact)
    d_preact = d_hidden * sigmoid_pre * (1.0 + preact * (1.0 - sigmoid_pre))
    d_pre_b = d_preact.astype(jnp.bfloat16)
    grad_out = lax.dot_general(hidden, cot_rows, (((0,), (0,)), ((), ())), preferred_element_type=jnp.float32).reshape(HID, D, N_EMB)
    grad_in = lax.dot_general(activated, d_pre_b, (((0,), (0,)), ((), ())), preferred_element_type=jnp.float32)
    grad_bias = lax.optimization_barrier(jnp.sum(d_preact, axis=0))
    d_act = lax.dot_general(d_pre_b, w_in, (((1,), (1,)), ((), ())), preferred_element_type=jnp.float32).reshape(TOKENS, N_EMB, RANK)
    inner_term = lax.optimization_barrier(jnp.mean(d_act * normed, axis=(1, 2)))[:, None, None]
    d_inter = (inv_rms * (d_act - normed * inner_term)).astype(jnp.bfloat16)
    back_fold = jnp.einsum('bek,bde->bdk', d_inter.astype(jnp.float32), emb_float, precision=highest)
    grad_proj = jnp.einsum('bde,bdk->ek', emb_float, back_fold, precision=highest)
    return (mixed, grad_out, grad_in, grad_bias, grad_proj)
```

```python
import jax
import jax.numpy as jnp
from jax import lax
from jax.sharding import PartitionSpec as P

epsilon = 1e-06
bf16 = jnp.bfloat16
f32 = jnp.float32


def swap(tiles, axis):
    return lax.all_to_all(tiles, axis, 0, 0, tiled=True)


def everyone(array, axis):
    size = lax.axis_size(axis)
    return swap(jnp.broadcast_to(array[None], (size, *array.shape)), axis)


def contract_last(left, right):
    return lax.dot_general(left, right, (((1,), (1,)), ((), ())), preferred_element_type=f32)


def contract_first(left, right):
    return lax.dot_general(left, right, (((0,), (0,)), ((), ())), preferred_element_type=f32)


def summed(tiles):
    return jnp.sum(tiles.astype(f32), axis=0)


def local(embeddings, projection, w_in, bias, w_out, cotangent):
    highest = lax.Precision.HIGHEST
    toks, feat, embs = embeddings.shape
    rank = projection.shape[1]
    rows, cols, batches = lax.axis_size("row"), lax.axis_size("col"), lax.axis_size("batch")
    own = toks // (rows * cols)
    hid = w_out.shape[0]
    hid_local = w_in.shape[1]
    flat_out = w_out.reshape(hid, feat * embs)
    cot_rows = cotangent.reshape(toks, feat * embs)
    partial = contract_last(cot_rows, flat_out).astype(bf16)
    partial = jnp.moveaxis(partial.reshape(toks, cols, hid_local), 1, 0)
    d_cols = summed(swap(partial, "col"))
    d_hidden = jnp.sum(everyone(d_cols, "row"), axis=0)
    every_cot = everyone(cot_rows, "batch")
    emb = swap(embeddings.reshape(cols * rows, own, feat, embs), ("col", "row"))
    emb = emb.reshape(cols, rows, own, feat, embs).transpose(2, 0, 3, 1, 4)
    emb = emb.reshape(own, cols * feat, rows * embs)
    emb_float = emb.astype(f32)
    folded = jnp.einsum("bde,ek->bdk", emb, projection, preferred_element_type=f32)
    interact = jnp.einsum("bde,bdk->bek", emb_float, folded, precision=highest)
    count = rows * embs * rank
    inv_rms = lax.rsqrt(jnp.sum(interact * interact, axis=(1, 2)) / count + epsilon)[:, None, None]
    normed = interact * inv_rms
    activated = normed.astype(bf16).reshape(own, rows, embs * rank)
    act = swap(jnp.moveaxis(activated, 1, 0), "row").reshape(rows * own, embs * rank)
    act = everyone(act, "col").reshape(toks, embs * rank)
    pre = jnp.dot(act, w_in, preferred_element_type=f32)
    preact = jnp.sum(everyone(pre, "row"), axis=0) + bias
    hidden = jax.nn.silu(preact).astype(bf16)
    sig = jax.nn.sigmoid(preact)
    d_preact = d_hidden * sig * (1.0 + preact * (1.0 - sig))
    d_pre_b = d_preact.astype(bf16)
    d_part = contract_last(d_pre_b, w_in).astype(bf16).reshape(cols, rows * own, embs * rank)
    d_rows = summed(swap(d_part, "col")).astype(bf16)
    d_act = swap(d_rows.reshape(rows, own, embs * rank), "row").astype(f32)
    d_act = jnp.moveaxis(d_act, 0, 1).reshape(own, rows * embs, rank)
    inner = (jnp.sum(d_act * normed, axis=(1, 2)) / count)[:, None, None]
    d_inter = (inv_rms * (d_act - normed * inner)).astype(bf16)
    back_fold = jnp.einsum("bek,bde->bdk", d_inter, emb, preferred_element_type=f32)
    part_proj = jnp.einsum("bde,bdk->ek", emb_float, back_fold, precision=highest)
    part_proj = jnp.sum(swap(part_proj.reshape(rows, embs, rank), "row"), axis=0)
    everywhere = ("batch", "col")
    group = batches * cols
    share = jnp.sum(swap(part_proj.reshape(group, -1), everywhere), axis=0)
    grad_proj = everyone(share, everywhere).reshape(embs, rank)
    hidden_all = everyone(hidden, "col")
    mixed = jnp.dot(
        jnp.moveaxis(hidden_all, 0, 1).reshape(toks, hid), flat_out, preferred_element_type=f32
    )
    mixed = mixed.astype(bf16).reshape(toks, feat, embs)
    by_batch = hidden_all.reshape(batches, cols // batches, toks, hid_local)
    own_hidden = swap(by_batch, "batch")
    own_hidden = own_hidden.transpose(0, 2, 1, 3).reshape(batches * toks, hid // batches)
    grad_out = contract_first(own_hidden, every_cot.reshape(batches * toks, feat * embs))
    grad_out = grad_out.reshape(hid // batches, feat, embs)
    in_part = contract_first(act, d_pre_b).astype(bf16)
    quarter = summed(swap(in_part.reshape(batches, -1, hid_local), "batch")).astype(bf16)
    grad_in = everyone(quarter, "batch").astype(f32).reshape(embs * rank, hid_local)
    grad_bias = jnp.sum(everyone(jnp.sum(d_preact, axis=0), "batch"), axis=0)
    return (mixed, grad_out, grad_in, grad_bias, grad_proj)


def solution(mesh):
    placed = (
        P("batch", "col", "row"),
        P(),
        P("row", "col"),
        P("col"),
        P(None, "col", "row"),
        P("batch", "col", "row"),
    )
    return jax.shard_map(
        local,
        mesh=mesh,
        in_specs=placed,
        out_specs=(
            P("batch", "col", "row"),
            P("batch", "col", "row"),
            P("row", "col"),
            P("col"),
            P("row", None),
        ),
        check_vma=False,
    )
```

```python
import functools

import jax
import jax.numpy as jnp
from jax import lax
from jax.experimental import pallas as pl
from jax.experimental.pallas import tpu as pltpu
from jax.sharding import PartitionSpec as P

epsilon = 1e-06
bf16 = jnp.bfloat16
f32 = jnp.float32
MESH = pl.DeviceIdType.MESH
VMEM = pltpu.VMEM
DMA = pltpu.SemaphoreType.DMA


def swap(tiles, axis):
    return lax.all_to_all(tiles, axis, 0, 0, tiled=True)


def everyone(array, axis):
    size = lax.axis_size(axis)
    return swap(jnp.broadcast_to(array[None], (size, *array.shape)), axis)


def contract_last(left, right):
    return lax.dot_general(left, right, (((1,), (1,)), ((), ())), preferred_element_type=f32)


def contract_first(left, right):
    return lax.dot_general(left, right, (((0,), (0,)), ((), ())), preferred_element_type=f32)


def dot(left, right):
    return jnp.dot(left, right, preferred_element_type=f32)


def summed(tiles):
    return jnp.sum(tiles.astype(f32), axis=0)


def send(src, dst, send_sem, recv_sem, **place):
    copy = pltpu.make_async_remote_copy(
        src_ref=src, dst_ref=dst, send_sem=send_sem, recv_sem=recv_sem,
        device_id=place, device_id_type=MESH,
    )
    copy.start()


def arrived(ref, sem):
    pltpu.make_async_copy(ref, ref, sem).wait()


def split(value):
    high = value.astype(bf16)
    return high, (value - high.astype(f32)).astype(bf16)


def places():
    me = {axis: lax.axis_index(axis) for axis in ("batch", "row", "col")}
    i, r, c = me["batch"], me["row"], me["col"]
    y = c // 4
    z = c - y * 4
    sibling = i + 1 - 2 * lax.rem(i, 2)
    across = lax.rem(i + 2, 4)
    return i, r, c, y, z, sibling, across


def forward_kernel(
    emb, proj, w_in, bias, d_part, cot,
    gathered, hidden, d_pre, d_pre_b, normed, inv, own_emb, every_cot,
    folds, to_row, from_row, d_y, d_z_out, d_z, d_x, pre_x,
    emb_send, emb_recv, row_send, row_recv, gather_send, gather_recv,
    dy_send, dy_recv, dz_send, dz_recv, dx_send, dx_recv, pre_send, pre_recv,
    cot_send, cot_recv, own_sem,
):
    i, r, c, y, z, sibling, across = places()
    me = c * 4 + r
    barrier = pltpu.get_barrier_semaphore()

    def greet(k, _):
        peer = lax.rem(me + k, 64)
        pl.semaphore_signal(
            barrier, inc=1, device_id={"col": peer // 4, "row": lax.rem(peer, 4)},
            device_id_type=MESH,
        )
        return 0

    lax.fori_loop(1, 64, greet, 0)
    for other in (sibling, across):
        pl.semaphore_signal(barrier, inc=1, device_id={"batch": other}, device_id_type=MESH)
    pl.semaphore_wait(barrier, 65)

    def give(k, _):
        peer = lax.rem(me + k, 64)
        send(
            emb.at[peer], own_emb.at[r, :, c], emb_send, emb_recv,
            col=peer // 4, row=lax.rem(peer, 4),
        )
        return 0

    keep = pltpu.make_async_copy(emb.at[me], own_emb.at[r, :, c], emb_recv)
    keep.start()
    lax.fori_loop(1, 64, give, 0)
    for k in (1, 2, 3):
        to = lax.rem(y + k, 4)
        send(
            d_part.at[:, pl.ds(pl.multiple_of(to * 512, 512), 512)], d_y.at[y],
            dy_send, dy_recv.at[y], col=to * 4 + z,
        )
    lanes = lax.broadcasted_iota(jnp.int32, (32, 128), 1)
    ranks = lax.broadcasted_iota(jnp.int32, (32, 128), 0)
    spread = (lax.rem(lanes, 32) == ranks).astype(f32).astype(bf16)
    wide = dot(proj[...], spread).astype(bf16)
    block = lax.broadcasted_iota(jnp.int32, (128, 128), 1) // 32
    at = lax.broadcasted_iota(jnp.int32, (256, 256), 0)
    of = lax.broadcasted_iota(jnp.int32, (256, 256), 1)
    source = lax.rem(at, 8) // 2 * 64 + lax.rem(at, 2) * 32 + at // 8
    order = (of == source).astype(f32).astype(bf16)
    arrived(own_emb, emb_recv)
    for s in range(2):
        tiles = [own_emb[q, s].reshape(128, 128) for q in range(4)]
        folded = sum(dot(tiles[q], wide[q * 128 : (q + 1) * 128]) for q in range(4))
        high, low = split(folded)
        for q in range(4):
            folds[q * 128 : (q + 1) * 128, :] = contract_first(tiles[q], high) + contract_first(
                tiles[q], low
            )
        inter = jnp.zeros((128, 128), f32)
        for j in range(4):
            inter = jnp.where(block == j, folds[pl.ds(j, 128, stride=4), :], inter)
        total = jnp.sum(jnp.sum(inter * inter, axis=0, keepdims=True), axis=1, keepdims=True)
        scale = lax.rsqrt(total / (512 * 32) + epsilon)
        norm = inter * scale
        normed[s] = norm
        inv[s] = jnp.broadcast_to(scale, (8, 128))
        for q in range(4):
            to_row[q, s] = norm[q * 32 : (q + 1) * 32].astype(bf16)
    from_row[r] = to_row[r]
    for k in (1, 2, 3):
        to = lax.rem(r + k, 4)
        send(to_row.at[to], from_row.at[r], row_send, row_recv.at[r], row=to)
    for k in (1, 2, 3):
        f = lax.rem(y + k, 4)
        arrived(d_y.at[f], dy_recv.at[f])
    d_y[y] = d_part[:, pl.ds(pl.multiple_of(y * 512, 512), 512)]
    for q in range(4):
        part = d_y[0, :, q * 128 : (q + 1) * 128].astype(f32)
        for f in (1, 2, 3):
            part = part + d_y[f, :, q * 128 : (q + 1) * 128].astype(f32)
        d_z_out[q] = part.astype(bf16)
    d_z[z] = d_z_out[z]
    for k in (1, 2, 3):
        to = lax.rem(z + k, 4)
        send(d_z_out.at[to], d_z.at[z], dz_send, dz_recv.at[z], col=y * 4 + to)
    for k in (1, 2, 3):
        f = lax.rem(r + k, 4)
        arrived(from_row.at[f], row_recv.at[f])
    rows = dot(order, from_row[...].reshape(256, 128))
    gathered[:, c] = rows.reshape(32, 8, 128).astype(bf16)
    for k in (1, 2, 3):
        to = lax.rem(z + k, 4)
        send(gathered.at[:, c], gathered.at[:, c], gather_send, gather_recv.at[c], col=y * 4 + to)
    for k in (1, 2, 3):
        to = lax.rem(y + k, 4)
        send(gathered.at[:, c], gathered.at[:, c], gather_send, gather_recv.at[c], col=to * 4 + z)
    for m in (1, 2, 3):
        slot = y * 4 + lax.rem(z + m, 4)
        arrived(gathered.at[:, slot], gather_recv.at[slot])
        for k in (1, 2, 3):
            to = lax.rem(y + k, 4)
            send(
                gathered.at[:, slot], gathered.at[:, slot], gather_send, gather_recv.at[slot],
                col=to * 4 + z,
            )
    mine = pltpu.make_async_copy(cot, every_cot.at[i], own_sem)
    mine.start()
    send(cot, every_cot.at[i], cot_send, cot_recv.at[i], batch=sibling)
    send(cot, every_cot.at[i], cot_send, cot_recv.at[i], batch=across)
    for k in (1, 2, 3):
        f = lax.rem(z + k, 4)
        arrived(d_z.at[f], dz_recv.at[f])
    d_x[r] = sum(d_z[f].astype(f32) for f in range(4))
    for k in (1, 2, 3):
        to = lax.rem(r + k, 4)
        send(d_x.at[r], d_x.at[r], dx_send, dx_recv.at[r], row=to)
    for m in (1, 2, 3):
        for k in range(4):
            slot = lax.rem(y + m, 4) * 4 + k
            arrived(gathered.at[:, slot], gather_recv.at[slot])
    pre = jnp.zeros((128, 128), f32)
    for e in range(32):
        pre = pre + dot(gathered[e].reshape(128, 128), w_in[e])
    pre_x[r] = pre
    for k in (1, 2, 3):
        to = lax.rem(r + k, 4)
        send(pre_x.at[r], pre_x.at[r], pre_send, pre_recv.at[r], row=to)
    arrived(every_cot.at[across], cot_recv.at[across])
    send(every_cot.at[across], every_cot.at[across], cot_send, cot_recv.at[across], batch=sibling)
    for k in (1, 2, 3):
        f = lax.rem(r + k, 4)
        arrived(d_x.at[f], dx_recv.at[f])
    d_hidden = (d_x[0] + d_x[1]) + (d_x[2] + d_x[3])
    for k in (1, 2, 3):
        f = lax.rem(r + k, 4)
        arrived(pre_x.at[f], pre_recv.at[f])
    preact = (pre_x[0] + pre_x[1]) + (pre_x[2] + pre_x[3]) + bias[...]
    sig = 1.0 / (1.0 + jnp.exp(-preact))
    hidden[...] = (preact * sig).astype(bf16)
    d_value = d_hidden * sig * (1.0 + preact * (1.0 - sig))
    d_pre[...] = d_value
    d_pre_b[...] = d_value.astype(bf16)
    diagonal = lax.rem(sibling + 2, 4)
    arrived(every_cot.at[sibling], cot_recv.at[sibling])
    arrived(every_cot.at[diagonal], cot_recv.at[diagonal])
    mine.wait()
    arrived(emb.at[pl.ds(0, 63)], emb_send)
    arrived(d_y.at[pl.ds(0, 3)], dy_send)
    arrived(d_z.at[pl.ds(0, 3)], dz_send)
    arrived(d_x.at[pl.ds(0, 3)], dx_send)
    arrived(pre_x.at[pl.ds(0, 3)], pre_send)
    arrived(from_row.at[pl.ds(0, 3)], row_send)
    arrived(every_cot.at[pl.ds(0, 3)], cot_send)
    arrived(gathered.at[:, pl.ds(0, 15)], gather_send)


def forward(emb, proj, w_in, bias, d_part, cot):
    out = jax.ShapeDtypeStruct
    return pl.pallas_call(
        forward_kernel,
        out_shape=(
            out((32, 16, 8, 128), bf16),
            out((128, 128), bf16),
            out((128, 128), f32),
            out((128, 128), bf16),
            out((2, 128, 128), f32),
            out((2, 8, 128), f32),
            out((4, 2, 16, 8, 128), bf16),
            out((4, 128, 1024), bf16),
        ),
        in_specs=[pl.BlockSpec(memory_space=VMEM)] * 6,
        out_specs=[pl.BlockSpec(memory_space=VMEM)] * 8,
        scratch_shapes=[
            VMEM((512, 128), f32),
            VMEM((4, 2, 32, 128), bf16),
            VMEM((4, 2, 32, 128), bf16),
            VMEM((4, 128, 512), bf16),
            VMEM((4, 128, 128), bf16),
            VMEM((4, 128, 128), bf16),
            VMEM((4, 128, 128), f32),
            VMEM((4, 128, 128), f32),
            DMA, DMA, DMA, DMA((4,)), DMA, DMA((16,)),
            DMA, DMA((4,)), DMA, DMA((4,)), DMA, DMA((4,)), DMA, DMA((4,)),
            DMA, DMA((4,)), DMA,
        ],
        compiler_params=pltpu.CompilerParams(
            collective_id=0, has_side_effects=True, vmem_limit_bytes=48 << 20
        ),
        name="forward",
    )(emb, proj, w_in, bias, d_part, cot)


def local(embeddings, projection, w_in, bias, w_out, cotangent):
    highest = lax.Precision.HIGHEST
    toks, feat, embs = embeddings.shape
    rank = projection.shape[1]
    rows, cols, batches = lax.axis_size("row"), lax.axis_size("col"), lax.axis_size("batch")
    own = toks // (rows * cols)
    hid = w_out.shape[0]
    hid_local = w_in.shape[1]
    count = rows * embs * rank
    flat_out = w_out.reshape(hid, feat * embs)
    cot_rows = cotangent.reshape(toks, feat * embs)
    d_part = contract_last(cot_rows, flat_out).astype(bf16)
    act, hidden, d_preact, d_pre_b, normed, inv, own_emb, every_cot = forward(
        embeddings.reshape(64, own, feat, embs), projection, w_in.reshape(32, 128, hid_local),
        bias.reshape(1, hid_local), d_part, cot_rows,
    )
    act = jnp.moveaxis(act.reshape(32, toks, 128), 1, 0).reshape(toks, embs * rank)
    emb = own_emb.reshape(rows, own, cols * feat, embs).transpose(1, 2, 0, 3)
    emb = emb.reshape(own, cols * feat, rows * embs)
    emb_float = emb.astype(f32)
    normed = normed.reshape(own, rows * embs, rank)
    inv_rms = inv[:, :1, :1]
    d_part = contract_last(d_pre_b, w_in).astype(bf16).reshape(cols, rows * own, embs * rank)
    d_rows = summed(swap(d_part, "col")).astype(bf16)
    d_act = swap(d_rows.reshape(rows, own, embs * rank), "row").astype(f32)
    d_act = jnp.moveaxis(d_act, 0, 1).reshape(own, rows * embs, rank)
    inner = (jnp.sum(d_act * normed, axis=(1, 2)) / count)[:, None, None]
    d_inter = (inv_rms * (d_act - normed * inner)).astype(bf16)
    back_fold = jnp.einsum("bek,bde->bdk", d_inter, emb, preferred_element_type=f32)
    part_proj = jnp.einsum("bde,bdk->ek", emb_float, back_fold, precision=highest)
    part_proj = jnp.sum(swap(part_proj.reshape(rows, embs, rank), "row"), axis=0)
    everywhere = ("batch", "col")
    group = batches * cols
    share = jnp.sum(swap(part_proj.reshape(group, -1), everywhere), axis=0)
    grad_proj = everyone(share, everywhere).reshape(embs, rank)
    hidden_all = everyone(hidden, "col")
    mixed = jnp.dot(
        jnp.moveaxis(hidden_all, 0, 1).reshape(toks, hid), flat_out, preferred_element_type=f32
    )
    mixed = mixed.astype(bf16).reshape(toks, feat, embs)
    by_batch = hidden_all.reshape(batches, cols // batches, toks, hid_local)
    own_hidden = swap(by_batch, "batch")
    own_hidden = own_hidden.transpose(0, 2, 1, 3).reshape(batches * toks, hid // batches)
    grad_out = contract_first(own_hidden, every_cot.reshape(batches * toks, feat * embs))
    grad_out = grad_out.reshape(hid // batches, feat, embs)
    in_part = contract_first(act, d_pre_b).astype(bf16)
    quarter = summed(swap(in_part.reshape(batches, -1, hid_local), "batch")).astype(bf16)
    grad_in = everyone(quarter, "batch").astype(f32).reshape(embs * rank, hid_local)
    grad_bias = jnp.sum(everyone(jnp.sum(d_preact, axis=0), "batch"), axis=0)
    return (mixed, grad_out, grad_in, grad_bias, grad_proj)


def solution(mesh):
    placed = (
        P("batch", "col", "row"),
        P(),
        P("row", "col"),
        P("col"),
        P(None, "col", "row"),
        P("batch", "col", "row"),
    )
    return jax.shard_map(
        local,
        mesh=mesh,
        in_specs=placed,
        out_specs=(
            P("batch", "col", "row"),
            P("batch", "col", "row"),
            P("row", "col"),
            P("col"),
            P("row", None),
        ),
        check_vma=False,
    )
```

```python
import functools

import jax
import jax.numpy as jnp
from jax import lax
from jax.experimental import pallas as pl
from jax.experimental.pallas import tpu as pltpu
from jax.sharding import PartitionSpec as P

epsilon = 1e-06
bf16 = jnp.bfloat16
f32 = jnp.float32
MESH = pl.DeviceIdType.MESH
VMEM = pltpu.VMEM
DMA = pltpu.SemaphoreType.DMA


def contract_last(left, right):
    return lax.dot_general(left, right, (((1,), (1,)), ((), ())), preferred_element_type=f32)


def contract_first(left, right):
    return lax.dot_general(left, right, (((0,), (0,)), ((), ())), preferred_element_type=f32)


def dot(left, right):
    return jnp.dot(left, right, preferred_element_type=f32)


def send(src, dst, send_sem, recv_sem, **place):
    copy = pltpu.make_async_remote_copy(
        src_ref=src, dst_ref=dst, send_sem=send_sem, recv_sem=recv_sem,
        device_id=place, device_id_type=MESH,
    )
    copy.start()


def arrived(ref, sem):
    pltpu.make_async_copy(ref, ref, sem).wait()


def split(value):
    high = value.astype(bf16)
    return high, (value - high.astype(f32)).astype(bf16)


def places():
    me = {axis: lax.axis_index(axis) for axis in ("batch", "row", "col")}
    i, r, c = me["batch"], me["row"], me["col"]
    y = c // 4
    z = c - y * 4
    sibling = i + 1 - 2 * lax.rem(i, 2)
    across = lax.rem(i + 2, 4)
    return i, r, c, y, z, sibling, across


def forward_kernel(
    emb, proj, w_in, bias, d_part, cot,
    gathered, hidden, d_pre, d_pre_b, normed, inv, own_emb, every_cot,
    folds, to_row, from_row, d_y, d_z_out, d_z, d_x, pre_x,
    emb_send, emb_recv, row_send, row_recv, gather_send, gather_recv,
    dy_send, dy_recv, dz_send, dz_recv, dx_send, dx_recv, pre_send, pre_recv,
    cot_send, cot_recv, own_sem,
):
    i, r, c, y, z, sibling, across = places()
    me = c * 4 + r
    barrier = pltpu.get_barrier_semaphore()

    def greet(k, _):
        peer = lax.rem(me + k, 64)
        pl.semaphore_signal(
            barrier, inc=1, device_id={"col": peer // 4, "row": lax.rem(peer, 4)},
            device_id_type=MESH,
        )
        return 0

    lax.fori_loop(1, 64, greet, 0)
    for other in (sibling, across):
        pl.semaphore_signal(barrier, inc=1, device_id={"batch": other}, device_id_type=MESH)
    pl.semaphore_wait(barrier, 65)

    def give(k, _):
        peer = lax.rem(me + k, 64)
        send(
            emb.at[peer], own_emb.at[r, :, c], emb_send, emb_recv,
            col=peer // 4, row=lax.rem(peer, 4),
        )
        return 0

    keep = pltpu.make_async_copy(emb.at[me], own_emb.at[r, :, c], emb_recv)
    keep.start()
    lax.fori_loop(1, 64, give, 0)
    for k in (1, 2, 3):
        to = lax.rem(y + k, 4)
        send(
            d_part.at[:, pl.ds(pl.multiple_of(to * 512, 512), 512)], d_y.at[y],
            dy_send, dy_recv.at[y], col=to * 4 + z,
        )
    lanes = lax.broadcasted_iota(jnp.int32, (32, 128), 1)
    ranks = lax.broadcasted_iota(jnp.int32, (32, 128), 0)
    spread = (lax.rem(lanes, 32) == ranks).astype(f32).astype(bf16)
    wide = dot(proj[...], spread).astype(bf16)
    block = lax.broadcasted_iota(jnp.int32, (128, 128), 1) // 32
    at = lax.broadcasted_iota(jnp.int32, (256, 256), 0)
    of = lax.broadcasted_iota(jnp.int32, (256, 256), 1)
    source = lax.rem(at, 8) // 2 * 64 + lax.rem(at, 2) * 32 + at // 8
    order = (of == source).astype(f32).astype(bf16)
    arrived(own_emb, emb_recv)
    for s in range(2):
        tiles = [own_emb[q, s].reshape(128, 128) for q in range(4)]
        folded = sum(dot(tiles[q], wide[q * 128 : (q + 1) * 128]) for q in range(4))
        high, low = split(folded)
        for q in range(4):
            folds[q * 128 : (q + 1) * 128, :] = contract_first(tiles[q], high) + contract_first(
                tiles[q], low
            )
        inter = jnp.zeros((128, 128), f32)
        for j in range(4):
            inter = jnp.where(block == j, folds[pl.ds(j, 128, stride=4), :], inter)
        total = jnp.sum(jnp.sum(inter * inter, axis=0, keepdims=True), axis=1, keepdims=True)
        scale = lax.rsqrt(total / (512 * 32) + epsilon)
        norm = inter * scale
        normed[s] = norm
        inv[s] = jnp.broadcast_to(scale, (8, 128))
        for q in range(4):
            to_row[q, s] = norm[q * 32 : (q + 1) * 32].astype(bf16)
    from_row[r] = to_row[r]
    for k in (1, 2, 3):
        to = lax.rem(r + k, 4)
        send(to_row.at[to], from_row.at[r], row_send, row_recv.at[r], row=to)
    for k in (1, 2, 3):
        f = lax.rem(y + k, 4)
        arrived(d_y.at[f], dy_recv.at[f])
    d_y[y] = d_part[:, pl.ds(pl.multiple_of(y * 512, 512), 512)]
    for q in range(4):
        part = d_y[0, :, q * 128 : (q + 1) * 128].astype(f32)
        for f in (1, 2, 3):
            part = part + d_y[f, :, q * 128 : (q + 1) * 128].astype(f32)
        d_z_out[q] = part.astype(bf16)
    d_z[z] = d_z_out[z]
    for k in (1, 2, 3):
        to = lax.rem(z + k, 4)
        send(d_z_out.at[to], d_z.at[z], dz_send, dz_recv.at[z], col=y * 4 + to)
    for k in (1, 2, 3):
        f = lax.rem(r + k, 4)
        arrived(from_row.at[f], row_recv.at[f])
    rows = dot(order, from_row[...].reshape(256, 128))
    gathered[:, c] = rows.reshape(32, 8, 128).astype(bf16)
    for k in (1, 2, 3):
        to = lax.rem(z + k, 4)
        send(gathered.at[:, c], gathered.at[:, c], gather_send, gather_recv.at[c], col=y * 4 + to)
    for k in (1, 2, 3):
        to = lax.rem(y + k, 4)
        send(gathered.at[:, c], gathered.at[:, c], gather_send, gather_recv.at[c], col=to * 4 + z)
    for m in (1, 2, 3):
        slot = y * 4 + lax.rem(z + m, 4)
        arrived(gathered.at[:, slot], gather_recv.at[slot])
        for k in (1, 2, 3):
            to = lax.rem(y + k, 4)
            send(
                gathered.at[:, slot], gathered.at[:, slot], gather_send, gather_recv.at[slot],
                col=to * 4 + z,
            )
    mine = pltpu.make_async_copy(cot, every_cot.at[i], own_sem)
    mine.start()
    send(cot, every_cot.at[i], cot_send, cot_recv.at[i], batch=sibling)
    send(cot, every_cot.at[i], cot_send, cot_recv.at[i], batch=across)
    for k in (1, 2, 3):
        f = lax.rem(z + k, 4)
        arrived(d_z.at[f], dz_recv.at[f])
    d_x[r] = sum(d_z[f].astype(f32) for f in range(4))
    for k in (1, 2, 3):
        to = lax.rem(r + k, 4)
        send(d_x.at[r], d_x.at[r], dx_send, dx_recv.at[r], row=to)
    for m in (1, 2, 3):
        for k in range(4):
            slot = lax.rem(y + m, 4) * 4 + k
            arrived(gathered.at[:, slot], gather_recv.at[slot])
    pre = jnp.zeros((128, 128), f32)
    for e in range(32):
        pre = pre + dot(gathered[e].reshape(128, 128), w_in[e])
    pre_x[r] = pre
    for k in (1, 2, 3):
        to = lax.rem(r + k, 4)
        send(pre_x.at[r], pre_x.at[r], pre_send, pre_recv.at[r], row=to)
    arrived(every_cot.at[across], cot_recv.at[across])
    send(every_cot.at[across], every_cot.at[across], cot_send, cot_recv.at[across], batch=sibling)
    for k in (1, 2, 3):
        f = lax.rem(r + k, 4)
        arrived(d_x.at[f], dx_recv.at[f])
    d_hidden = (d_x[0] + d_x[1]) + (d_x[2] + d_x[3])
    for k in (1, 2, 3):
        f = lax.rem(r + k, 4)
        arrived(pre_x.at[f], pre_recv.at[f])
    preact = (pre_x[0] + pre_x[1]) + (pre_x[2] + pre_x[3]) + bias[...]
    sig = 1.0 / (1.0 + jnp.exp(-preact))
    hidden[...] = (preact * sig).astype(bf16)
    d_value = d_hidden * sig * (1.0 + preact * (1.0 - sig))
    d_pre[...] = d_value
    d_pre_b[...] = d_value.astype(bf16)
    diagonal = lax.rem(sibling + 2, 4)
    arrived(every_cot.at[sibling], cot_recv.at[sibling])
    arrived(every_cot.at[diagonal], cot_recv.at[diagonal])
    mine.wait()
    arrived(emb.at[pl.ds(0, 63)], emb_send)
    arrived(d_y.at[pl.ds(0, 3)], dy_send)
    arrived(d_z.at[pl.ds(0, 3)], dz_send)
    arrived(d_x.at[pl.ds(0, 3)], dx_send)
    arrived(pre_x.at[pl.ds(0, 3)], pre_send)
    arrived(from_row.at[pl.ds(0, 3)], row_send)
    arrived(every_cot.at[pl.ds(0, 3)], cot_send)
    arrived(gathered.at[:, pl.ds(0, 15)], gather_send)


def forward(emb, proj, w_in, bias, d_part, cot):
    out = jax.ShapeDtypeStruct
    return pl.pallas_call(
        forward_kernel,
        out_shape=(
            out((32, 16, 8, 128), bf16),
            out((128, 128), bf16),
            out((128, 128), f32),
            out((128, 128), bf16),
            out((2, 128, 128), f32),
            out((2, 8, 128), f32),
            out((4, 2, 16, 8, 128), bf16),
            out((4, 128, 1024), bf16),
        ),
        in_specs=[pl.BlockSpec(memory_space=VMEM)] * 6,
        out_specs=[pl.BlockSpec(memory_space=VMEM)] * 8,
        scratch_shapes=[
            VMEM((512, 128), f32),
            VMEM((4, 2, 32, 128), bf16),
            VMEM((4, 2, 32, 128), bf16),
            VMEM((4, 128, 512), bf16),
            VMEM((4, 128, 128), bf16),
            VMEM((4, 128, 128), bf16),
            VMEM((4, 128, 128), f32),
            VMEM((4, 128, 128), f32),
            DMA, DMA, DMA, DMA((4,)), DMA, DMA((16,)),
            DMA, DMA((4,)), DMA, DMA((4,)), DMA, DMA((4,)), DMA, DMA((4,)),
            DMA, DMA((4,)), DMA,
        ],
        compiler_params=pltpu.CompilerParams(
            collective_id=0, has_side_effects=True, vmem_limit_bytes=48 << 20
        ),
        name="forward",
    )(emb, proj, w_in, bias, d_part, cot)


def lanes_of(slot, size=128):
    return pl.ds(pl.multiple_of(slot * size, size), size)


def backward_kernel(
    hidden, d_pre_b, d_pre, w_in, gathered, normed, inv, own_emb,
    hidden_all, own_hidden, grad_in, grad_proj, grad_bias,
    d_act, d_y, d_z_out, d_z, d_row_out, d_row, spread, acts, d_all, bias_all,
    proj_out, proj_x, proj_y, proj_z, proj_b,
    h_send, h_recv, oh_send, oh_recv, dy_send, dy_recv, dz_send, dz_recv, row_send, row_recv,
    acts_send, acts_recv, all_send, all_recv, in_send, in_recv, bias_send, bias_recv,
    px_send, px_recv, py_send, py_recv, pz_send, pz_recv, pb_send, pb_recv, own_sem,
):
    i, r, c, y, z, sibling, across = places()
    barrier = pltpu.get_barrier_semaphore()
    for k in (1, 2, 3):
        for place in (
            {"row": lax.rem(r + k, 4)},
            {"col": lax.rem(y + k, 4) * 4 + z},
            {"col": y * 4 + lax.rem(z + k, 4)},
            {"batch": lax.rem(i + k, 4)},
        ):
            pl.semaphore_signal(barrier, inc=1, device_id=place, device_id_type=MESH)
    pl.semaphore_wait(barrier, 12)
    mine = pltpu.make_async_copy(gathered.at[pl.ds(8 * i, 8)], acts.at[i], own_sem)
    mine.start()
    for k in (1, 2, 3):
        to = lax.rem(z + k, 4)
        send(hidden, hidden_all.at[:, lanes_of(c)], h_send, h_recv.at[c], col=y * 4 + to)
    for half in range(2):
        for e in range(16):
            part = contract_last(d_pre_b[...], w_in[half * 16 + e])
            d_act[half, e] = part.reshape(16, 8, 128).astype(bf16)
        for k in (1, 2, 3):
            to = lax.rem(y + k, 4)
            send(
                d_act.at[half, :, pl.ds(4 * to, 4)], d_y.at[half, y],
                dy_send, dy_recv.at[half, y], col=to * 4 + z,
            )
    for k in (1, 2, 3):
        to = lax.rem(y + k, 4)
        send(hidden, hidden_all.at[:, lanes_of(c)], h_send, h_recv.at[c], col=to * 4 + z)
    hidden_all[:, lanes_of(c)] = hidden[...]
    bias_all[i] = jnp.broadcast_to(jnp.sum(d_pre[...], axis=0, keepdims=True), (8, 128))
    d_all[i] = d_pre_b[...]
    for k in (1, 2, 3):
        to = lax.rem(i + k, 4)
        send(d_pre_b, d_all.at[i], all_send, all_recv.at[i], batch=to)
        send(bias_all.at[i], bias_all.at[i], bias_send, bias_recv.at[i], batch=to)
        send(gathered.at[pl.ds(8 * to, 8)], acts.at[i], acts_send, acts_recv.at[i], batch=to)
    for m in (1, 2, 3):
        slot = y * 4 + lax.rem(z + m, 4)
        arrived(hidden_all.at[:, lanes_of(slot)], h_recv.at[slot])
        for k in (1, 2, 3):
            to = lax.rem(y + k, 4)
            send(
                hidden_all.at[:, lanes_of(slot)], hidden_all.at[:, lanes_of(slot)],
                h_send, h_recv.at[slot], col=to * 4 + z,
            )
    at = lax.broadcasted_iota(jnp.int32, (256, 256), 0)
    of = lax.broadcasted_iota(jnp.int32, (256, 256), 1)
    source = lax.rem(at, 8) // 2 * 64 + lax.rem(at, 2) * 32 + at // 8
    order = (of == source).astype(f32).astype(bf16)
    for half in range(2):
        d_y[half, y] = d_act[half, :, pl.ds(4 * y, 4)]
        for k in (1, 2, 3):
            f = lax.rem(y + k, 4)
            arrived(d_y.at[half, f], dy_recv.at[half, f])
        for q in range(4):
            part = d_y[half, 0, :, q].astype(f32)
            for f in (1, 2, 3):
                part = part + d_y[half, f, :, q].astype(f32)
            d_z_out[half, q] = part.astype(bf16)
        d_z[half, z] = d_z_out[half, z]
        for k in (1, 2, 3):
            to = lax.rem(z + k, 4)
            send(
                d_z_out.at[half, to], d_z.at[half, z], dz_send, dz_recv.at[half, z],
                col=y * 4 + to,
            )
    for m in (1, 2, 3):
        for k in range(4):
            slot = lax.rem(y + m, 4) * 4 + k
            arrived(hidden_all.at[:, lanes_of(slot)], h_recv.at[slot])
    for k in (1, 2, 3):
        to = lax.rem(i + k, 4)
        send(
            hidden_all.at[:, lanes_of(to, 512)], own_hidden.at[i], oh_send, oh_recv.at[i],
            batch=to,
        )
    own_hidden[i] = hidden_all[:, lanes_of(i, 512)]
    mine.wait()
    for k in (1, 2, 3):
        f = lax.rem(i + k, 4)
        arrived(d_all.at[f], all_recv.at[f])
        arrived(acts.at[f], acts_recv.at[f])
    for e in range(8):
        part = contract_first(acts[0, e].reshape(128, 128), d_all[0])
        for f in (1, 2, 3):
            part = part + contract_first(acts[f, e].reshape(128, 128), d_all[f])
        grad_in[i, e] = part.astype(bf16)
    send(grad_in.at[i], grad_in.at[i], in_send, in_recv.at[i], batch=sibling)
    send(grad_in.at[i], grad_in.at[i], in_send, in_recv.at[i], batch=across)
    for half in range(2):
        for k in (1, 2, 3):
            f = lax.rem(z + k, 4)
            arrived(d_z.at[half, f], dz_recv.at[half, f])
    total = jnp.concatenate(
        [
            sum(d_z[half, f].astype(f32) for f in range(4)).reshape(128, 128)
            for half in range(2)
        ],
        axis=0,
    )
    high, low = split(total)
    d_row_out[...] = (contract_first(order, high) + contract_first(order, low)).reshape(
        4, 2, 32, 128
    )
    d_row[r] = d_row_out[r]
    for k in (1, 2, 3):
        to = lax.rem(r + k, 4)
        send(d_row_out.at[to], d_row.at[r], row_send, row_recv.at[r], row=to)
    block = lax.broadcasted_iota(jnp.int32, (128, 128), 1) // 32
    for k in (1, 2, 3):
        f = lax.rem(r + k, 4)
        arrived(d_row.at[f], row_recv.at[f])
    for s in range(2):
        grad = d_row[:, s].reshape(128, 128)
        norm = normed[s]
        inner = jnp.sum(jnp.sum(grad * norm, axis=0, keepdims=True), axis=1, keepdims=True)
        d_inter = (inv[s, 0:1, :] * (grad - norm * (inner / (512 * 32)))).astype(bf16).astype(f32)
        for j in range(4):
            spread[pl.ds(j, 128, stride=4), :] = jnp.where(block == j, d_inter, 0.0)
        tiles = [own_emb[q, s].reshape(128, 128) for q in range(4)]
        fold = sum(
            dot(tiles[q], spread[q * 128 : (q + 1) * 128, :].astype(bf16)) for q in range(4)
        )
        fold = fold + pltpu.roll(fold, 32, 1)
        fold = fold + pltpu.roll(fold, 64, 1)
        high, low = split(fold)
        for q in range(4):
            part = contract_first(high, tiles[q])[:32] + contract_first(low, tiles[q])[:32]
            if s == 0:
                proj_out[q] = part
            else:
                proj_out[q] += part
    proj_x[r] = proj_out[r]
    for k in (1, 2, 3):
        to = lax.rem(r + k, 4)
        send(proj_out.at[to], proj_x.at[r], px_send, px_recv.at[r], row=to)
    for k in (1, 2, 3):
        f = lax.rem(r + k, 4)
        arrived(proj_x.at[f], px_recv.at[f])
    proj_y[y] = (proj_x[0] + proj_x[1]) + (proj_x[2] + proj_x[3])
    for k in (1, 2, 3):
        to = lax.rem(y + k, 4)
        send(proj_y.at[y], proj_y.at[y], py_send, py_recv.at[y], col=to * 4 + z)
    for k in (1, 2, 3):
        f = lax.rem(y + k, 4)
        arrived(proj_y.at[f], py_recv.at[f])
    proj_z[z] = (proj_y[0] + proj_y[1]) + (proj_y[2] + proj_y[3])
    for k in (1, 2, 3):
        to = lax.rem(z + k, 4)
        send(proj_z.at[z], proj_z.at[z], pz_send, pz_recv.at[z], col=y * 4 + to)
    arrived(grad_in.at[across], in_recv.at[across])
    send(grad_in.at[across], grad_in.at[across], in_send, in_recv.at[across], batch=sibling)
    for k in (1, 2, 3):
        f = lax.rem(z + k, 4)
        arrived(proj_z.at[f], pz_recv.at[f])
    proj_b[i] = (proj_z[0] + proj_z[1]) + (proj_z[2] + proj_z[3])
    for k in (1, 2, 3):
        to = lax.rem(i + k, 4)
        send(proj_b.at[i], proj_b.at[i], pb_send, pb_recv.at[i], batch=to)
    for k in (1, 2, 3):
        f = lax.rem(i + k, 4)
        arrived(bias_all.at[f], bias_recv.at[f])
        arrived(own_hidden.at[f], oh_recv.at[f])
    grad_bias[...] = (bias_all[0] + bias_all[1]) + (bias_all[2] + bias_all[3])
    for k in (1, 2, 3):
        f = lax.rem(i + k, 4)
        arrived(proj_b.at[f], pb_recv.at[f])
    grad_proj[...] = (proj_b[0] + proj_b[1]) + (proj_b[2] + proj_b[3])
    diagonal = lax.rem(sibling + 2, 4)
    arrived(grad_in.at[sibling], in_recv.at[sibling])
    arrived(grad_in.at[diagonal], in_recv.at[diagonal])
    three = pl.ds(0, 3)
    arrived(hidden_all.at[:, pl.ds(0, 15 * 128)], h_send)
    arrived(own_hidden.at[three], oh_send)
    arrived(d_act.at[:, :, pl.ds(0, 12)], dy_send)
    arrived(d_z.at[:, three], dz_send)
    arrived(d_row.at[three], row_send)
    arrived(acts.at[three], acts_send)
    arrived(d_all.at[three], all_send)
    arrived(grad_in.at[three], in_send)
    arrived(bias_all.at[three], bias_send)
    arrived(proj_x.at[three], px_send)
    arrived(proj_y.at[three], py_send)
    arrived(proj_z.at[three], pz_send)
    arrived(proj_b.at[three], pb_send)


def backward(hidden, d_pre_b, d_pre, w_in, gathered, normed, inv, own_emb):
    out = jax.ShapeDtypeStruct
    pair = [DMA, DMA((4,))]
    return pl.pallas_call(
        backward_kernel,
        out_shape=(
            out((128, 2048), bf16),
            out((4, 128, 512), bf16),
            out((4, 8, 128, 128), bf16),
            out((32, 128), f32),
            out((8, 128), f32),
        ),
        in_specs=[pl.BlockSpec(memory_space=VMEM)] * 8,
        out_specs=[pl.BlockSpec(memory_space=VMEM)] * 5,
        scratch_shapes=[
            VMEM((2, 16, 16, 8, 128), bf16),
            VMEM((2, 4, 16, 4, 8, 128), bf16),
            VMEM((2, 4, 16, 8, 128), bf16),
            VMEM((2, 4, 16, 8, 128), bf16),
            VMEM((4, 2, 32, 128), f32),
            VMEM((4, 2, 32, 128), f32),
            VMEM((512, 128), f32),
            VMEM((4, 8, 16, 8, 128), bf16),
            VMEM((4, 128, 128), bf16),
            VMEM((4, 8, 128), f32),
            VMEM((4, 32, 128), f32),
            VMEM((4, 32, 128), f32),
            VMEM((4, 32, 128), f32),
            VMEM((4, 32, 128), f32),
            VMEM((4, 32, 128), f32),
            DMA, DMA((16,)), *pair, DMA, DMA((2, 4)), DMA, DMA((2, 4)), *pair,
            *pair, *pair, *pair, *pair,
            *pair, *pair, *pair, *pair, DMA,
        ],
        compiler_params=pltpu.CompilerParams(
            collective_id=1, has_side_effects=True, vmem_limit_bytes=48 << 20
        ),
        name="backward",
    )(hidden, d_pre_b, d_pre, w_in, gathered, normed, inv, own_emb)


def local(embeddings, projection, w_in, bias, w_out, cotangent):
    toks, feat, embs = embeddings.shape
    hid = w_out.shape[0]
    hid_local = w_in.shape[1]
    flat_out = w_out.reshape(hid, feat * embs)
    cot_rows = cotangent.reshape(toks, feat * embs)
    d_part = contract_last(cot_rows, flat_out).astype(bf16)
    w_tiles = w_in.reshape(32, 128, hid_local)
    act, hidden, d_pre, d_pre_b, normed, inv, own_emb, every_cot = forward(
        embeddings.reshape(64, 2, feat, embs), projection, w_tiles,
        bias.reshape(1, hid_local), d_part, cot_rows,
    )
    hidden_all, own_hidden, grad_in, grad_proj, grad_bias = backward(
        hidden, d_pre_b, d_pre, w_tiles, act, normed, inv, own_emb
    )
    mixed = jnp.dot(hidden_all, flat_out, preferred_element_type=f32)
    mixed = mixed.astype(bf16).reshape(toks, feat, embs)
    grad_out = contract_first(
        own_hidden.reshape(4 * toks, hid // 4), every_cot.reshape(4 * toks, feat * embs)
    )
    grad_out = grad_out.reshape(hid // 4, feat, embs)
    grad_in = grad_in.astype(f32).reshape(w_in.shape)
    return (mixed, grad_out, grad_in, grad_bias[0], grad_proj.T)


def solution(mesh):
    placed = (
        P("batch", "col", "row"),
        P(),
        P("row", "col"),
        P("col"),
        P(None, "col", "row"),
        P("batch", "col", "row"),
    )
    return jax.shard_map(
        local,
        mesh=mesh,
        in_specs=placed,
        out_specs=(
            P("batch", "col", "row"),
            P("batch", "col", "row"),
            P("row", "col"),
            P("col"),
            P("row", None),
        ),
        check_vma=False,
    )
```

```python
import jax
import jax.numpy as jnp
from jax import lax
from jax.experimental import pallas as pl
from jax.experimental.pallas import tpu as pltpu
from jax.sharding import PartitionSpec as P

epsilon = 1e-06
bf16 = jnp.bfloat16
f32 = jnp.float32
MESH = pl.DeviceIdType.MESH
VMEM = pltpu.VMEM
DMA = pltpu.SemaphoreType.DMA
others = (1, 2, 3)


def contract_last(left, right):
    return lax.dot_general(left, right, (((1,), (1,)), ((), ())), preferred_element_type=f32)


def contract_first(left, right):
    return lax.dot_general(left, right, (((0,), (0,)), ((), ())), preferred_element_type=f32)


def dot(left, right):
    return jnp.dot(left, right, preferred_element_type=f32)


def send(src, dst, send_sem, recv_sem, **place):
    copy = pltpu.make_async_remote_copy(
        src_ref=src, dst_ref=dst, send_sem=send_sem, recv_sem=recv_sem,
        device_id=place, device_id_type=MESH,
    )
    copy.start()


def arrived(ref, sem):
    pltpu.make_async_copy(ref, ref, sem).wait()


def split(value):
    high = value.astype(bf16)
    return high, (value - high.astype(f32)).astype(bf16)


def four(parts):
    return (parts[0] + parts[1]) + (parts[2] + parts[3])


def turn(place, k):
    return lax.rem(place + k, 4)


def lanes_of(slot, size=128):
    return pl.ds(pl.multiple_of(slot * size, size), size)


def whole_sum(value):
    return jnp.sum(jnp.sum(value, axis=0, keepdims=True), axis=1, keepdims=True)


def ordering(size, high):
    at = lax.broadcasted_iota(jnp.int32, (size, size), 0)
    of = lax.broadcasted_iota(jnp.int32, (size, size), 1)
    source = lax.rem(at, 8) // 2 * (2 * high) + lax.rem(at, 2) * high + at // 8
    return (of == source).astype(f32).astype(bf16)


def kernel(
    emb, proj, w_in_far, bias, w_out_far, cot,
    mixed, grad_out, grad_in, grad_bias, grad_proj,
    w_in, w_out, w_split, stage, every_cot, own_emb, folds, normed, inv,
    part_out, part_y, part_z_out, part_z, part_x,
    to_row, raw, gathered, pre_x, hidden, d_pre_b,
    d_act, d_y, d_z_out, d_z, acts, d_all, bias_all, hidden_all, own_hidden, hidden_t,
    proj_out, proj_x, proj_z, proj_b,
    load_in, load_out, emb_send, emb_recv, cot_send, cot_recv,
    py_send, py_recv, pz_send, pz_recv, px_send, px_recv,
    near_send, far_send, raw_recv, pre_send, pre_recv,
    h_send, h_recv, oh_send, oh_recv, dy_send, dy_recv, dz_send, dz_recv,
    acts_send, acts_recv, all_send, all_recv, in_send, in_recv, bias_send, bias_recv,
    gx_send, gx_recv, gz_send, gz_recv, gb_send, gb_recv, own_sem,
):
    i = lax.axis_index("batch")
    r = lax.axis_index("row")
    c = lax.axis_index("col")
    y = c // 4
    z = c - y * 4
    sibling = i + 1 - 2 * lax.rem(i, 2)
    across = turn(i, 2)
    diagonal = turn(sibling, 2)
    me = c * 4 + r
    three = pl.ds(0, 3)
    barrier = pltpu.get_barrier_semaphore()

    def greet(k, _):
        peer = lax.rem(me + k, 64)
        pl.semaphore_signal(
            barrier, inc=1, device_id={"col": peer // 4, "row": lax.rem(peer, 4)},
            device_id_type=MESH,
        )
        return 0

    lax.fori_loop(1, 64, greet, 0)
    for k in others:
        pl.semaphore_signal(barrier, inc=1, device_id={"batch": turn(i, k)}, device_id_type=MESH)
    take_out = pltpu.make_async_copy(w_out_far, w_out, load_out)
    take_out.start()
    take_in = pltpu.make_async_copy(w_in_far, w_in, load_in)
    take_in.start()
    stage[...] = cot[...].astype(f32).reshape(1024, 128)
    for d in range(8):
        every_cot[i, d] = stage[pl.ds(d, 128, stride=8), :].astype(bf16)
    pl.semaphore_wait(barrier, 66)

    keep = pltpu.make_async_copy(emb.at[me], own_emb.at[r, :, c], emb_recv)
    keep.start()

    def give(k, _):
        peer = lax.rem(me + k, 64)
        send(
            emb.at[peer], own_emb.at[r, :, c], emb_send, emb_recv,
            col=peer // 4, row=lax.rem(peer, 4),
        )
        return 0

    lax.fori_loop(1, 64, give, 0)

    take_out.wait()
    for k in (1, 2, 3, 0):
        to = turn(y, k)

        def divide(n, _):
            at = pl.multiple_of(to * 512 + n * 128, 128)
            stage[...] = w_out[pl.ds(at, 128)].astype(f32).reshape(1024, 128)
            for d in range(8):
                w_split[d, pl.ds(at, 128), :] = stage[pl.ds(d, 128, stride=8), :].astype(bf16)
            return 0

        lax.fori_loop(0, 4, divide, 0)
        part = jnp.zeros((128, 512), f32)
        for d in range(8):
            part = part + contract_last(every_cot[i, d], w_split[d, lanes_of(to, 512), :])
        for q in range(4):
            part_out[to, q] = part[:, q * 128 : (q + 1) * 128].astype(bf16)
        if k:
            send(part_out.at[to], part_y.at[y], py_send, py_recv.at[y], col=to * 4 + z)
        else:
            part_y[y] = part_out[y]

    lanes = lax.broadcasted_iota(jnp.int32, (32, 128), 1)
    ranks = lax.broadcasted_iota(jnp.int32, (32, 128), 0)
    repeat = (lax.rem(lanes, 32) == ranks).astype(f32).astype(bf16)
    wide = contract_first(proj[...], repeat).astype(bf16)
    block = lax.broadcasted_iota(jnp.int32, (128, 128), 1) // 32
    order = ordering(256, 32)

    def sample(s):
        return jnp.concatenate([own_emb[q, s].reshape(128, 128) for q in range(4)], axis=1)

    arrived(own_emb, emb_recv)
    for s in range(2):
        own = sample(s)
        high, low = split(dot(own, wide))
        both = contract_first(own, jnp.concatenate([high, low], axis=1))
        folds[...] = both[:, :128] + both[:, 128:]
        inter = jnp.zeros((128, 128), f32)
        for j in range(4):
            inter = jnp.where(block == j, folds[pl.ds(j, 128, stride=4), :], inter)
        scale = lax.rsqrt(whole_sum(inter * inter) / (512 * 32) + epsilon)
        norm = inter * scale
        normed[s] = norm
        inv[s] = jnp.broadcast_to(scale, (8, 128))
        for q in range(4):
            to_row[q, s] = norm[q * 32 : (q + 1) * 32].astype(bf16)
    raw[c, r] = to_row[r]
    plane = z * 4 + r

    def scatter(k, _):
        peer = lax.rem(plane + k, 16)
        to_z = peer // 4
        to_r = lax.rem(peer, 4)
        send(to_row.at[to_r], raw.at[c, r], near_send, raw_recv.at[c], col=y * 4 + to_z, row=to_r)
        return 0

    lax.fori_loop(1, 16, scatter, 0)

    for k in others:
        f = turn(y, k)
        arrived(part_y.at[f], py_recv.at[f])
    for q in range(4):
        part_z_out[q] = four([part_y[f, q].astype(f32) for f in range(4)]).astype(bf16)
    part_z[z] = part_z_out[z]
    for k in others:
        to = turn(z, k)
        send(part_z_out.at[to], part_z.at[z], pz_send, pz_recv.at[z], col=y * 4 + to)

    arrived(raw.at[c, three], raw_recv.at[c])
    for k in others:
        send(raw.at[c], raw.at[c], far_send, raw_recv.at[c], col=turn(y, k) * 4 + z)
    for m in others:
        slot = y * 4 + turn(z, m)
        arrived(raw.at[slot], raw_recv.at[slot])
        for k in others:
            send(raw.at[slot], raw.at[slot], far_send, raw_recv.at[slot], col=turn(y, k) * 4 + z)
    send(every_cot.at[i], every_cot.at[i], cot_send, cot_recv.at[i], batch=sibling)
    send(every_cot.at[i], every_cot.at[i], cot_send, cot_recv.at[i], batch=across)

    def lay(slot):
        rows = dot(order, raw[slot].reshape(256, 128))
        gathered[:, slot] = rows.reshape(32, 8, 128).astype(bf16)

    for q in range(4):
        lay(y * 4 + q)
    for k in others:
        f = turn(z, k)
        arrived(part_z.at[f], pz_recv.at[f])
    part_x[r] = four([part_z[f].astype(f32) for f in range(4)])
    for k in others:
        send(part_x.at[r], part_x.at[r], px_send, px_recv.at[r], row=turn(r, k))
    take_in.wait()
    for k in range(4):
        for m in others:
            slot = turn(y, m) * 4 + turn(z, k)
            arrived(raw.at[slot], raw_recv.at[slot])
            lay(slot)
    pre = jnp.zeros((128, 128), f32)
    for e in range(32):
        pre = pre + dot(gathered[e].reshape(128, 128), w_in[e])
    pre_x[r] = pre
    for k in others:
        send(pre_x.at[r], pre_x.at[r], pre_send, pre_recv.at[r], row=turn(r, k))
    for k in others:
        to = turn(i, k)
        send(gathered.at[pl.ds(8 * to, 8)], acts.at[i], acts_send, acts_recv.at[i], batch=to)
    mine = pltpu.make_async_copy(gathered.at[pl.ds(8 * i, 8)], acts.at[i], own_sem)
    mine.start()
    arrived(every_cot.at[across], cot_recv.at[across])
    send(every_cot.at[across], every_cot.at[across], cot_send, cot_recv.at[across], batch=sibling)
    for k in others:
        f = turn(r, k)
        arrived(part_x.at[f], px_recv.at[f])
    d_hidden = four(part_x)
    for k in others:
        f = turn(r, k)
        arrived(pre_x.at[f], pre_recv.at[f])
    preact = four(pre_x) + bias[...]
    sig = 1.0 / (1.0 + jnp.exp(-preact))
    hidden[...] = (preact * sig).astype(bf16)
    d_value = d_hidden * sig * (1.0 + preact * (1.0 - sig))
    d_pre_b[...] = d_value.astype(bf16)
    bias_all[i] = jnp.broadcast_to(jnp.sum(d_value, axis=0, keepdims=True), (8, 128))

    for k in others:
        send(hidden, hidden_all.at[:, lanes_of(c)], h_send, h_recv.at[c], col=y * 4 + turn(z, k))
    for half in range(2):
        for e in range(16):
            part = contract_last(d_pre_b[...], w_in[half * 16 + e])
            d_act[half, e] = part.reshape(16, 8, 128).astype(bf16)
        for k in others:
            to = turn(y, k)
            send(
                d_act.at[half, :, pl.ds(4 * to, 4)], d_y.at[half, y],
                dy_send, dy_recv.at[half, y], col=to * 4 + z,
            )
    for k in others:
        send(hidden, hidden_all.at[:, lanes_of(c)], h_send, h_recv.at[c], col=turn(y, k) * 4 + z)
    hidden_all[:, lanes_of(c)] = hidden[...]
    d_all[i] = d_pre_b[...]
    for k in others:
        to = turn(i, k)
        send(d_pre_b, d_all.at[i], all_send, all_recv.at[i], batch=to)
        send(bias_all.at[i], bias_all.at[i], bias_send, bias_recv.at[i], batch=to)
    for m in others:
        slot = y * 4 + turn(z, m)
        place = hidden_all.at[:, lanes_of(slot)]
        arrived(place, h_recv.at[slot])
        for k in others:
            send(place, place, h_send, h_recv.at[slot], col=turn(y, k) * 4 + z)
    undo = ordering(128, 16)
    for half in range(2):
        d_y[half, y] = d_act[half, :, pl.ds(4 * y, 4)]
        for k in others:
            f = turn(y, k)
            arrived(d_y.at[half, f], dy_recv.at[half, f])
        for q in range(4):
            part = four([d_y[half, f, :, q].astype(f32) for f in range(4)])
            rows = contract_first(undo, part.reshape(128, 128).astype(bf16))
            for g in range(4):
                d_z_out[half, q * 4 + g] = (
                    rows[g * 32 : (g + 1) * 32].reshape(2, 16, 128).astype(bf16)
                )
        d_z[half, plane] = d_z_out[half, plane]

        def hand(k, _):
            peer = lax.rem(plane + k, 16)
            send(
                d_z_out.at[half, peer], d_z.at[half, plane], dz_send, dz_recv.at[half],
                col=y * 4 + peer // 4, row=lax.rem(peer, 4),
            )
            return 0

        lax.fori_loop(1, 16, hand, 0)
    for m in others:
        for k in range(4):
            slot = turn(y, m) * 4 + k
            arrived(hidden_all.at[:, lanes_of(slot)], h_recv.at[slot])
    for k in others:
        to = turn(i, k)
        send(
            hidden_all.at[:, lanes_of(to, 512)], own_hidden.at[i], oh_send, oh_recv.at[i],
            batch=to,
        )
    own_hidden[i] = hidden_all[:, lanes_of(i, 512)]
    mine.wait()
    for k in others:
        f = turn(i, k)
        arrived(d_all.at[f], all_recv.at[f])
        arrived(acts.at[f], acts_recv.at[f])
    for e in range(8):
        part = four([contract_first(acts[f, e].reshape(128, 128), d_all[f]) for f in range(4)])
        grad_in[i, e] = part.astype(bf16)
    send(grad_in.at[i], grad_in.at[i], in_send, in_recv.at[i], batch=sibling)
    send(grad_in.at[i], grad_in.at[i], in_send, in_recv.at[i], batch=across)
    for half in range(2):
        arrived(d_z.at[half, pl.ds(0, 15)], dz_recv.at[half])
    for s in range(2):
        grad = jnp.concatenate(
            [
                four([d_z[half, q * 4 + g, s].astype(f32) for q in range(4)])
                for g in range(4)
                for half in range(2)
            ],
            axis=0,
        )
        norm = normed[s]
        inner = whole_sum(grad * norm) / (512 * 32)
        d_inter = (inv[s, 0:1, :] * (grad - norm * inner)).astype(bf16).astype(f32)
        for j in range(4):
            folds[pl.ds(j, 128, stride=4), :] = jnp.where(block == j, d_inter, 0.0)
        own = sample(s)
        fold = dot(own, folds[...].astype(bf16))
        fold = fold + pltpu.roll(fold, 32, 1)
        fold = fold + pltpu.roll(fold, 64, 1)
        high, low = split(jnp.transpose(fold)[:32])
        both = dot(jnp.concatenate([high, low], axis=0), own)
        for q in range(4):
            part = both[:32, q * 128 : (q + 1) * 128] + both[32:, q * 128 : (q + 1) * 128]
            if s == 0:
                proj_out[q] = part
            else:
                proj_out[q] += part
    flat = y * 4 + r
    proj_x[flat] = proj_out[r]

    def hand_on(k, _):
        peer = lax.rem(flat + k, 16)
        to_r = lax.rem(peer, 4)
        send(
            proj_out.at[to_r], proj_x.at[flat], gx_send, gx_recv,
            col=peer // 4 * 4 + z, row=to_r,
        )
        return 0

    lax.fori_loop(1, 16, hand_on, 0)
    for d in range(8):
        stage[pl.ds(d, 128, stride=8), :] = dot(hidden_all[...], w_split[d])
    mixed[...] = stage[...].reshape(128, 8, 128).astype(bf16)
    arrived(proj_x.at[pl.ds(0, 15)], gx_recv)
    proj_z[z] = four([four([proj_x[q * 4 + g] for g in range(4)]) for q in range(4)])
    for k in others:
        send(proj_z.at[z], proj_z.at[z], gz_send, gz_recv.at[z], col=y * 4 + turn(z, k))
    arrived(grad_in.at[across], in_recv.at[across])
    send(grad_in.at[across], grad_in.at[across], in_send, in_recv.at[across], batch=sibling)
    for k in others:
        f = turn(i, k)
        arrived(own_hidden.at[f], oh_recv.at[f])
    arrived(every_cot.at[sibling], cot_recv.at[sibling])
    arrived(every_cot.at[diagonal], cot_recv.at[diagonal])
    for f in range(4):
        hidden_t[:, f * 128 : (f + 1) * 128] = jnp.transpose(own_hidden[f])

    def outer(d):
        cots = jnp.concatenate([every_cot[f, d] for f in range(4)], axis=0)
        grad_out[pl.ds(d, 512, stride=8), :] = dot(hidden_t[...], cots)

    for d in range(4):
        outer(d)
    for k in others:
        f = turn(z, k)
        arrived(proj_z.at[f], gz_recv.at[f])
    proj_b[i] = four(proj_z)
    for k in others:
        send(proj_b.at[i], proj_b.at[i], gb_send, gb_recv.at[i], batch=turn(i, k))
    for d in range(4, 8):
        outer(d)
    for k in others:
        f = turn(i, k)
        arrived(bias_all.at[f], bias_recv.at[f])
    grad_bias[...] = four(bias_all)
    for k in others:
        f = turn(i, k)
        arrived(proj_b.at[f], gb_recv.at[f])
    grad_proj[...] = four(proj_b)
    arrived(grad_in.at[sibling], in_recv.at[sibling])
    arrived(grad_in.at[diagonal], in_recv.at[diagonal])
    arrived(emb.at[pl.ds(0, 63)], emb_send)
    arrived(every_cot.at[three], cot_send)
    arrived(part_y.at[three], py_send)
    arrived(part_z.at[three], pz_send)
    arrived(part_x.at[three], px_send)
    arrived(raw.at[pl.ds(0, 15), 0], near_send)
    arrived(raw.at[pl.ds(0, 12)], far_send)
    arrived(pre_x.at[three], pre_send)
    arrived(hidden_all.at[:, pl.ds(0, 15 * 128)], h_send)
    arrived(own_hidden.at[three], oh_send)
    arrived(d_act.at[:, :, pl.ds(0, 12)], dy_send)
    arrived(d_z.at[:, pl.ds(0, 15)], dz_send)
    arrived(acts.at[three], acts_send)
    arrived(d_all.at[three], all_send)
    arrived(grad_in.at[three], in_send)
    arrived(bias_all.at[three], bias_send)
    arrived(proj_x.at[pl.ds(0, 15)], gx_send)
    arrived(proj_z.at[three], gz_send)
    arrived(proj_b.at[three], gb_send)


def everything(emb, proj, w_in, bias, w_out, cot):
    out = jax.ShapeDtypeStruct
    pair = [DMA, DMA((4,))]
    far = pl.BlockSpec(memory_space=pltpu.HBM)
    near = pl.BlockSpec(memory_space=VMEM)
    return pl.pallas_call(
        kernel,
        out_shape=(
            out((128, 8, 128), bf16),
            out((4096, 128), f32),
            out((4, 8, 128, 128), bf16),
            out((8, 128), f32),
            out((32, 128), f32),
        ),
        in_specs=[far, near, far, near, far, near],
        out_specs=[near] * 5,
        scratch_shapes=[
            VMEM((32, 128, 128), bf16),
            VMEM((2048, 8, 128), bf16),
            VMEM((8, 2048, 128), bf16),
            VMEM((1024, 128), f32),
            VMEM((4, 8, 128, 128), bf16),
            VMEM((4, 2, 16, 8, 128), bf16),
            VMEM((512, 128), f32),
            VMEM((2, 128, 128), f32),
            VMEM((2, 8, 128), f32),
            VMEM((4, 4, 128, 128), bf16),
            VMEM((4, 4, 128, 128), bf16),
            VMEM((4, 128, 128), bf16),
            VMEM((4, 128, 128), bf16),
            VMEM((4, 128, 128), f32),
            VMEM((4, 2, 32, 128), bf16),
            VMEM((16, 4, 2, 32, 128), bf16),
            VMEM((32, 16, 8, 128), bf16),
            VMEM((4, 128, 128), f32),
            VMEM((128, 128), bf16),
            VMEM((128, 128), bf16),
            VMEM((2, 16, 16, 8, 128), bf16),
            VMEM((2, 4, 16, 4, 8, 128), bf16),
            VMEM((2, 16, 2, 16, 128), bf16),
            VMEM((2, 16, 2, 16, 128), bf16),
            VMEM((4, 8, 16, 8, 128), bf16),
            VMEM((4, 128, 128), bf16),
            VMEM((4, 8, 128), f32),
            VMEM((128, 2048), bf16),
            VMEM((4, 128, 512), bf16),
            VMEM((512, 512), bf16),
            VMEM((4, 32, 128), f32),
            VMEM((16, 32, 128), f32),
            VMEM((4, 32, 128), f32),
            VMEM((4, 32, 128), f32),
            DMA, DMA, DMA, DMA, *pair,
            *pair, *pair, *pair,
            DMA, DMA, DMA((16,)), *pair,
            DMA, DMA((16,)), *pair, DMA, DMA((2, 4)), DMA, DMA((2,)),
            *pair, *pair, *pair, *pair,
            DMA, DMA, *pair, *pair, DMA,
        ],
        compiler_params=pltpu.CompilerParams(
            collective_id=0, has_side_effects=True, vmem_limit_bytes=49 << 20
        ),
        name="block",
    )(emb, proj, w_in, bias, w_out, cot)


def local(embeddings, projection, w_in, bias, w_out, cotangent):
    mixed, grad_out, grad_in, grad_bias, grad_proj = everything(
        embeddings.reshape(64, 2, 8, 128), projection.T, w_in.reshape(32, 128, 128),
        bias.reshape(1, 128), w_out, cotangent,
    )
    return (
        mixed, grad_out.reshape(512, 8, 128), grad_in.astype(f32).reshape(4096, 128),
        grad_bias[0], grad_proj.T,
    )


def solution(mesh):
    placed = (
        P("batch", "col", "row"),
        P(),
        P("row", "col"),
        P("col"),
        P(None, "col", "row"),
        P("batch", "col", "row"),
    )
    return jax.shard_map(
        local,
        mesh=mesh,
        in_specs=placed,
        out_specs=(
            P("batch", "col", "row"),
            P("batch", "col", "row"),
            P("row", "col"),
            P("col"),
            P("row", None),
        ),
        check_vma=False,
    )
```

```python
import jax
import jax.numpy as jnp
from jax import lax
from jax.experimental import pallas as pl
from jax.experimental.pallas import tpu as pltpu
from jax.sharding import PartitionSpec as P

epsilon = 1e-06
bf16 = jnp.bfloat16
f32 = jnp.float32
MESH = pl.DeviceIdType.MESH
VMEM = pltpu.VMEM
DMA = pltpu.SemaphoreType.DMA
others = (1, 2, 3)


def contract_last(left, right):
    return lax.dot_general(left, right, (((1,), (1,)), ((), ())), preferred_element_type=f32)


def contract_first(left, right):
    return lax.dot_general(left, right, (((0,), (0,)), ((), ())), preferred_element_type=f32)


def dot(left, right):
    return jnp.dot(left, right, preferred_element_type=f32)


def send(src, dst, send_sem, recv_sem, **place):
    copy = pltpu.make_async_remote_copy(
        src_ref=src, dst_ref=dst, send_sem=send_sem, recv_sem=recv_sem,
        device_id=place, device_id_type=MESH,
    )
    copy.start()


def arrived(ref, sem):
    pltpu.make_async_copy(ref, ref, sem).wait()


def split(value):
    high = value.astype(bf16)
    return high, (value - high.astype(f32)).astype(bf16)


def four(parts):
    return (parts[0] + parts[1]) + (parts[2] + parts[3])


def turn(place, k):
    return lax.rem(place + k, 4)


def lanes_of(slot, size=128):
    return pl.ds(pl.multiple_of(slot * size, size), size)


def whole_sum(value):
    return jnp.sum(jnp.sum(value, axis=0, keepdims=True), axis=1, keepdims=True)


def ordering(size, high):
    at = lax.broadcasted_iota(jnp.int32, (size, size), 0)
    of = lax.broadcasted_iota(jnp.int32, (size, size), 1)
    source = lax.rem(at, 8) // 2 * (2 * high) + lax.rem(at, 2) * high + at // 8
    return (of == source).astype(f32).astype(bf16)


def kernel(
    emb, proj_far, w_in_far, bias_far, w_out_far, cot_far,
    mixed, grad_out, grad_in, grad_bias, grad_proj,
    proj, w_in, bias, w_out, cot, w_split, stage, every_cot, own_emb, folds, normed, inv,
    part_out, part_y, part_z_out, part_z, part_x,
    to_row, raw, gathered, pre_x, hidden, d_pre_b,
    d_act, d_y, d_z_out, d_z, in_part, in_near, in_both, bias_all, hidden_all, own_hidden, hidden_t,
    proj_out, proj_x, proj_z, proj_b,
    load_in, load_out, load_cot, load_proj, load_bias, emb_send, emb_recv, cot_send, cot_recv,
    py_send, py_recv, pz_send, pz_recv, px_send, px_recv,
    near_send, far_send, raw_recv, pre_send, pre_recv,
    h_send, h_recv, oh_send, oh_recv, dy_send, dy_recv, dz_send, dz_recv,
    near_in_send, near_in_recv, both_send, both_recv, in_send, in_recv, bias_send, bias_recv,
    gx_send, gx_recv, gz_send, gz_recv, gb_send, gb_recv,
):
    i = lax.axis_index("batch")
    r = lax.axis_index("row")
    c = lax.axis_index("col")
    y = c // 4
    z = c - y * 4
    sibling = i + 1 - 2 * lax.rem(i, 2)
    across = turn(i, 2)
    diagonal = turn(sibling, 2)
    me = c * 4 + r
    three = pl.ds(0, 3)
    barrier = pltpu.get_barrier_semaphore()

    def greet(k, _):
        peer = lax.rem(me + k, 64)
        pl.semaphore_signal(
            barrier, inc=1, device_id={"col": peer // 4, "row": lax.rem(peer, 4)},
            device_id_type=MESH,
        )
        return 0

    lax.fori_loop(1, 64, greet, 0)
    for k in others:
        pl.semaphore_signal(barrier, inc=1, device_id={"batch": turn(i, k)}, device_id_type=MESH)
    take_cot = pltpu.make_async_copy(cot_far, cot, load_cot)
    take_cot.start()
    take_out = []
    for k in (1, 2, 3, 0):
        at = lanes_of(turn(y, k), 512)
        take_out.append(pltpu.make_async_copy(w_out_far.at[at], w_out.at[at], load_out.at[k]))
        take_out[-1].start()
    take_proj = pltpu.make_async_copy(proj_far, proj, load_proj)
    take_proj.start()
    take_bias = pltpu.make_async_copy(bias_far, bias, load_bias)
    take_bias.start()
    take_in = pltpu.make_async_copy(w_in_far, w_in, load_in)
    take_in.start()
    take_cot.wait()
    stage[...] = cot[...].astype(f32).reshape(1024, 128)
    for d in range(8):
        every_cot[i, d] = stage[pl.ds(d, 128, stride=8), :].astype(bf16)

    def from_output(k):
        to = turn(y, k)

        def divide(n, _):
            at = pl.multiple_of(to * 512 + n * 128, 128)
            stage[...] = w_out[pl.ds(at, 128)].astype(f32).reshape(1024, 128)
            for d in range(8):
                w_split[d, pl.ds(at, 128), :] = stage[pl.ds(d, 128, stride=8), :].astype(bf16)
            return 0

        lax.fori_loop(0, 4, divide, 0)
        part = jnp.zeros((128, 512), f32)
        for d in range(8):
            part = part + contract_last(every_cot[i, d], w_split[d, lanes_of(to, 512), :])
        for q in range(4):
            part_out[to, q] = part[:, q * 128 : (q + 1) * 128].astype(bf16)

    def share_output(k):
        to = turn(y, k)
        send(part_out.at[to], part_y.at[y], py_send, py_recv.at[y], col=to * 4 + z)

    for n in (0, 1):
        take_out[n].wait()
        from_output(n + 1)
    pl.semaphore_wait(barrier, 66)

    keep = pltpu.make_async_copy(emb.at[me], own_emb.at[r, :, c], emb_recv)
    keep.start()

    def give(k, _):
        peer = lax.rem(me + k, 64)
        send(
            emb.at[peer], own_emb.at[r, :, c], emb_send, emb_recv,
            col=peer // 4, row=lax.rem(peer, 4),
        )
        return 0

    lax.fori_loop(1, 64, give, 0)
    share_output(1)
    share_output(2)
    take_out[2].wait()
    from_output(3)
    share_output(3)
    take_out[3].wait()
    from_output(0)
    part_y[y] = part_out[y]
    take_proj.wait()
    take_bias.wait()
    lanes = lax.broadcasted_iota(jnp.int32, (32, 128), 1)
    ranks = lax.broadcasted_iota(jnp.int32, (32, 128), 0)
    repeat = (lax.rem(lanes, 32) == ranks).astype(f32).astype(bf16)
    wide = contract_first(proj[...], repeat).astype(bf16)
    block = lax.broadcasted_iota(jnp.int32, (128, 128), 1) // 32
    order = ordering(256, 32)

    def sample(s):
        return jnp.concatenate([own_emb[q, s].reshape(128, 128) for q in range(4)], axis=1)

    arrived(own_emb, emb_recv)
    for s in range(2):
        own = sample(s)
        high, low = split(dot(own, wide))
        both = contract_first(own, jnp.concatenate([high, low], axis=1))
        folds[...] = both[:, :128] + both[:, 128:]
        inter = jnp.zeros((128, 128), f32)
        for j in range(4):
            inter = jnp.where(block == j, folds[pl.ds(j, 128, stride=4), :], inter)
        scale = lax.rsqrt(whole_sum(inter * inter) / (512 * 32) + epsilon)
        norm = inter * scale
        normed[s] = norm
        inv[s] = jnp.broadcast_to(scale, (8, 128))
        for q in range(4):
            to_row[q, s] = norm[q * 32 : (q + 1) * 32].astype(bf16)
    raw[c, r] = to_row[r]
    plane = z * 4 + r

    def scatter(k, _):
        peer = lax.rem(plane + k, 16)
        to_z = peer // 4
        to_r = lax.rem(peer, 4)
        send(to_row.at[to_r], raw.at[c, r], near_send, raw_recv.at[c], col=y * 4 + to_z, row=to_r)
        return 0

    lax.fori_loop(1, 16, scatter, 0)

    for k in others:
        f = turn(y, k)
        arrived(part_y.at[f], py_recv.at[f])
    for q in range(4):
        part_z_out[q] = four([part_y[f, q].astype(f32) for f in range(4)]).astype(bf16)
    part_z[z] = part_z_out[z]
    for k in others:
        to = turn(z, k)
        send(part_z_out.at[to], part_z.at[z], pz_send, pz_recv.at[z], col=y * 4 + to)

    arrived(raw.at[c, three], raw_recv.at[c])
    for k in others:
        send(raw.at[c], raw.at[c], far_send, raw_recv.at[c], col=turn(y, k) * 4 + z)
    for m in (1, 3, 2):
        slot = y * 4 + turn(z, m)
        arrived(raw.at[slot], raw_recv.at[slot])
        for k in others:
            send(raw.at[slot], raw.at[slot], far_send, raw_recv.at[slot], col=turn(y, k) * 4 + z)
    send(every_cot.at[i], every_cot.at[i], cot_send, cot_recv.at[i], batch=sibling)
    send(every_cot.at[i], every_cot.at[i], cot_send, cot_recv.at[i], batch=across)

    def lay(slot):
        rows = dot(order, raw[slot].reshape(256, 128))
        gathered[:, slot] = rows.reshape(32, 8, 128).astype(bf16)

    for q in range(4):
        lay(y * 4 + q)
    for k in others:
        f = turn(z, k)
        arrived(part_z.at[f], pz_recv.at[f])
    part_x[r] = four([part_z[f].astype(f32) for f in range(4)])
    for k in others:
        send(part_x.at[r], part_x.at[r], px_send, px_recv.at[r], row=turn(r, k))
    take_in.wait()
    for k in range(4):
        for m in others:
            slot = turn(y, m) * 4 + turn(z, k)
            arrived(raw.at[slot], raw_recv.at[slot])
            lay(slot)
    pre = jnp.zeros((128, 128), f32)
    for e in range(32):
        pre = pre + dot(gathered[e].reshape(128, 128), w_in[e])
    pre_x[r] = pre
    for k in others:
        send(pre_x.at[r], pre_x.at[r], pre_send, pre_recv.at[r], row=turn(r, k))
    for k in others:
        f = turn(r, k)
        arrived(part_x.at[f], px_recv.at[f])
    d_hidden = four(part_x)
    for k in others:
        f = turn(r, k)
        arrived(pre_x.at[f], pre_recv.at[f])
    preact = four(pre_x) + bias[...]
    sig = 1.0 / (1.0 + jnp.exp(-preact))
    hidden[...] = (preact * sig).astype(bf16)
    d_value = d_hidden * sig * (1.0 + preact * (1.0 - sig))
    d_pre_b[...] = d_value.astype(bf16)
    bias_all[i] = jnp.broadcast_to(jnp.sum(d_value, axis=0, keepdims=True), (8, 128))

    for k in others:
        send(hidden, hidden_all.at[:, lanes_of(c)], h_send, h_recv.at[c], col=y * 4 + turn(z, k))
    for half in range(4):
        for e in range(8):
            part = contract_last(d_pre_b[...], w_in[half * 8 + e])
            d_act[half, e] = part.reshape(16, 8, 128).astype(bf16)
        for k in others:
            to = turn(y, k)
            send(
                d_act.at[half, :, pl.ds(4 * to, 4)], d_y.at[half, y],
                dy_send, dy_recv.at[half, y], col=to * 4 + z,
            )
    for k in others:
        send(hidden, hidden_all.at[:, lanes_of(c)], h_send, h_recv.at[c], col=turn(y, k) * 4 + z)
    hidden_all[:, lanes_of(c)] = hidden[...]
    for k in others:
        to = turn(i, k)
        send(bias_all.at[i], bias_all.at[i], bias_send, bias_recv.at[i], batch=to)
    arrived(every_cot.at[across], cot_recv.at[across])
    send(every_cot.at[across], every_cot.at[across], cot_send, cot_recv.at[across], batch=sibling)
    core = lax.rem(i, 2)
    chip = i // 2
    for h in range(2):
        for e in range(16):
            in_part[h, e] = contract_first(gathered[h * 16 + e].reshape(128, 128), d_pre_b[...])
    send(in_part.at[1 - core], in_near, near_in_send, near_in_recv, batch=sibling)
    for m in (1, 3, 2):
        slot = y * 4 + turn(z, m)
        place = hidden_all.at[:, lanes_of(slot)]
        arrived(place, h_recv.at[slot])
        for k in others:
            send(place, place, h_send, h_recv.at[slot], col=turn(y, k) * 4 + z)
    undo = ordering(64, 8)
    for half in range(4):
        d_y[half, y] = d_act[half, :, pl.ds(4 * y, 4)]
        for k in others:
            f = turn(y, k)
            arrived(d_y.at[half, f], dy_recv.at[half, f])
        for q in range(4):
            part = four([d_y[half, f, :, q].astype(f32) for f in range(4)])
            rows = contract_first(undo, part.reshape(64, 128).astype(bf16))
            for g in range(4):
                d_z_out[half, q * 4 + g] = (
                    rows[g * 16 : (g + 1) * 16].reshape(2, 8, 128).astype(bf16)
                )
        d_z[half, plane] = d_z_out[half, plane]

        def hand(k, _):
            peer = lax.rem(plane + k, 16)
            send(
                d_z_out.at[half, peer], d_z.at[half, plane], dz_send, dz_recv.at[half],
                col=y * 4 + peer // 4, row=lax.rem(peer, 4),
            )
            return 0

        lax.fori_loop(1, 16, hand, 0)
        if half == 0:
            arrived(in_near, near_in_recv)
            in_both[chip] = (in_part[core] + in_near[...]).astype(bf16)
            send(in_both.at[chip], in_both.at[chip], both_send, both_recv, batch=across)
    for m in others:
        for k in range(4):
            slot = turn(y, m) * 4 + k
            arrived(hidden_all.at[:, lanes_of(slot)], h_recv.at[slot])
    for k in others:
        to = turn(i, k)
        send(
            hidden_all.at[:, lanes_of(to, 512)], own_hidden.at[i], oh_send, oh_recv.at[i],
            batch=to,
        )
    own_hidden[i] = hidden_all[:, lanes_of(i, 512)]
    for half in range(4):
        arrived(d_z.at[half, pl.ds(0, 15)], dz_recv.at[half])
    for s in range(2):
        grad = jnp.concatenate(
            [
                four([d_z[half, q * 4 + g, s].astype(f32) for q in range(4)])
                for g in range(4)
                for half in range(4)
            ],
            axis=0,
        )
        norm = normed[s]
        inner = whole_sum(grad * norm) / (512 * 32)
        d_inter = (inv[s, 0:1, :] * (grad - norm * inner)).astype(bf16).astype(f32)
        for j in range(4):
            folds[pl.ds(j, 128, stride=4), :] = jnp.where(block == j, d_inter, 0.0)
        own = sample(s)
        fold = dot(own, folds[...].astype(bf16))
        fold = fold + pltpu.roll(fold, 32, 1)
        fold = fold + pltpu.roll(fold, 64, 1)
        high, low = split(jnp.transpose(fold)[:32])
        both = dot(jnp.concatenate([high, low], axis=0), own)
        for q in range(4):
            part = both[:32, q * 128 : (q + 1) * 128] + both[32:, q * 128 : (q + 1) * 128]
            if s == 0:
                proj_out[q] = part
            else:
                proj_out[q] += part
    flat = y * 4 + r
    proj_x[flat] = proj_out[r]

    def hand_on(k, _):
        peer = lax.rem(flat + k, 16)
        to_r = lax.rem(peer, 4)
        send(
            proj_out.at[to_r], proj_x.at[flat], gx_send, gx_recv,
            col=peer // 4 * 4 + z, row=to_r,
        )
        return 0

    lax.fori_loop(1, 16, hand_on, 0)
    for d in range(8):
        stage[pl.ds(d, 128, stride=8), :] = dot(hidden_all[...], w_split[d])
    mixed[...] = stage[...].reshape(128, 8, 128).astype(bf16)
    arrived(proj_x.at[pl.ds(0, 15)], gx_recv)
    proj_z[z] = four([four([proj_x[q * 4 + g] for g in range(4)]) for q in range(4)])
    for k in others:
        send(proj_z.at[z], proj_z.at[z], gz_send, gz_recv.at[z], col=y * 4 + turn(z, k))
    arrived(in_both.at[1 - chip], both_recv)
    grad_in[core] = in_both[0].astype(f32) + in_both[1].astype(f32)
    send(grad_in.at[core], grad_in.at[core], in_send, in_recv, batch=sibling)
    for k in others:
        f = turn(i, k)
        arrived(own_hidden.at[f], oh_recv.at[f])
    arrived(every_cot.at[sibling], cot_recv.at[sibling])
    arrived(every_cot.at[diagonal], cot_recv.at[diagonal])
    for f in range(4):
        hidden_t[:, f * 128 : (f + 1) * 128] = jnp.transpose(own_hidden[f])

    def outer(d):
        cots = jnp.concatenate([every_cot[f, d] for f in range(4)], axis=0)
        grad_out[pl.ds(d, 512, stride=8), :] = dot(hidden_t[...], cots)

    for d in range(4):
        outer(d)
    for k in others:
        f = turn(z, k)
        arrived(proj_z.at[f], gz_recv.at[f])
    proj_b[i] = four(proj_z)
    for k in others:
        send(proj_b.at[i], proj_b.at[i], gb_send, gb_recv.at[i], batch=turn(i, k))
    for d in range(4, 8):
        outer(d)
    for k in others:
        f = turn(i, k)
        arrived(bias_all.at[f], bias_recv.at[f])
    grad_bias[...] = four(bias_all)
    for k in others:
        f = turn(i, k)
        arrived(proj_b.at[f], gb_recv.at[f])
    grad_proj[...] = four(proj_b)
    arrived(grad_in.at[1 - core], in_recv)
    arrived(emb.at[pl.ds(0, 63)], emb_send)
    arrived(every_cot.at[three], cot_send)
    arrived(part_y.at[three], py_send)
    arrived(part_z.at[three], pz_send)
    arrived(part_x.at[three], px_send)
    arrived(raw.at[pl.ds(0, 15), 0], near_send)
    arrived(raw.at[pl.ds(0, 12)], far_send)
    arrived(pre_x.at[three], pre_send)
    arrived(hidden_all.at[:, pl.ds(0, 15 * 128)], h_send)
    arrived(own_hidden.at[three], oh_send)
    arrived(d_act.at[:, :, pl.ds(0, 12)], dy_send)
    arrived(d_z.at[:, pl.ds(0, 15)], dz_send)
    arrived(in_near, near_in_send)
    arrived(in_both.at[chip], both_send)
    arrived(grad_in.at[core], in_send)
    arrived(bias_all.at[three], bias_send)
    arrived(proj_x.at[pl.ds(0, 15)], gx_send)
    arrived(proj_z.at[three], gz_send)
    arrived(proj_b.at[three], gb_send)


def everything(emb, proj, w_in, bias, w_out, cot):
    out = jax.ShapeDtypeStruct
    pair = [DMA, DMA((4,))]
    far = pl.BlockSpec(memory_space=pltpu.HBM)
    near = pl.BlockSpec(memory_space=VMEM)
    return pl.pallas_call(
        kernel,
        out_shape=(
            out((128, 8, 128), bf16),
            out((4096, 128), f32),
            out((2, 16, 128, 128), f32),
            out((8, 128), f32),
            out((32, 128), f32),
        ),
        in_specs=[far] * 6,
        out_specs=[near] * 5,
        scratch_shapes=[
            VMEM((32, 512), bf16),
            VMEM((32, 128, 128), bf16),
            VMEM((1, 128), f32),
            VMEM((2048, 8, 128), bf16),
            VMEM((128, 8, 128), bf16),
            VMEM((8, 2048, 128), bf16),
            VMEM((1024, 128), f32),
            VMEM((4, 8, 128, 128), bf16),
            VMEM((4, 2, 16, 8, 128), bf16),
            VMEM((512, 128), f32),
            VMEM((2, 128, 128), f32),
            VMEM((2, 8, 128), f32),
            VMEM((4, 4, 128, 128), bf16),
            VMEM((4, 4, 128, 128), bf16),
            VMEM((4, 128, 128), bf16),
            VMEM((4, 128, 128), bf16),
            VMEM((4, 128, 128), f32),
            VMEM((4, 2, 32, 128), bf16),
            VMEM((16, 4, 2, 32, 128), bf16),
            VMEM((32, 16, 8, 128), bf16),
            VMEM((4, 128, 128), f32),
            VMEM((128, 128), bf16),
            VMEM((128, 128), bf16),
            VMEM((4, 8, 16, 8, 128), bf16),
            VMEM((4, 4, 8, 4, 8, 128), bf16),
            VMEM((4, 16, 2, 8, 128), bf16),
            VMEM((4, 16, 2, 8, 128), bf16),
            VMEM((2, 16, 128, 128), f32),
            VMEM((16, 128, 128), f32),
            VMEM((2, 16, 128, 128), bf16),
            VMEM((4, 8, 128), f32),
            VMEM((128, 2048), bf16),
            VMEM((4, 128, 512), bf16),
            VMEM((512, 512), bf16),
            VMEM((4, 32, 128), f32),
            VMEM((16, 32, 128), f32),
            VMEM((4, 32, 128), f32),
            VMEM((4, 32, 128), f32),
            DMA, DMA((4,)), DMA, DMA, DMA, DMA, DMA, *pair,
            *pair, *pair, *pair,
            DMA, DMA, DMA((16,)), *pair,
            DMA, DMA((16,)), *pair, DMA, DMA((4, 4)), DMA, DMA((4,)),
            DMA, DMA, DMA, DMA, DMA, DMA, *pair,
            DMA, DMA, *pair, *pair,
        ],
        compiler_params=pltpu.CompilerParams(
            collective_id=0, has_side_effects=True, vmem_limit_bytes=49 << 20
        ),
        name="block",
    )(*[pltpu.with_memory_space_constraint(a, pltpu.HBM) for a in (emb, proj, w_in, bias, w_out, cot)])


def local(embeddings, projection, w_in, bias, w_out, cotangent):
    mixed, grad_out, grad_in, grad_bias, grad_proj = everything(
        embeddings.reshape(64, 2, 8, 128), projection.T, w_in.reshape(32, 128, 128),
        bias.reshape(1, 128), w_out, cotangent,
    )
    return (
        mixed, grad_out.reshape(512, 8, 128), grad_in.reshape(4096, 128),
        grad_bias[0], grad_proj.T,
    )


def solution(mesh):
    placed = (
        P("batch", "col", "row"),
        P(),
        P("row", "col"),
        P("col"),
        P(None, "col", "row"),
        P("batch", "col", "row"),
    )
    return jax.shard_map(
        local,
        mesh=mesh,
        in_specs=placed,
        out_specs=(
            P("batch", "col", "row"),
            P("batch", "col", "row"),
            P("row", "col"),
            P("col"),
            P("row", None),
        ),
        check_vma=False,
    )
```

```python
import jax
import jax.numpy as jnp
from jax import lax
from jax.experimental import pallas as pl
from jax.experimental.pallas import tpu as pltpu
from jax.sharding import PartitionSpec as P

epsilon = 1e-06
bf16 = jnp.bfloat16
f32 = jnp.float32
MESH = pl.DeviceIdType.MESH
VMEM = pltpu.VMEM
DMA = pltpu.SemaphoreType.DMA
others = (1, 2, 3)


def contract_last(left, right):
    return lax.dot_general(left, right, (((1,), (1,)), ((), ())), preferred_element_type=f32)


def contract_first(left, right):
    return lax.dot_general(left, right, (((0,), (0,)), ((), ())), preferred_element_type=f32)


def dot(left, right):
    return jnp.dot(left, right, preferred_element_type=f32)


def send(src, dst, send_sem, recv_sem, **place):
    copy = pltpu.make_async_remote_copy(
        src_ref=src, dst_ref=dst, send_sem=send_sem, recv_sem=recv_sem,
        device_id=place, device_id_type=MESH,
    )
    copy.start()


def arrived(ref, sem):
    pltpu.make_async_copy(ref, ref, sem).wait()


def split(value):
    high = value.astype(bf16)
    return high, (value - high.astype(f32)).astype(bf16)


def four(parts):
    return (parts[0] + parts[1]) + (parts[2] + parts[3])


def turn(place, k):
    return lax.rem(place + k, 4)


def lanes_of(slot, size=128):
    return pl.ds(pl.multiple_of(slot * size, size), size)


def whole_sum(value):
    return jnp.sum(jnp.sum(value, axis=0, keepdims=True), axis=1, keepdims=True)


def ordering(size, high):
    at = lax.broadcasted_iota(jnp.int32, (size, size), 0)
    of = lax.broadcasted_iota(jnp.int32, (size, size), 1)
    source = lax.rem(at, 8) // 2 * (2 * high) + lax.rem(at, 2) * high + at // 8
    return (of == source).astype(f32).astype(bf16)


def kernel(
    emb, proj_far, w_in_far, bias_far, w_out_far, cot_far,
    mixed, grad_out, grad_in, grad_bias, grad_proj,
    proj, w_in, bias, w_out, cot, w_split, stage, every_cot, own_emb, folds, normed, inv,
    part_out, part_y, part_z_out, part_z, part_x,
    to_row, raw, gathered, pre_x, hidden, d_pre_b,
    d_act, d_y, d_z_out, d_z, acts, d_all, bias_all, hidden_all, own_hidden, hidden_t,
    proj_out, proj_x, proj_z, proj_b,
    load_in, load_out, load_cot, load_proj, load_bias, emb_send, emb_recv, cot_send, cot_recv,
    py_send, py_recv, pz_send, pz_recv, px_send, px_recv,
    near_send, far_send, raw_recv, pre_send, pre_recv,
    h_send, h_recv, oh_send, oh_recv, dy_send, dy_recv, dz_send, dz_recv,
    acts_send, acts_recv, all_send, all_recv, in_send, in_recv, bias_send, bias_recv,
    gx_send, gx_recv, gz_send, gz_recv, gb_send, gb_recv, own_sem,
):
    i = lax.axis_index("batch")
    r = lax.axis_index("row")
    c = lax.axis_index("col")
    y = c // 4
    z = c - y * 4
    sibling = i + 1 - 2 * lax.rem(i, 2)
    across = turn(i, 2)
    diagonal = turn(sibling, 2)
    me = c * 4 + r
    three = pl.ds(0, 3)
    barrier = pltpu.get_barrier_semaphore()

    def greet(k, _):
        peer = lax.rem(me + k, 64)
        pl.semaphore_signal(
            barrier, inc=1, device_id={"col": peer // 4, "row": lax.rem(peer, 4)},
            device_id_type=MESH,
        )
        return 0

    lax.fori_loop(1, 64, greet, 0)
    for k in others:
        pl.semaphore_signal(barrier, inc=1, device_id={"batch": turn(i, k)}, device_id_type=MESH)
    take_cot = pltpu.make_async_copy(cot_far, cot, load_cot)
    take_cot.start()
    take_out = []
    for k in (1, 2, 3, 0):
        at = lanes_of(turn(y, k), 512)
        take_out.append(pltpu.make_async_copy(w_out_far.at[at], w_out.at[at], load_out.at[k]))
        take_out[-1].start()
    take_proj = pltpu.make_async_copy(proj_far, proj, load_proj)
    take_proj.start()
    take_bias = pltpu.make_async_copy(bias_far, bias, load_bias)
    take_bias.start()
    take_in = pltpu.make_async_copy(w_in_far, w_in, load_in)
    take_in.start()
    take_cot.wait()
    stage[...] = cot[...].astype(f32).reshape(1024, 128)
    for d in range(8):
        every_cot[i, d] = stage[pl.ds(d, 128, stride=8), :].astype(bf16)

    def from_output(k):
        to = turn(y, k)

        def divide(n, _):
            at = pl.multiple_of(to * 512 + n * 128, 128)
            stage[...] = w_out[pl.ds(at, 128)].astype(f32).reshape(1024, 128)
            for d in range(8):
                w_split[d, pl.ds(at, 128), :] = stage[pl.ds(d, 128, stride=8), :].astype(bf16)
            return 0

        lax.fori_loop(0, 4, divide, 0)
        part = jnp.zeros((128, 512), f32)
        for d in range(8):
            part = part + contract_last(every_cot[i, d], w_split[d, lanes_of(to, 512), :])
        for q in range(4):
            part_out[to, q] = part[:, q * 128 : (q + 1) * 128].astype(bf16)

    def share_output(k):
        to = turn(y, k)
        send(part_out.at[to], part_y.at[y], py_send, py_recv.at[y], col=to * 4 + z)

    for n in (0, 1):
        take_out[n].wait()
        from_output(n + 1)
    pl.semaphore_wait(barrier, 66)

    keep = pltpu.make_async_copy(emb.at[me], own_emb.at[r, :, c], emb_recv)
    keep.start()

    def give(k, _):
        peer = lax.rem(me + k, 64)
        send(
            emb.at[peer], own_emb.at[r, :, c], emb_send, emb_recv,
            col=peer // 4, row=lax.rem(peer, 4),
        )
        return 0

    lax.fori_loop(1, 64, give, 0)
    share_output(1)
    share_output(2)
    take_out[2].wait()
    from_output(3)
    share_output(3)
    take_out[3].wait()
    from_output(0)
    part_y[y] = part_out[y]
    take_proj.wait()
    take_bias.wait()
    lanes = lax.broadcasted_iota(jnp.int32, (32, 128), 1)
    ranks = lax.broadcasted_iota(jnp.int32, (32, 128), 0)
    repeat = (lax.rem(lanes, 32) == ranks).astype(f32).astype(bf16)
    wide = contract_first(proj[...], repeat).astype(bf16)
    block = lax.broadcasted_iota(jnp.int32, (128, 128), 1) // 32
    order = ordering(256, 32)

    def sample(s):
        return jnp.concatenate([own_emb[q, s].reshape(128, 128) for q in range(4)], axis=1)

    arrived(own_emb, emb_recv)
    for s in range(2):
        own = sample(s)
        high, low = split(dot(own, wide))
        both = contract_first(own, jnp.concatenate([high, low], axis=1))
        folds[...] = both[:, :128] + both[:, 128:]
        inter = jnp.zeros((128, 128), f32)
        for j in range(4):
            inter = jnp.where(block == j, folds[pl.ds(j, 128, stride=4), :], inter)
        scale = lax.rsqrt(whole_sum(inter * inter) / (512 * 32) + epsilon)
        norm = inter * scale
        normed[s] = norm
        inv[s] = jnp.broadcast_to(scale, (8, 128))
        for q in range(4):
            to_row[q, s] = norm[q * 32 : (q + 1) * 32].astype(bf16)
    raw[c, r] = to_row[r]
    plane = z * 4 + r

    def scatter(k, _):
        peer = lax.rem(plane + k, 16)
        to_z = peer // 4
        to_r = lax.rem(peer, 4)
        send(to_row.at[to_r], raw.at[c, r], near_send, raw_recv.at[c], col=y * 4 + to_z, row=to_r)
        return 0

    lax.fori_loop(1, 16, scatter, 0)

    for k in others:
        f = turn(y, k)
        arrived(part_y.at[f], py_recv.at[f])
    for q in range(4):
        part_z_out[q] = four([part_y[f, q].astype(f32) for f in range(4)]).astype(bf16)
    part_z[z] = part_z_out[z]
    for k in others:
        to = turn(z, k)
        send(part_z_out.at[to], part_z.at[z], pz_send, pz_recv.at[z], col=y * 4 + to)

    arrived(raw.at[c, three], raw_recv.at[c])
    for k in others:
        send(raw.at[c], raw.at[c], far_send, raw_recv.at[c], col=turn(y, k) * 4 + z)
    for m in (1, 3, 2):
        slot = y * 4 + turn(z, m)
        arrived(raw.at[slot], raw_recv.at[slot])
        for k in others:
            send(raw.at[slot], raw.at[slot], far_send, raw_recv.at[slot], col=turn(y, k) * 4 + z)
    send(every_cot.at[i], every_cot.at[i], cot_send, cot_recv.at[i], batch=sibling)
    send(every_cot.at[i], every_cot.at[i], cot_send, cot_recv.at[i], batch=across)

    def lay(slot):
        rows = dot(order, raw[slot].reshape(256, 128))
        gathered[:, slot] = rows.reshape(32, 8, 128).astype(bf16)

    for q in range(4):
        lay(y * 4 + q)
    for k in others:
        f = turn(z, k)
        arrived(part_z.at[f], pz_recv.at[f])
    part_x[r] = four([part_z[f].astype(f32) for f in range(4)])
    for k in others:
        send(part_x.at[r], part_x.at[r], px_send, px_recv.at[r], row=turn(r, k))
    take_in.wait()
    for k in range(4):
        for m in others:
            slot = turn(y, m) * 4 + turn(z, k)
            arrived(raw.at[slot], raw_recv.at[slot])
            lay(slot)
    pre = jnp.zeros((128, 128), f32)
    for e in range(32):
        pre = pre + dot(gathered[e].reshape(128, 128), w_in[e])
    pre_x[r] = pre
    for k in others:
        send(pre_x.at[r], pre_x.at[r], pre_send, pre_recv.at[r], row=turn(r, k))
    for k in others:
        to = turn(i, k)
        send(gathered.at[pl.ds(8 * to, 8)], acts.at[i], acts_send, acts_recv.at[i], batch=to)
    mine = pltpu.make_async_copy(gathered.at[pl.ds(8 * i, 8)], acts.at[i], own_sem)
    mine.start()
    for k in others:
        f = turn(r, k)
        arrived(part_x.at[f], px_recv.at[f])
    d_hidden = four(part_x)
    for k in others:
        f = turn(r, k)
        arrived(pre_x.at[f], pre_recv.at[f])
    preact = four(pre_x) + bias[...]
    sig = 1.0 / (1.0 + jnp.exp(-preact))
    hidden[...] = (preact * sig).astype(bf16)
    d_value = d_hidden * sig * (1.0 + preact * (1.0 - sig))
    d_pre_b[...] = d_value.astype(bf16)
    bias_all[i] = jnp.broadcast_to(jnp.sum(d_value, axis=0, keepdims=True), (8, 128))

    for k in others:
        send(hidden, hidden_all.at[:, lanes_of(c)], h_send, h_recv.at[c], col=y * 4 + turn(z, k))
    for half in range(2):
        for e in range(16):
            part = contract_last(d_pre_b[...], w_in[half * 16 + e])
            d_act[half, e] = part.reshape(16, 8, 128).astype(bf16)
        for k in others:
            to = turn(y, k)
            send(
                d_act.at[half, :, pl.ds(4 * to, 4)], d_y.at[half, y],
                dy_send, dy_recv.at[half, y], col=to * 4 + z,
            )
    for k in others:
        send(hidden, hidden_all.at[:, lanes_of(c)], h_send, h_recv.at[c], col=turn(y, k) * 4 + z)
    hidden_all[:, lanes_of(c)] = hidden[...]
    d_all[i] = d_pre_b[...]
    for k in others:
        to = turn(i, k)
        send(d_pre_b, d_all.at[i], all_send, all_recv.at[i], batch=to)
        send(bias_all.at[i], bias_all.at[i], bias_send, bias_recv.at[i], batch=to)
    for m in others:
        slot = y * 4 + turn(z, m)
        place = hidden_all.at[:, lanes_of(slot)]
        arrived(place, h_recv.at[slot])
        for k in others:
            send(place, place, h_send, h_recv.at[slot], col=turn(y, k) * 4 + z)
    arrived(every_cot.at[across], cot_recv.at[across])
    send(every_cot.at[across], every_cot.at[across], cot_send, cot_recv.at[across], batch=sibling)
    undo = ordering(128, 16)
    for half in range(2):
        d_y[half, y] = d_act[half, :, pl.ds(4 * y, 4)]
        for k in others:
            f = turn(y, k)
            arrived(d_y.at[half, f], dy_recv.at[half, f])
        for q in range(4):
            part = four([d_y[half, f, :, q].astype(f32) for f in range(4)])
            rows = contract_first(undo, part.reshape(128, 128).astype(bf16))
            for g in range(4):
                d_z_out[half, q * 4 + g] = (
                    rows[g * 32 : (g + 1) * 32].reshape(2, 16, 128).astype(bf16)
                )
        d_z[half, plane] = d_z_out[half, plane]

        def hand(k, _):
            peer = lax.rem(plane + k, 16)
            send(
                d_z_out.at[half, peer], d_z.at[half, plane], dz_send, dz_recv.at[half],
                col=y * 4 + peer // 4, row=lax.rem(peer, 4),
            )
            return 0

        lax.fori_loop(1, 16, hand, 0)
    for m in others:
        for k in range(4):
            slot = turn(y, m) * 4 + k
            arrived(hidden_all.at[:, lanes_of(slot)], h_recv.at[slot])
    for k in others:
        to = turn(i, k)
        send(
            hidden_all.at[:, lanes_of(to, 512)], own_hidden.at[i], oh_send, oh_recv.at[i],
            batch=to,
        )
    own_hidden[i] = hidden_all[:, lanes_of(i, 512)]
    mine.wait()
    for k in others:
        f = turn(i, k)
        arrived(d_all.at[f], all_recv.at[f])
        arrived(acts.at[f], acts_recv.at[f])
    for e in range(8):
        part = four([contract_first(acts[f, e].reshape(128, 128), d_all[f]) for f in range(4)])
        grad_in[i, e] = part.astype(bf16)
    send(grad_in.at[i], grad_in.at[i], in_send, in_recv.at[i], batch=sibling)
    send(grad_in.at[i], grad_in.at[i], in_send, in_recv.at[i], batch=across)
    for half in range(2):
        arrived(d_z.at[half, pl.ds(0, 15)], dz_recv.at[half])
    for s in range(2):
        grad = jnp.concatenate(
            [
                four([d_z[half, q * 4 + g, s].astype(f32) for q in range(4)])
                for g in range(4)
                for half in range(2)
            ],
            axis=0,
        )
        norm = normed[s]
        inner = whole_sum(grad * norm) / (512 * 32)
        d_inter = (inv[s, 0:1, :] * (grad - norm * inner)).astype(bf16).astype(f32)
        for j in range(4):
            folds[pl.ds(j, 128, stride=4), :] = jnp.where(block == j, d_inter, 0.0)
        own = sample(s)
        fold = dot(own, folds[...].astype(bf16))
        fold = fold + pltpu.roll(fold, 32, 1)
        fold = fold + pltpu.roll(fold, 64, 1)
        high, low = split(jnp.transpose(fold)[:32])
        both = dot(jnp.concatenate([high, low], axis=0), own)
        for q in range(4):
            part = both[:32, q * 128 : (q + 1) * 128] + both[32:, q * 128 : (q + 1) * 128]
            if s == 0:
                proj_out[q] = part
            else:
                proj_out[q] += part
    flat = y * 4 + r
    proj_x[flat] = proj_out[r]

    def hand_on(k, _):
        peer = lax.rem(flat + k, 16)
        to_r = lax.rem(peer, 4)
        send(
            proj_out.at[to_r], proj_x.at[flat], gx_send, gx_recv,
            col=peer // 4 * 4 + z, row=to_r,
        )
        return 0

    lax.fori_loop(1, 16, hand_on, 0)
    for d in range(8):
        stage[pl.ds(d, 128, stride=8), :] = dot(hidden_all[...], w_split[d])
    mixed[...] = stage[...].reshape(128, 8, 128).astype(bf16)
    arrived(proj_x.at[pl.ds(0, 15)], gx_recv)
    proj_z[z] = four([four([proj_x[q * 4 + g] for g in range(4)]) for q in range(4)])
    for k in others:
        send(proj_z.at[z], proj_z.at[z], gz_send, gz_recv.at[z], col=y * 4 + turn(z, k))
    arrived(grad_in.at[across], in_recv.at[across])
    send(grad_in.at[across], grad_in.at[across], in_send, in_recv.at[across], batch=sibling)
    for k in others:
        f = turn(i, k)
        arrived(own_hidden.at[f], oh_recv.at[f])
    arrived(every_cot.at[sibling], cot_recv.at[sibling])
    arrived(every_cot.at[diagonal], cot_recv.at[diagonal])
    for f in range(4):
        hidden_t[:, f * 128 : (f + 1) * 128] = jnp.transpose(own_hidden[f])

    def outer(d):
        cots = jnp.concatenate([every_cot[f, d] for f in range(4)], axis=0)
        grad_out[pl.ds(d, 512, stride=8), :] = dot(hidden_t[...], cots)

    for d in range(4):
        outer(d)
    for k in others:
        f = turn(z, k)
        arrived(proj_z.at[f], gz_recv.at[f])
    proj_b[i] = four(proj_z)
    for k in others:
        send(proj_b.at[i], proj_b.at[i], gb_send, gb_recv.at[i], batch=turn(i, k))
    for d in range(4, 8):
        outer(d)
    for k in others:
        f = turn(i, k)
        arrived(bias_all.at[f], bias_recv.at[f])
    grad_bias[...] = four(bias_all)
    for k in others:
        f = turn(i, k)
        arrived(proj_b.at[f], gb_recv.at[f])
    grad_proj[...] = four(proj_b)
    arrived(grad_in.at[sibling], in_recv.at[sibling])
    arrived(grad_in.at[diagonal], in_recv.at[diagonal])
    arrived(emb.at[pl.ds(0, 63)], emb_send)
    arrived(every_cot.at[three], cot_send)
    arrived(part_y.at[three], py_send)
    arrived(part_z.at[three], pz_send)
    arrived(part_x.at[three], px_send)
    arrived(raw.at[pl.ds(0, 15), 0], near_send)
    arrived(raw.at[pl.ds(0, 12)], far_send)
    arrived(pre_x.at[three], pre_send)
    arrived(hidden_all.at[:, pl.ds(0, 15 * 128)], h_send)
    arrived(own_hidden.at[three], oh_send)
    arrived(d_act.at[:, :, pl.ds(0, 12)], dy_send)
    arrived(d_z.at[:, pl.ds(0, 15)], dz_send)
    arrived(acts.at[three], acts_send)
    arrived(d_all.at[three], all_send)
    arrived(grad_in.at[three], in_send)
    arrived(bias_all.at[three], bias_send)
    arrived(proj_x.at[pl.ds(0, 15)], gx_send)
    arrived(proj_z.at[three], gz_send)
    arrived(proj_b.at[three], gb_send)


def everything(emb, proj, w_in, bias, w_out, cot):
    out = jax.ShapeDtypeStruct
    pair = [DMA, DMA((4,))]
    far = pl.BlockSpec(memory_space=pltpu.HBM)
    near = pl.BlockSpec(memory_space=VMEM)
    return pl.pallas_call(
        kernel,
        out_shape=(
            out((128, 8, 128), bf16),
            out((4096, 128), f32),
            out((4, 8, 128, 128), bf16),
            out((8, 128), f32),
            out((32, 128), f32),
        ),
        in_specs=[far] * 6,
        out_specs=[near] * 5,
        scratch_shapes=[
            VMEM((32, 512), bf16),
            VMEM((32, 128, 128), bf16),
            VMEM((1, 128), f32),
            VMEM((2048, 8, 128), bf16),
            VMEM((128, 8, 128), bf16),
            VMEM((8, 2048, 128), bf16),
            VMEM((1024, 128), f32),
            VMEM((4, 8, 128, 128), bf16),
            VMEM((4, 2, 16, 8, 128), bf16),
            VMEM((512, 128), f32),
            VMEM((2, 128, 128), f32),
            VMEM((2, 8, 128), f32),
            VMEM((4, 4, 128, 128), bf16),
            VMEM((4, 4, 128, 128), bf16),
            VMEM((4, 128, 128), bf16),
            VMEM((4, 128, 128), bf16),
            VMEM((4, 128, 128), f32),
            VMEM((4, 2, 32, 128), bf16),
            VMEM((16, 4, 2, 32, 128), bf16),
            VMEM((32, 16, 8, 128), bf16),
            VMEM((4, 128, 128), f32),
            VMEM((128, 128), bf16),
            VMEM((128, 128), bf16),
            VMEM((2, 16, 16, 8, 128), bf16),
            VMEM((2, 4, 16, 4, 8, 128), bf16),
            VMEM((2, 16, 2, 16, 128), bf16),
            VMEM((2, 16, 2, 16, 128), bf16),
            VMEM((4, 8, 16, 8, 128), bf16),
            VMEM((4, 128, 128), bf16),
            VMEM((4, 8, 128), f32),
            VMEM((128, 2048), bf16),
            VMEM((4, 128, 512), bf16),
            VMEM((512, 512), bf16),
            VMEM((4, 32, 128), f32),
            VMEM((16, 32, 128), f32),
            VMEM((4, 32, 128), f32),
            VMEM((4, 32, 128), f32),
            DMA, DMA((4,)), DMA, DMA, DMA, DMA, DMA, *pair,
            *pair, *pair, *pair,
            DMA, DMA, DMA((16,)), *pair,
            DMA, DMA((16,)), *pair, DMA, DMA((2, 4)), DMA, DMA((2,)),
            *pair, *pair, *pair, *pair,
            DMA, DMA, *pair, *pair, DMA,
        ],
        compiler_params=pltpu.CompilerParams(
            collective_id=0, has_side_effects=True, vmem_limit_bytes=49 << 20
        ),
        name="block",
    )(*[pltpu.with_memory_space_constraint(a, pltpu.HBM) for a in (emb, proj, w_in, bias, w_out, cot)])


def local(embeddings, projection, w_in, bias, w_out, cotangent):
    mixed, grad_out, grad_in, grad_bias, grad_proj = everything(
        embeddings.reshape(64, 2, 8, 128), projection.T, w_in.reshape(32, 128, 128),
        bias.reshape(1, 128), w_out, cotangent,
    )
    return (
        mixed, grad_out.reshape(512, 8, 128), grad_in.astype(f32).reshape(4096, 128),
        grad_bias[0], grad_proj.T,
    )


def solution(mesh):
    placed = (
        P("batch", "col", "row"),
        P(),
        P("row", "col"),
        P("col"),
        P(None, "col", "row"),
        P("batch", "col", "row"),
    )
    return jax.shard_map(
        local,
        mesh=mesh,
        in_specs=placed,
        out_specs=(
            P("batch", "col", "row"),
            P("batch", "col", "row"),
            P("row", "col"),
            P("col"),
            P("row", None),
        ),
        check_vma=False,
    )
```

```python
import jax
import jax.numpy as jnp
from jax import lax
from jax.experimental import pallas as pl
from jax.experimental.pallas import tpu as pltpu
from jax.sharding import PartitionSpec as P

epsilon = 1e-06
bf16 = jnp.bfloat16
f32 = jnp.float32
MESH = pl.DeviceIdType.MESH
VMEM = pltpu.VMEM
DMA = pltpu.SemaphoreType.DMA
others = (1, 2, 3)
pieces = ((0, 16), (16, 16))


def contract_last(left, right):
    return lax.dot_general(left, right, (((1,), (1,)), ((), ())), preferred_element_type=f32)


def contract_first(left, right):
    return lax.dot_general(left, right, (((0,), (0,)), ((), ())), preferred_element_type=f32)


def dot(left, right):
    return jnp.dot(left, right, preferred_element_type=f32)


def send(src, dst, send_sem, recv_sem, **place):
    copy = pltpu.make_async_remote_copy(
        src_ref=src, dst_ref=dst, send_sem=send_sem, recv_sem=recv_sem,
        device_id=place, device_id_type=MESH,
    )
    copy.start()


def arrived(ref, sem):
    pltpu.make_async_copy(ref, ref, sem).wait()


def split(value):
    high = value.astype(bf16)
    return high, (value - high.astype(f32)).astype(bf16)


def four(parts):
    return (parts[0] + parts[1]) + (parts[2] + parts[3])


def turn(place, k):
    return lax.rem(place + k, 4)


def lanes_of(slot, size=128):
    return pl.ds(pl.multiple_of(slot * size, size), size)


def whole_sum(value):
    return jnp.sum(jnp.sum(value, axis=0, keepdims=True), axis=1, keepdims=True)


def ordering(size, high):
    at = lax.broadcasted_iota(jnp.int32, (size, size), 0)
    of = lax.broadcasted_iota(jnp.int32, (size, size), 1)
    source = lax.rem(at, 8) // 2 * (2 * high) + lax.rem(at, 2) * high + at // 8
    return (of == source).astype(f32).astype(bf16)


def kernel(
    emb, proj_far, w_in_far, bias_far, w_out_far, cot_far,
    mixed, grad_out, grad_in, grad_bias, grad_proj,
    proj, w_in, bias, w_out, cot, w_split, stage, every_cot, own_emb, folds, normed, inv,
    part_out, part_y, part_z_out, part_z, part_x,
    to_row, raw, gathered, pre_x, hidden, d_pre_b,
    d_act, d_y, z_out, z_in, acts, d_all, bias_all, hidden_all, own_hidden, hidden_t,
    proj_out, proj_x, proj_z, proj_b,
    load_in, load_out, load_cot, load_proj, load_bias, emb_send, emb_recv, cot_send, cot_recv,
    py_send, py_recv, pz_send, pz_recv, px_send, px_recv,
    near_send, far_send, raw_recv, pre_send, pre_recv,
    h_send, h_recv, oh_send, oh_recv, dy_send, dy_recv, dz_send, dz_recv,
    acts_send, acts_recv, all_send, all_recv, in_send, in_recv, bias_send, bias_recv,
    gx_send, gx_recv, gz_send, gz_recv, gb_send, gb_recv, own_sem,
):
    i = lax.axis_index("batch")
    r = lax.axis_index("row")
    c = lax.axis_index("col")
    y = c // 4
    z = c - y * 4
    sibling = i + 1 - 2 * lax.rem(i, 2)
    across = turn(i, 2)
    diagonal = turn(sibling, 2)
    me = c * 4 + r
    three = pl.ds(0, 3)
    barrier = pltpu.get_barrier_semaphore()

    def greet(k, _):
        peer = lax.rem(me + k, 64)
        pl.semaphore_signal(
            barrier, inc=1, device_id={"col": peer // 4, "row": lax.rem(peer, 4)},
            device_id_type=MESH,
        )
        return 0

    lax.fori_loop(1, 64, greet, 0)
    for k in others:
        pl.semaphore_signal(barrier, inc=1, device_id={"batch": turn(i, k)}, device_id_type=MESH)
    take_cot = pltpu.make_async_copy(cot_far, cot, load_cot)
    take_cot.start()
    take_out = []
    for k in (1, 2, 3, 0):
        at = lanes_of(turn(y, k), 512)
        take_out.append(pltpu.make_async_copy(w_out_far.at[at], w_out.at[at], load_out.at[k]))
        take_out[-1].start()
    take_proj = pltpu.make_async_copy(proj_far, proj, load_proj)
    take_proj.start()
    take_bias = pltpu.make_async_copy(bias_far, bias, load_bias)
    take_bias.start()
    take_in = pltpu.make_async_copy(w_in_far, w_in, load_in)
    take_in.start()
    take_cot.wait()
    stage[...] = cot[...].astype(f32).reshape(1024, 128)
    for d in range(8):
        every_cot[i, d] = stage[pl.ds(d, 128, stride=8), :].astype(bf16)

    def from_output(k):
        to = turn(y, k)

        def divide(n, _):
            at = pl.multiple_of(to * 512 + n * 128, 128)
            stage[...] = w_out[pl.ds(at, 128)].astype(f32).reshape(1024, 128)
            for d in range(8):
                w_split[d, pl.ds(at, 128), :] = stage[pl.ds(d, 128, stride=8), :].astype(bf16)
            return 0

        lax.fori_loop(0, 4, divide, 0)
        part = jnp.zeros((128, 512), f32)
        for d in range(8):
            part = part + contract_last(every_cot[i, d], w_split[d, lanes_of(to, 512), :])
        for q in range(4):
            part_out[to, q] = part[:, q * 128 : (q + 1) * 128].astype(bf16)

    def share_output(k):
        to = turn(y, k)
        send(part_out.at[to], part_y.at[y], py_send, py_recv.at[y], col=to * 4 + z)

    for n in (0, 1):
        take_out[n].wait()
        from_output(n + 1)
    pl.semaphore_wait(barrier, 66)

    keep = pltpu.make_async_copy(emb.at[me], own_emb.at[r, :, c], emb_recv)
    keep.start()

    def give(k, _):
        peer = lax.rem(me + k, 64)
        send(
            emb.at[peer], own_emb.at[r, :, c], emb_send, emb_recv,
            col=peer // 4, row=lax.rem(peer, 4),
        )
        return 0

    lax.fori_loop(1, 64, give, 0)
    share_output(1)
    share_output(2)
    take_out[2].wait()
    from_output(3)
    share_output(3)
    take_out[3].wait()
    from_output(0)
    part_y[y] = part_out[y]
    take_proj.wait()
    take_bias.wait()
    lanes = lax.broadcasted_iota(jnp.int32, (32, 128), 1)
    ranks = lax.broadcasted_iota(jnp.int32, (32, 128), 0)
    repeat = (lax.rem(lanes, 32) == ranks).astype(f32).astype(bf16)
    wide = contract_first(proj[...], repeat).astype(bf16)
    block = lax.broadcasted_iota(jnp.int32, (128, 128), 1) // 32
    order = ordering(256, 32)

    def sample(s):
        return jnp.concatenate([own_emb[q, s].reshape(128, 128) for q in range(4)], axis=1)

    arrived(own_emb, emb_recv)
    for s in range(2):
        own = sample(s)
        high, low = split(dot(own, wide))
        both = contract_first(own, jnp.concatenate([high, low], axis=1))
        folds[...] = both[:, :128] + both[:, 128:]
        inter = jnp.zeros((128, 128), f32)
        for j in range(4):
            inter = jnp.where(block == j, folds[pl.ds(j, 128, stride=4), :], inter)
        scale = lax.rsqrt(whole_sum(inter * inter) / (512 * 32) + epsilon)
        norm = inter * scale
        normed[s] = norm
        inv[s] = jnp.broadcast_to(scale, (8, 128))
        for q in range(4):
            to_row[q, s] = norm[q * 32 : (q + 1) * 32].astype(bf16)
    raw[c, r] = to_row[r]
    plane = z * 4 + r

    def scatter(k, _):
        peer = lax.rem(plane + k, 16)
        to_z = peer // 4
        to_r = lax.rem(peer, 4)
        send(to_row.at[to_r], raw.at[c, r], near_send, raw_recv.at[c], col=y * 4 + to_z, row=to_r)
        return 0

    lax.fori_loop(1, 16, scatter, 0)

    for k in others:
        f = turn(y, k)
        arrived(part_y.at[f], py_recv.at[f])
    for q in range(4):
        part_z_out[q] = four([part_y[f, q].astype(f32) for f in range(4)]).astype(bf16)
    part_z[z] = part_z_out[z]
    for k in others:
        to = turn(z, k)
        send(part_z_out.at[to], part_z.at[z], pz_send, pz_recv.at[z], col=y * 4 + to)

    arrived(raw.at[c, three], raw_recv.at[c])
    for k in others:
        send(raw.at[c], raw.at[c], far_send, raw_recv.at[c], col=turn(y, k) * 4 + z)
    for m in (1, 3, 2):
        slot = y * 4 + turn(z, m)
        arrived(raw.at[slot], raw_recv.at[slot])
        for k in others:
            send(raw.at[slot], raw.at[slot], far_send, raw_recv.at[slot], col=turn(y, k) * 4 + z)
    send(every_cot.at[i], every_cot.at[i], cot_send, cot_recv.at[i], batch=sibling)
    send(every_cot.at[i], every_cot.at[i], cot_send, cot_recv.at[i], batch=across)

    def lay(slot):
        rows = dot(order, raw[slot].reshape(256, 128))
        gathered[:, slot] = rows.reshape(32, 8, 128).astype(bf16)

    for q in range(4):
        lay(y * 4 + q)
    for k in others:
        f = turn(z, k)
        arrived(part_z.at[f], pz_recv.at[f])
    part_x[r] = four([part_z[f].astype(f32) for f in range(4)])
    for k in others:
        send(part_x.at[r], part_x.at[r], px_send, px_recv.at[r], row=turn(r, k))
    take_in.wait()
    for k in range(4):
        for m in others:
            slot = turn(y, m) * 4 + turn(z, k)
            arrived(raw.at[slot], raw_recv.at[slot])
            lay(slot)
    pre = jnp.zeros((128, 128), f32)
    for e in range(32):
        pre = pre + dot(gathered[e].reshape(128, 128), w_in[e])
    pre_x[r] = pre
    for k in others:
        send(pre_x.at[r], pre_x.at[r], pre_send, pre_recv.at[r], row=turn(r, k))
    for k in others:
        to = turn(i, k)
        send(gathered.at[pl.ds(8 * to, 8)], acts.at[i], acts_send, acts_recv.at[i], batch=to)
    mine = pltpu.make_async_copy(gathered.at[pl.ds(8 * i, 8)], acts.at[i], own_sem)
    mine.start()
    for k in others:
        f = turn(r, k)
        arrived(part_x.at[f], px_recv.at[f])
    d_hidden = four(part_x)
    for k in others:
        f = turn(r, k)
        arrived(pre_x.at[f], pre_recv.at[f])
    preact = four(pre_x) + bias[...]
    sig = 1.0 / (1.0 + jnp.exp(-preact))
    hidden[...] = (preact * sig).astype(bf16)
    d_value = d_hidden * sig * (1.0 + preact * (1.0 - sig))
    d_pre_b[...] = d_value.astype(bf16)
    bias_all[i] = jnp.broadcast_to(jnp.sum(d_value, axis=0, keepdims=True), (8, 128))

    for k in others:
        send(hidden, hidden_all.at[:, lanes_of(c)], h_send, h_recv.at[c], col=y * 4 + turn(z, k))
    for n, (first, size) in enumerate(pieces):
        for e in range(first, first + size):
            part = contract_last(d_pre_b[...], w_in[e])
            d_act[e] = part.reshape(16, 8, 128).astype(bf16)
        for k in others:
            to = turn(y, k)
            send(
                d_act.at[pl.ds(first, size), pl.ds(4 * to, 4)],
                d_y.at[y, pl.ds(first, size)],
                dy_send, dy_recv.at[n, y], col=to * 4 + z,
            )
    for k in others:
        send(hidden, hidden_all.at[:, lanes_of(c)], h_send, h_recv.at[c], col=turn(y, k) * 4 + z)
    hidden_all[:, lanes_of(c)] = hidden[...]
    d_all[i] = d_pre_b[...]
    for k in others:
        to = turn(i, k)
        send(d_pre_b, d_all.at[i], all_send, all_recv.at[i], batch=to)
        send(bias_all.at[i], bias_all.at[i], bias_send, bias_recv.at[i], batch=to)
    for m in others:
        slot = y * 4 + turn(z, m)
        place = hidden_all.at[:, lanes_of(slot)]
        arrived(place, h_recv.at[slot])
        for k in others:
            send(place, place, h_send, h_recv.at[slot], col=turn(y, k) * 4 + z)
    arrived(every_cot.at[across], cot_recv.at[across])
    send(every_cot.at[across], every_cot.at[across], cot_send, cot_recv.at[across], batch=sibling)
    for n, (first, size) in enumerate(pieces):
        d_z_out, d_z = z_out[n], z_in[n]
        undo = ordering(8 * size, size)
        span = pl.ds(first, size)
        d_y[y, span] = d_act[span, pl.ds(4 * y, 4)]
        for k in others:
            f = turn(y, k)
            arrived(d_y.at[f, span], dy_recv.at[n, f])
        for q in range(4):
            part = four([d_y[f, span, q].astype(f32) for f in range(4)])
            rows = contract_first(undo, part.reshape(8 * size, 128).astype(bf16))
            for g in range(4):
                d_z_out[q * 4 + g] = (
                    rows[g * 2 * size : (g + 1) * 2 * size].reshape(2, size, 128).astype(bf16)
                )
        d_z[plane] = d_z_out[plane]

        def hand(k, _):
            peer = lax.rem(plane + k, 16)
            send(
                d_z_out.at[peer], d_z.at[plane], dz_send.at[n], dz_recv.at[n],
                col=y * 4 + peer // 4, row=lax.rem(peer, 4),
            )
            return 0

        lax.fori_loop(1, 16, hand, 0)
    for m in others:
        for k in range(4):
            slot = turn(y, m) * 4 + k
            arrived(hidden_all.at[:, lanes_of(slot)], h_recv.at[slot])
    for k in others:
        to = turn(i, k)
        send(
            hidden_all.at[:, lanes_of(to, 512)], own_hidden.at[i], oh_send, oh_recv.at[i],
            batch=to,
        )
    own_hidden[i] = hidden_all[:, lanes_of(i, 512)]
    mine.wait()
    for k in others:
        f = turn(i, k)
        arrived(d_all.at[f], all_recv.at[f])
        arrived(acts.at[f], acts_recv.at[f])
    for e in range(8):
        part = four([contract_first(acts[f, e].reshape(128, 128), d_all[f]) for f in range(4)])
        grad_in[i, e] = part.astype(bf16)
    send(grad_in.at[i], grad_in.at[i], in_send, in_recv.at[i], batch=sibling)
    send(grad_in.at[i], grad_in.at[i], in_send, in_recv.at[i], batch=across)
    for n in range(len(pieces)):
        arrived(z_in[n].at[pl.ds(0, 15)], dz_recv.at[n])
    for s in range(2):
        grad = jnp.concatenate(
            [
                four([d_z[q * 4 + g, s].astype(f32) for q in range(4)])
                for g in range(4)
                for d_z in z_in
            ],
            axis=0,
        )
        norm = normed[s]
        inner = whole_sum(grad * norm) / (512 * 32)
        d_inter = (inv[s, 0:1, :] * (grad - norm * inner)).astype(bf16).astype(f32)
        for j in range(4):
            folds[pl.ds(j, 128, stride=4), :] = jnp.where(block == j, d_inter, 0.0)
        own = sample(s)
        fold = dot(own, folds[...].astype(bf16))
        fold = fold + pltpu.roll(fold, 32, 1)
        fold = fold + pltpu.roll(fold, 64, 1)
        high, low = split(jnp.transpose(fold)[:32])
        both = dot(jnp.concatenate([high, low], axis=0), own)
        for q in range(4):
            part = both[:32, q * 128 : (q + 1) * 128] + both[32:, q * 128 : (q + 1) * 128]
            if s == 0:
                proj_out[q] = part
            else:
                proj_out[q] += part
    flat = y * 4 + r
    proj_x[flat] = proj_out[r]

    def hand_on(k, _):
        peer = lax.rem(flat + k, 16)
        to_r = lax.rem(peer, 4)
        send(
            proj_out.at[to_r], proj_x.at[flat], gx_send, gx_recv,
            col=peer // 4 * 4 + z, row=to_r,
        )
        return 0

    lax.fori_loop(1, 16, hand_on, 0)
    for d in range(8):
        stage[pl.ds(d, 128, stride=8), :] = dot(hidden_all[...], w_split[d])
    mixed[...] = stage[...].reshape(128, 8, 128).astype(bf16)
    arrived(proj_x.at[pl.ds(0, 15)], gx_recv)
    proj_z[z] = four([four([proj_x[q * 4 + g] for g in range(4)]) for q in range(4)])
    for k in others:
        send(proj_z.at[z], proj_z.at[z], gz_send, gz_recv.at[z], col=y * 4 + turn(z, k))
    arrived(grad_in.at[across], in_recv.at[across])
    send(grad_in.at[across], grad_in.at[across], in_send, in_recv.at[across], batch=sibling)
    for k in others:
        f = turn(i, k)
        arrived(own_hidden.at[f], oh_recv.at[f])
    arrived(every_cot.at[sibling], cot_recv.at[sibling])
    arrived(every_cot.at[diagonal], cot_recv.at[diagonal])
    for f in range(4):
        hidden_t[:, f * 128 : (f + 1) * 128] = jnp.transpose(own_hidden[f])

    def outer(d):
        cots = jnp.concatenate([every_cot[f, d] for f in range(4)], axis=0)
        grad_out[pl.ds(d, 512, stride=8), :] = dot(hidden_t[...], cots)

    for d in range(4):
        outer(d)
    for k in others:
        f = turn(z, k)
        arrived(proj_z.at[f], gz_recv.at[f])
    proj_b[i] = four(proj_z)
    for k in others:
        send(proj_b.at[i], proj_b.at[i], gb_send, gb_recv.at[i], batch=turn(i, k))
    for d in range(4, 8):
        outer(d)
    for k in others:
        f = turn(i, k)
        arrived(bias_all.at[f], bias_recv.at[f])
    grad_bias[...] = four(bias_all)
    for k in others:
        f = turn(i, k)
        arrived(proj_b.at[f], gb_recv.at[f])
    grad_proj[...] = four(proj_b)
    arrived(grad_in.at[sibling], in_recv.at[sibling])
    arrived(grad_in.at[diagonal], in_recv.at[diagonal])
    arrived(emb.at[pl.ds(0, 63)], emb_send)
    arrived(every_cot.at[three], cot_send)
    arrived(part_y.at[three], py_send)
    arrived(part_z.at[three], pz_send)
    arrived(part_x.at[three], px_send)
    arrived(raw.at[pl.ds(0, 15), 0], near_send)
    arrived(raw.at[pl.ds(0, 12)], far_send)
    arrived(pre_x.at[three], pre_send)
    arrived(hidden_all.at[:, pl.ds(0, 15 * 128)], h_send)
    arrived(own_hidden.at[three], oh_send)
    arrived(d_act.at[:, pl.ds(0, 12)], dy_send)
    for n in range(len(pieces)):
        arrived(z_out[n].at[pl.ds(0, 15)], dz_send.at[n])
    arrived(acts.at[three], acts_send)
    arrived(d_all.at[three], all_send)
    arrived(grad_in.at[three], in_send)
    arrived(bias_all.at[three], bias_send)
    arrived(proj_x.at[pl.ds(0, 15)], gx_send)
    arrived(proj_z.at[three], gz_send)
    arrived(proj_b.at[three], gb_send)


def everything(emb, proj, w_in, bias, w_out, cot):
    out = jax.ShapeDtypeStruct
    pair = [DMA, DMA((4,))]
    count = len(pieces)
    far = pl.BlockSpec(memory_space=pltpu.HBM)
    near = pl.BlockSpec(memory_space=VMEM)
    return pl.pallas_call(
        kernel,
        out_shape=(
            out((128, 8, 128), bf16),
            out((4096, 128), f32),
            out((4, 8, 128, 128), bf16),
            out((8, 128), f32),
            out((32, 128), f32),
        ),
        in_specs=[far] * 6,
        out_specs=[near] * 5,
        scratch_shapes=[
            VMEM((32, 512), bf16),
            VMEM((32, 128, 128), bf16),
            VMEM((1, 128), f32),
            VMEM((2048, 8, 128), bf16),
            VMEM((128, 8, 128), bf16),
            VMEM((8, 2048, 128), bf16),
            VMEM((1024, 128), f32),
            VMEM((4, 8, 128, 128), bf16),
            VMEM((4, 2, 16, 8, 128), bf16),
            VMEM((512, 128), f32),
            VMEM((2, 128, 128), f32),
            VMEM((2, 8, 128), f32),
            VMEM((4, 4, 128, 128), bf16),
            VMEM((4, 4, 128, 128), bf16),
            VMEM((4, 128, 128), bf16),
            VMEM((4, 128, 128), bf16),
            VMEM((4, 128, 128), f32),
            VMEM((4, 2, 32, 128), bf16),
            VMEM((16, 4, 2, 32, 128), bf16),
            VMEM((32, 16, 8, 128), bf16),
            VMEM((4, 128, 128), f32),
            VMEM((128, 128), bf16),
            VMEM((128, 128), bf16),
            VMEM((32, 16, 8, 128), bf16),
            VMEM((4, 32, 4, 8, 128), bf16),
            tuple(VMEM((16, 2, size, 128), bf16) for _, size in pieces),
            tuple(VMEM((16, 2, size, 128), bf16) for _, size in pieces),
            VMEM((4, 8, 16, 8, 128), bf16),
            VMEM((4, 128, 128), bf16),
            VMEM((4, 8, 128), f32),
            VMEM((128, 2048), bf16),
            VMEM((4, 128, 512), bf16),
            VMEM((512, 512), bf16),
            VMEM((4, 32, 128), f32),
            VMEM((16, 32, 128), f32),
            VMEM((4, 32, 128), f32),
            VMEM((4, 32, 128), f32),
            DMA, DMA((4,)), DMA, DMA, DMA, DMA, DMA, *pair,
            *pair, *pair, *pair,
            DMA, DMA, DMA((16,)), *pair,
            DMA, DMA((16,)), *pair, DMA, DMA((count, 4)), DMA((count,)), DMA((count,)),
            *pair, *pair, *pair, *pair,
            DMA, DMA, *pair, *pair, DMA,
        ],
        compiler_params=pltpu.CompilerParams(
            collective_id=0, has_side_effects=True, vmem_limit_bytes=49 << 20
        ),
        name="block",
    )(*[pltpu.with_memory_space_constraint(a, pltpu.HBM) for a in (emb, proj, w_in, bias, w_out, cot)])


def finish_kernel(
    mixed, grad_out, grad_in, grad_bias, grad_proj,
    mixed_far, grad_out_far, grad_in_far, grad_bias_far, grad_proj_far,
    wide, sems,
):
    copies = [
        pltpu.make_async_copy(grad_out, grad_out_far, sems.at[0]),
        pltpu.make_async_copy(mixed, mixed_far, sems.at[1]),
        pltpu.make_async_copy(grad_bias.at[pl.ds(0, 1)], grad_bias_far, sems.at[2]),
        pltpu.make_async_copy(grad_proj, grad_proj_far, sems.at[3]),
    ]
    for copy in copies:
        copy.start()
    for f in range(4):
        wide[f] = grad_in[f].astype(f32)
        copies.append(pltpu.make_async_copy(wide.at[f], grad_in_far.at[f], sems.at[4 + f]))
        copies[-1].start()
    for copy in copies:
        copy.wait()


def finish(mixed, grad_out, grad_in, grad_bias, grad_proj):
    near = pl.BlockSpec(memory_space=VMEM)
    far = pl.BlockSpec(memory_space=pltpu.HBM)
    return pl.pallas_call(
        finish_kernel,
        out_shape=(
            pltpu.HBM((128, 8, 128), bf16),
            pltpu.HBM((4096, 128), f32),
            pltpu.HBM((4, 8, 128, 128), f32),
            pltpu.HBM((1, 128), f32),
            pltpu.HBM((32, 128), f32),
        ),
        in_specs=[near] * 5,
        out_specs=[far] * 5,
        scratch_shapes=[VMEM((4, 8, 128, 128), f32), DMA((8,))],
        compiler_params=pltpu.CompilerParams(vmem_limit_bytes=16 << 20),
        name="finish",
    )(mixed, grad_out, grad_in, grad_bias, grad_proj)


def local(embeddings, projection, w_in, bias, w_out, cotangent):
    results = everything(
        embeddings.reshape(64, 2, 8, 128), projection.T, w_in.reshape(32, 128, 128),
        bias.reshape(1, 128), w_out, cotangent,
    )
    mixed, grad_out, grad_in, grad_bias, grad_proj = finish(*results)
    return (
        mixed, grad_out.reshape(512, 8, 128), grad_in.reshape(4096, 128),
        grad_bias.reshape(128), grad_proj.T,
    )


def solution(mesh):
    placed = (
        P("batch", "col", "row"),
        P(),
        P("row", "col"),
        P("col"),
        P(None, "col", "row"),
        P("batch", "col", "row"),
    )
    return jax.shard_map(
        local,
        mesh=mesh,
        in_specs=placed,
        out_specs=(
            P("batch", "col", "row"),
            P("batch", "col", "row"),
            P("row", "col"),
            P("col"),
            P("row", None),
        ),
        check_vma=False,
    )
```

```python
import jax
import jax.numpy as jnp
from jax import lax
from jax.experimental import pallas as pl
from jax.experimental.pallas import tpu as pltpu
from jax.sharding import PartitionSpec as P

epsilon = 1e-06
bf16 = jnp.bfloat16
f32 = jnp.float32
MESH = pl.DeviceIdType.MESH
VMEM = pltpu.VMEM
DMA = pltpu.SemaphoreType.DMA
others = (2, 1, 3)
pieces = ((0, 16), (16, 16))


def contract_last(left, right):
    return lax.dot_general(left, right, (((1,), (1,)), ((), ())), preferred_element_type=f32)


def contract_first(left, right):
    return lax.dot_general(left, right, (((0,), (0,)), ((), ())), preferred_element_type=f32)


def dot(left, right):
    return jnp.dot(left, right, preferred_element_type=f32)


def send(src, dst, send_sem, recv_sem, **place):
    copy = pltpu.make_async_remote_copy(
        src_ref=src, dst_ref=dst, send_sem=send_sem, recv_sem=recv_sem,
        device_id=place, device_id_type=MESH,
    )
    copy.start()


def arrived(ref, sem):
    pltpu.make_async_copy(ref, ref, sem).wait()


def split(value):
    high = value.astype(bf16)
    return high, (value - high.astype(f32)).astype(bf16)


def four(parts):
    return (parts[0] + parts[1]) + (parts[2] + parts[3])


def turn(place, k):
    return lax.rem(place + k, 4)


def lanes_of(slot, size=128):
    return pl.ds(pl.multiple_of(slot * size, size), size)


def whole_sum(value):
    return jnp.sum(jnp.sum(value, axis=0, keepdims=True), axis=1, keepdims=True)


def ordering(size, high):
    at = lax.broadcasted_iota(jnp.int32, (size, size), 0)
    of = lax.broadcasted_iota(jnp.int32, (size, size), 1)
    source = lax.rem(at, 8) // 2 * (2 * high) + lax.rem(at, 2) * high + at // 8
    return (of == source).astype(f32).astype(bf16)


def kernel(
    emb, proj_far, w_in_far, bias_far, w_out_far, cot_far,
    mixed, grad_out, grad_in, grad_bias, grad_proj,
    proj, w_in, w_turned, bias, w_out, cot, w_split, stage, every_cot, own_emb, folds, normed, inv,
    part_out, part_y, part_z_out, part_z, part_x,
    to_row, raw, gathered, pre_x, hidden, d_pre_b,
    d_act, d_y, z_out, z_in, acts, d_all, bias_all, hidden_all, own_hidden, hidden_t,
    proj_out, proj_x, proj_z, proj_b,
    load_in, load_out, load_cot, load_proj, load_bias, emb_send, emb_recv, cot_send, cot_recv,
    py_send, py_recv, pz_send, pz_recv, px_send, px_recv,
    near_send, far_send, raw_recv, pre_send, pre_recv,
    h_send, h_recv, oh_send, oh_recv, dy_send, dy_recv, dz_send, dz_recv,
    acts_send, acts_recv, all_send, all_recv, in_send, in_recv, bias_send, bias_recv,
    gx_send, gx_recv, gz_send, gz_recv, gb_send, gb_recv, own_sem,
):
    i = lax.axis_index("batch")
    r = lax.axis_index("row")
    c = lax.axis_index("col")
    y = c // 4
    z = c - y * 4
    sibling = i + 1 - 2 * lax.rem(i, 2)
    across = turn(i, 2)
    diagonal = turn(sibling, 2)
    me = c * 4 + r
    three = pl.ds(0, 3)
    barrier = pltpu.get_barrier_semaphore()

    def greet(k, _):
        peer = lax.rem(me + 1 + lax.rem(k + 40, 63), 64)
        pl.semaphore_signal(
            barrier, inc=1, device_id={"col": peer // 4, "row": lax.rem(peer, 4)},
            device_id_type=MESH,
        )
        return 0

    lax.fori_loop(1, 64, greet, 0)
    for k in others:
        pl.semaphore_signal(barrier, inc=1, device_id={"batch": turn(i, k)}, device_id_type=MESH)
    take_cot = pltpu.make_async_copy(cot_far, cot, load_cot)
    take_cot.start()
    take_out = []
    for k in (1, 2, 3, 0):
        at = lanes_of(turn(y, k), 512)
        take_out.append(pltpu.make_async_copy(w_out_far.at[at], w_out.at[at], load_out.at[k]))
        take_out[-1].start()
    take_proj = pltpu.make_async_copy(proj_far, proj, load_proj)
    take_proj.start()
    take_bias = pltpu.make_async_copy(bias_far, bias, load_bias)
    take_bias.start()
    take_in = pltpu.make_async_copy(w_in_far, w_in, load_in)
    take_in.start()
    take_cot.wait()
    stage[...] = cot[...].astype(f32).reshape(1024, 128)
    for d in range(8):
        every_cot[i, d] = stage[pl.ds(d, 128, stride=8), :].astype(bf16)

    def from_output(k):
        to = turn(y, k)

        def divide(n, _):
            at = pl.multiple_of(to * 512 + n * 128, 128)
            stage[...] = w_out[pl.ds(at, 128)].astype(f32).reshape(1024, 128)
            for d in range(8):
                w_split[d, pl.ds(at, 128), :] = stage[pl.ds(d, 128, stride=8), :].astype(bf16)
            return 0

        lax.fori_loop(0, 4, divide, 0)
        part = jnp.zeros((128, 512), f32)
        for d in range(8):
            part = part + contract_last(every_cot[i, d], w_split[d, lanes_of(to, 512), :])
        for q in range(4):
            part_out[to, q] = part[:, q * 128 : (q + 1) * 128].astype(bf16)

    def share_output(k):
        to = turn(y, k)
        send(part_out.at[to], part_y.at[y], py_send, py_recv.at[y], col=to * 4 + z)

    for n in (0, 1):
        take_out[n].wait()
        from_output(n + 1)
    pl.semaphore_wait(barrier, 66)

    keep = pltpu.make_async_copy(emb.at[me], own_emb.at[r, :, c], emb_recv)
    keep.start()

    def give(k, _):
        peer = lax.rem(me + 1 + lax.rem(k + 40, 63), 64)
        send(
            emb.at[peer], own_emb.at[r, :, c], emb_send, emb_recv,
            col=peer // 4, row=lax.rem(peer, 4),
        )
        return 0

    lax.fori_loop(1, 64, give, 0)
    share_output(1)
    share_output(2)
    take_out[2].wait()
    from_output(3)
    share_output(3)
    take_out[3].wait()
    from_output(0)
    part_y[y] = part_out[y]
    take_proj.wait()
    take_bias.wait()
    lanes = lax.broadcasted_iota(jnp.int32, (32, 128), 1)
    ranks = lax.broadcasted_iota(jnp.int32, (32, 128), 0)
    repeat = (lax.rem(lanes, 32) == ranks).astype(f32).astype(bf16)
    wide = contract_first(proj[...], repeat).astype(bf16)
    block = lax.broadcasted_iota(jnp.int32, (128, 128), 1) // 32
    order = ordering(256, 32)

    def sample(s):
        return jnp.concatenate([own_emb[q, s].reshape(128, 128) for q in range(4)], axis=1)

    arrived(own_emb, emb_recv)
    for s in range(2):
        own = sample(s)
        high, low = split(dot(own, wide))
        both = contract_first(own, jnp.concatenate([high, low], axis=1))
        folds[...] = both[:, :128] + both[:, 128:]
        inter = jnp.zeros((128, 128), f32)
        for j in range(4):
            inter = jnp.where(block == j, folds[pl.ds(j, 128, stride=4), :], inter)
        scale = lax.rsqrt(whole_sum(inter * inter) / (512 * 32) + epsilon)
        norm = inter * scale
        normed[s] = norm
        inv[s] = jnp.broadcast_to(scale, (8, 128))
        for q in range(4):
            to_row[q, s] = norm[q * 32 : (q + 1) * 32].astype(bf16)
    raw[c, r] = to_row[r]
    plane = z * 4 + r

    def scatter(k, _):
        peer = lax.rem(plane + 1 + lax.rem(k + 8, 15), 16)
        to_z = peer // 4
        to_r = lax.rem(peer, 4)
        send(to_row.at[to_r], raw.at[c, r], near_send, raw_recv.at[c], col=y * 4 + to_z, row=to_r)
        return 0

    lax.fori_loop(1, 16, scatter, 0)

    for k in others:
        f = turn(y, k)
        arrived(part_y.at[f], py_recv.at[f])
    for q in range(4):
        part_z_out[q] = four([part_y[f, q].astype(f32) for f in range(4)]).astype(bf16)
    part_z[z] = part_z_out[z]
    for k in others:
        to = turn(z, k)
        send(part_z_out.at[to], part_z.at[z], pz_send, pz_recv.at[z], col=y * 4 + to)

    arrived(raw.at[c, three], raw_recv.at[c])
    for k in others:
        send(raw.at[c], raw.at[c], far_send, raw_recv.at[c], col=turn(y, k) * 4 + z)
    for m in (1, 3, 2):
        slot = y * 4 + turn(z, m)
        arrived(raw.at[slot], raw_recv.at[slot])
        for k in others:
            send(raw.at[slot], raw.at[slot], far_send, raw_recv.at[slot], col=turn(y, k) * 4 + z)
    send(every_cot.at[i], every_cot.at[i], cot_send, cot_recv.at[i], batch=sibling)
    send(every_cot.at[i], every_cot.at[i], cot_send, cot_recv.at[i], batch=across)

    def lay(slot):
        rows = dot(order, raw[slot].reshape(256, 128))
        gathered[:, slot] = rows.reshape(32, 8, 128).astype(bf16)

    for q in range(4):
        lay(y * 4 + q)
    for k in others:
        f = turn(z, k)
        arrived(part_z.at[f], pz_recv.at[f])
    part_x[r] = four([part_z[f].astype(f32) for f in range(4)])
    for k in others:
        send(part_x.at[r], part_x.at[r], px_send, px_recv.at[r], row=turn(r, k))
    take_in.wait()
    for e in range(32):
        w_turned[e] = jnp.transpose(w_in[e])
    for k in range(4):
        for m in others:
            slot = turn(y, m) * 4 + turn(z, k)
            arrived(raw.at[slot], raw_recv.at[slot])
            lay(slot)
    pre = jnp.zeros((128, 128), f32)
    for e in range(32):
        pre = pre + dot(gathered[e].reshape(128, 128), w_in[e])
    pre_x[r] = pre
    for k in others:
        send(pre_x.at[r], pre_x.at[r], pre_send, pre_recv.at[r], row=turn(r, k))
    for k in others:
        to = turn(i, k)
        send(gathered.at[pl.ds(8 * to, 8)], acts.at[i], acts_send, acts_recv.at[i], batch=to)
    mine = pltpu.make_async_copy(gathered.at[pl.ds(8 * i, 8)], acts.at[i], own_sem)
    mine.start()
    for k in others:
        f = turn(r, k)
        arrived(part_x.at[f], px_recv.at[f])
    d_hidden = four(part_x)
    for k in others:
        f = turn(r, k)
        arrived(pre_x.at[f], pre_recv.at[f])
    preact = four(pre_x) + bias[...]
    sig = 1.0 / (1.0 + jnp.exp(-preact))
    hidden[...] = (preact * sig).astype(bf16)
    d_value = d_hidden * sig * (1.0 + preact * (1.0 - sig))
    d_pre_b[...] = d_value.astype(bf16)
    bias_all[i] = jnp.broadcast_to(jnp.sum(d_value, axis=0, keepdims=True), (8, 128))

    for k in others:
        send(hidden, hidden_all.at[:, lanes_of(c)], h_send, h_recv.at[c], col=y * 4 + turn(z, k))
    for n, (first, size) in enumerate(pieces):
        for e in range(first, first + size):
            part = dot(d_pre_b[...], w_turned[e])
            d_act[e] = part.reshape(16, 8, 128).astype(bf16)
        for k in others:
            to = turn(y, k)
            send(
                d_act.at[pl.ds(first, size), pl.ds(4 * to, 4)],
                d_y.at[y, pl.ds(first, size)],
                dy_send, dy_recv.at[n, y], col=to * 4 + z,
            )
    for k in others:
        send(hidden, hidden_all.at[:, lanes_of(c)], h_send, h_recv.at[c], col=turn(y, k) * 4 + z)
    hidden_all[:, lanes_of(c)] = hidden[...]
    d_all[i] = d_pre_b[...]
    for k in others:
        to = turn(i, k)
        send(d_pre_b, d_all.at[i], all_send, all_recv.at[i], batch=to)
        send(bias_all.at[i], bias_all.at[i], bias_send, bias_recv.at[i], batch=to)
    for m in others:
        slot = y * 4 + turn(z, m)
        place = hidden_all.at[:, lanes_of(slot)]
        arrived(place, h_recv.at[slot])
        for k in others:
            send(place, place, h_send, h_recv.at[slot], col=turn(y, k) * 4 + z)
    arrived(every_cot.at[across], cot_recv.at[across])
    send(every_cot.at[across], every_cot.at[across], cot_send, cot_recv.at[across], batch=sibling)
    for n, (first, size) in enumerate(pieces):
        d_z_out, d_z = z_out[n], z_in[n]
        undo = ordering(8 * size, size)
        span = pl.ds(first, size)
        d_y[y, span] = d_act[span, pl.ds(4 * y, 4)]
        for k in others:
            f = turn(y, k)
            arrived(d_y.at[f, span], dy_recv.at[n, f])
        for q in range(4):
            part = four([d_y[f, span, q].astype(f32) for f in range(4)])
            rows = contract_first(undo, part.reshape(8 * size, 128).astype(bf16))
            for g in range(4):
                d_z_out[q * 4 + g] = (
                    rows[g * 2 * size : (g + 1) * 2 * size].reshape(2, size, 128).astype(bf16)
                )
        d_z[plane] = d_z_out[plane]

        def hand(k, _):
            peer = lax.rem(plane + 1 + lax.rem(k + 8, 15), 16)
            send(
                d_z_out.at[peer], d_z.at[plane], dz_send.at[n], dz_recv.at[n],
                col=y * 4 + peer // 4, row=lax.rem(peer, 4),
            )
            return 0

        lax.fori_loop(1, 16, hand, 0)
    for m in others:
        for k in range(4):
            slot = turn(y, m) * 4 + k
            arrived(hidden_all.at[:, lanes_of(slot)], h_recv.at[slot])
    own_hidden[i] = hidden_all[:, lanes_of(i, 512)]
    mine.wait()
    for k in others:
        f = turn(i, k)
        arrived(d_all.at[f], all_recv.at[f])
        arrived(acts.at[f], acts_recv.at[f])
    for e in range(8):
        part = four([contract_first(acts[f, e].reshape(128, 128), d_all[f]) for f in range(4)])
        grad_in[i, e] = part.astype(bf16)
    send(grad_in.at[i], grad_in.at[i], in_send, in_recv.at[i], batch=sibling)
    send(grad_in.at[i], grad_in.at[i], in_send, in_recv.at[i], batch=across)
    for n in range(len(pieces)):
        arrived(z_in[n].at[pl.ds(0, 15)], dz_recv.at[n])
    for k in others:
        to = turn(i, k)
        send(
            hidden_all.at[:, lanes_of(to, 512)], own_hidden.at[i], oh_send, oh_recv.at[i],
            batch=to,
        )
    for s in range(2):
        grad = jnp.concatenate(
            [
                four([d_z[q * 4 + g, s].astype(f32) for q in range(4)])
                for g in range(4)
                for d_z in z_in
            ],
            axis=0,
        )
        norm = normed[s]
        inner = whole_sum(grad * norm) / (512 * 32)
        d_inter = (inv[s, 0:1, :] * (grad - norm * inner)).astype(bf16).astype(f32)
        for j in range(4):
            folds[pl.ds(j, 128, stride=4), :] = jnp.where(block == j, d_inter, 0.0)
        own = sample(s)
        fold = dot(own, folds[...].astype(bf16))
        fold = fold + pltpu.roll(fold, 32, 1)
        fold = fold + pltpu.roll(fold, 64, 1)
        high, low = split(jnp.transpose(fold)[:32])
        both = dot(jnp.concatenate([high, low], axis=0), own)
        for q in range(4):
            part = both[:32, q * 128 : (q + 1) * 128] + both[32:, q * 128 : (q + 1) * 128]
            if s == 0:
                proj_out[q] = part
            else:
                proj_out[q] += part
    flat = y * 4 + r
    proj_x[flat] = proj_out[r]

    def hand_on(k, _):
        peer = lax.rem(flat + 1 + lax.rem(k + 8, 15), 16)
        to_r = lax.rem(peer, 4)
        send(
            proj_out.at[to_r], proj_x.at[flat], gx_send, gx_recv,
            col=peer // 4 * 4 + z, row=to_r,
        )
        return 0

    lax.fori_loop(1, 16, hand_on, 0)
    for d in range(8):
        stage[pl.ds(d, 128, stride=8), :] = dot(hidden_all[...], w_split[d])
    mixed[...] = stage[...].reshape(128, 8, 128).astype(bf16)
    arrived(proj_x.at[pl.ds(0, 15)], gx_recv)
    proj_z[z] = four([four([proj_x[q * 4 + g] for g in range(4)]) for q in range(4)])
    for k in others:
        send(proj_z.at[z], proj_z.at[z], gz_send, gz_recv.at[z], col=y * 4 + turn(z, k))
    for k in others:
        f = turn(z, k)
        arrived(proj_z.at[f], gz_recv.at[f])
    proj_b[i] = four(proj_z)
    for k in others:
        send(proj_b.at[i], proj_b.at[i], gb_send, gb_recv.at[i], batch=turn(i, k))
    arrived(grad_in.at[across], in_recv.at[across])
    send(grad_in.at[across], grad_in.at[across], in_send, in_recv.at[across], batch=sibling)
    for k in others:
        f = turn(i, k)
        arrived(own_hidden.at[f], oh_recv.at[f])
    arrived(every_cot.at[sibling], cot_recv.at[sibling])
    arrived(every_cot.at[diagonal], cot_recv.at[diagonal])
    for f in range(4):
        hidden_t[:, f * 128 : (f + 1) * 128] = jnp.transpose(own_hidden[f])

    def outer(d):
        cots = jnp.concatenate([every_cot[f, d] for f in range(4)], axis=0)
        grad_out[pl.ds(d, 512, stride=8), :] = dot(hidden_t[...], cots)

    for d in range(4):
        outer(d)
    for d in range(4, 8):
        outer(d)
    for k in others:
        f = turn(i, k)
        arrived(bias_all.at[f], bias_recv.at[f])
    grad_bias[...] = four(bias_all)
    for k in others:
        f = turn(i, k)
        arrived(proj_b.at[f], gb_recv.at[f])
    grad_proj[...] = four(proj_b)
    arrived(grad_in.at[sibling], in_recv.at[sibling])
    arrived(grad_in.at[diagonal], in_recv.at[diagonal])
    arrived(emb.at[pl.ds(0, 63)], emb_send)
    arrived(every_cot.at[three], cot_send)
    arrived(part_y.at[three], py_send)
    arrived(part_z.at[three], pz_send)
    arrived(part_x.at[three], px_send)
    arrived(raw.at[pl.ds(0, 15), 0], near_send)
    arrived(raw.at[pl.ds(0, 12)], far_send)
    arrived(pre_x.at[three], pre_send)
    arrived(hidden_all.at[:, pl.ds(0, 15 * 128)], h_send)
    arrived(own_hidden.at[three], oh_send)
    arrived(d_act.at[:, pl.ds(0, 12)], dy_send)
    for n in range(len(pieces)):
        arrived(z_out[n].at[pl.ds(0, 15)], dz_send.at[n])
    arrived(acts.at[three], acts_send)
    arrived(d_all.at[three], all_send)
    arrived(grad_in.at[three], in_send)
    arrived(bias_all.at[three], bias_send)
    arrived(proj_x.at[pl.ds(0, 15)], gx_send)
    arrived(proj_z.at[three], gz_send)
    arrived(proj_b.at[three], gb_send)


def everything(emb, proj, w_in, bias, w_out, cot):
    out = jax.ShapeDtypeStruct
    pair = [DMA, DMA((4,))]
    count = len(pieces)
    far = pl.BlockSpec(memory_space=pltpu.HBM)
    near = pl.BlockSpec(memory_space=VMEM)
    return pl.pallas_call(
        kernel,
        out_shape=(
            out((128, 8, 128), bf16),
            out((4096, 128), f32),
            out((4, 8, 128, 128), bf16),
            out((8, 128), f32),
            out((32, 128), f32),
        ),
        in_specs=[far] * 6,
        out_specs=[near] * 5,
        scratch_shapes=[
            VMEM((32, 512), bf16),
            VMEM((32, 128, 128), bf16),
            VMEM((32, 128, 128), bf16),
            VMEM((1, 128), f32),
            VMEM((2048, 8, 128), bf16),
            VMEM((128, 8, 128), bf16),
            VMEM((8, 2048, 128), bf16),
            VMEM((1024, 128), f32),
            VMEM((4, 8, 128, 128), bf16),
            VMEM((4, 2, 16, 8, 128), bf16),
            VMEM((512, 128), f32),
            VMEM((2, 128, 128), f32),
            VMEM((2, 8, 128), f32),
            VMEM((4, 4, 128, 128), bf16),
            VMEM((4, 4, 128, 128), bf16),
            VMEM((4, 128, 128), bf16),
            VMEM((4, 128, 128), bf16),
            VMEM((4, 128, 128), f32),
            VMEM((4, 2, 32, 128), bf16),
            VMEM((16, 4, 2, 32, 128), bf16),
            VMEM((32, 16, 8, 128), bf16),
            VMEM((4, 128, 128), f32),
            VMEM((128, 128), bf16),
            VMEM((128, 128), bf16),
            VMEM((32, 16, 8, 128), bf16),
            VMEM((4, 32, 4, 8, 128), bf16),
            tuple(VMEM((16, 2, size, 128), bf16) for _, size in pieces),
            tuple(VMEM((16, 2, size, 128), bf16) for _, size in pieces),
            VMEM((4, 8, 16, 8, 128), bf16),
            VMEM((4, 128, 128), bf16),
            VMEM((4, 8, 128), f32),
            VMEM((128, 2048), bf16),
            VMEM((4, 128, 512), bf16),
            VMEM((512, 512), bf16),
            VMEM((4, 32, 128), f32),
            VMEM((16, 32, 128), f32),
            VMEM((4, 32, 128), f32),
            VMEM((4, 32, 128), f32),
            DMA, DMA((4,)), DMA, DMA, DMA, DMA, DMA, *pair,
            *pair, *pair, *pair,
            DMA, DMA, DMA((16,)), *pair,
            DMA, DMA((16,)), *pair, DMA, DMA((count, 4)), DMA((count,)), DMA((count,)),
            *pair, *pair, *pair, *pair,
            DMA, DMA, *pair, *pair, DMA,
        ],
        compiler_params=pltpu.CompilerParams(
            collective_id=0, has_side_effects=True, vmem_limit_bytes=49 << 20
        ),
        name="block",
    )(*[pltpu.with_memory_space_constraint(a, pltpu.HBM) for a in (emb, proj, w_in, bias, w_out, cot)])


def finish_kernel(
    mixed, grad_out, grad_in, grad_bias, grad_proj,
    mixed_far, grad_out_far, grad_in_far, grad_bias_far, grad_proj_far,
    wide, sems,
):
    copies = [
        pltpu.make_async_copy(grad_out, grad_out_far, sems.at[0]),
        pltpu.make_async_copy(mixed, mixed_far, sems.at[1]),
        pltpu.make_async_copy(grad_bias.at[pl.ds(0, 1)], grad_bias_far, sems.at[2]),
        pltpu.make_async_copy(grad_proj, grad_proj_far, sems.at[3]),
    ]
    for copy in copies:
        copy.start()
    for f in range(4):
        wide[f] = grad_in[f].astype(f32)
        copies.append(pltpu.make_async_copy(wide.at[f], grad_in_far.at[f], sems.at[4 + f]))
        copies[-1].start()
    for copy in copies:
        copy.wait()


def finish(mixed, grad_out, grad_in, grad_bias, grad_proj):
    near = pl.BlockSpec(memory_space=VMEM)
    far = pl.BlockSpec(memory_space=pltpu.HBM)
    return pl.pallas_call(
        finish_kernel,
        out_shape=(
            pltpu.HBM((128, 8, 128), bf16),
            pltpu.HBM((4096, 128), f32),
            pltpu.HBM((4, 8, 128, 128), f32),
            pltpu.HBM((1, 128), f32),
            pltpu.HBM((32, 128), f32),
        ),
        in_specs=[near] * 5,
        out_specs=[far] * 5,
        scratch_shapes=[VMEM((4, 8, 128, 128), f32), DMA((8,))],
        compiler_params=pltpu.CompilerParams(vmem_limit_bytes=16 << 20),
        name="finish",
    )(mixed, grad_out, grad_in, grad_bias, grad_proj)


def local(embeddings, projection, w_in, bias, w_out, cotangent):
    results = everything(
        embeddings.reshape(64, 2, 8, 128), projection.T, w_in.reshape(32, 128, 128),
        bias.reshape(1, 128), w_out, cotangent,
    )
    mixed, grad_out, grad_in, grad_bias, grad_proj = finish(*results)
    return (
        mixed, grad_out.reshape(512, 8, 128), grad_in.reshape(4096, 128),
        grad_bias.reshape(128), grad_proj.T,
    )


def solution(mesh):
    placed = (
        P("batch", "col", "row"),
        P(),
        P("row", "col"),
        P("col"),
        P(None, "col", "row"),
        P("batch", "col", "row"),
    )
    return jax.shard_map(
        local,
        mesh=mesh,
        in_specs=placed,
        out_specs=(
            P("batch", "col", "row"),
            P("batch", "col", "row"),
            P("row", "col"),
            P("col"),
            P("row", None),
        ),
        check_vma=False,
    )
```

```python
import jax
import jax.numpy as jnp
from jax import lax
from jax.experimental import pallas as pl
from jax.experimental.pallas import tpu as pltpu
from jax.sharding import PartitionSpec as P

epsilon = 1e-06
bf16 = jnp.bfloat16
f32 = jnp.float32
MESH = pl.DeviceIdType.MESH
VMEM = pltpu.VMEM
DMA = pltpu.SemaphoreType.DMA
others = (2, 1, 3)
pieces = ((0, 16), (16, 16))


def contract_last(left, right):
    return lax.dot_general(left, right, (((1,), (1,)), ((), ())), preferred_element_type=f32)


def contract_first(left, right):
    return lax.dot_general(left, right, (((0,), (0,)), ((), ())), preferred_element_type=f32)


def dot(left, right):
    return jnp.dot(left, right, preferred_element_type=f32)


def send(src, dst, send_sem, recv_sem, **place):
    copy = pltpu.make_async_remote_copy(
        src_ref=src, dst_ref=dst, send_sem=send_sem, recv_sem=recv_sem,
        device_id=place, device_id_type=MESH,
    )
    copy.start()


def arrived(ref, sem):
    pltpu.make_async_copy(ref, ref, sem).wait()


def split(value):
    high = value.astype(bf16)
    return high, (value - high.astype(f32)).astype(bf16)


def four(parts):
    return (parts[0] + parts[1]) + (parts[2] + parts[3])


def turn(place, k):
    return lax.rem(place + k, 4)


def lanes_of(slot, size=128):
    return pl.ds(pl.multiple_of(slot * size, size), size)


def whole_sum(value):
    return jnp.sum(jnp.sum(value, axis=0, keepdims=True), axis=1, keepdims=True)


def ordering(size, high):
    at = lax.broadcasted_iota(jnp.int32, (size, size), 0)
    of = lax.broadcasted_iota(jnp.int32, (size, size), 1)
    source = lax.rem(at, 8) // 2 * (2 * high) + lax.rem(at, 2) * high + at // 8
    return (of == source).astype(f32).astype(bf16)


def kernel(
    emb, proj_far, w_in_far, bias_far, w_out_far, cot_far,
    mixed, grad_out, grad_wide, grad_bias, grad_proj,
    proj, w_in, w_turned, bias, w_out, cot, w_split, stage, every_cot, own_emb, folds, normed, inv,
    part_out, part_y, part_z_out, part_z, part_x,
    to_row, raw, gathered, pre_x, hidden, d_pre_b,
    d_act, d_y, z_out, z_in, grad_in, acts, d_all, bias_all, hidden_all, own_hidden, hidden_t,
    proj_out, proj_x, proj_z, proj_b,
    load_in, load_out, load_cot, load_proj, load_bias, emb_send, emb_recv, cot_send, cot_recv,
    py_send, py_recv, pz_send, pz_recv, px_send, px_recv,
    near_send, far_send, raw_recv, pre_send, pre_recv,
    h_send, h_recv, oh_send, oh_recv, dy_send, dy_recv, dz_send, dz_recv,
    acts_send, acts_recv, all_send, all_recv, in_send, in_recv, bias_send, bias_recv,
    gx_send, gx_recv, gz_send, gz_recv, gb_send, gb_recv, own_sem,
):
    i = lax.axis_index("batch")
    r = lax.axis_index("row")
    c = lax.axis_index("col")
    y = c // 4
    z = c - y * 4
    sibling = i + 1 - 2 * lax.rem(i, 2)
    across = turn(i, 2)
    diagonal = turn(sibling, 2)
    me = c * 4 + r
    three = pl.ds(0, 3)
    barrier = pltpu.get_barrier_semaphore()

    def greet(k, _):
        peer = lax.rem(me + 1 + lax.rem(k + 40, 63), 64)
        pl.semaphore_signal(
            barrier, inc=1, device_id={"col": peer // 4, "row": lax.rem(peer, 4)},
            device_id_type=MESH,
        )
        return 0

    lax.fori_loop(1, 64, greet, 0)
    for k in others:
        pl.semaphore_signal(barrier, inc=1, device_id={"batch": turn(i, k)}, device_id_type=MESH)
    take_cot = pltpu.make_async_copy(cot_far, cot, load_cot)
    take_cot.start()
    take_out = []
    for k in (1, 2, 3, 0):
        at = lanes_of(turn(y, k), 512)
        take_out.append(pltpu.make_async_copy(w_out_far.at[at], w_out.at[at], load_out.at[k]))
        take_out[-1].start()
    take_proj = pltpu.make_async_copy(proj_far, proj, load_proj)
    take_proj.start()
    take_bias = pltpu.make_async_copy(bias_far, bias, load_bias)
    take_bias.start()
    take_in = pltpu.make_async_copy(w_in_far, w_in, load_in)
    take_in.start()
    take_cot.wait()
    stage[...] = cot[...].astype(f32).reshape(1024, 128)
    for d in range(8):
        every_cot[i, d] = stage[pl.ds(d, 128, stride=8), :].astype(bf16)

    def from_output(k):
        to = turn(y, k)

        def divide(n, _):
            at = pl.multiple_of(to * 512 + n * 128, 128)
            stage[...] = w_out[pl.ds(at, 128)].astype(f32).reshape(1024, 128)
            for d in range(8):
                w_split[d, pl.ds(at, 128), :] = stage[pl.ds(d, 128, stride=8), :].astype(bf16)
            return 0

        lax.fori_loop(0, 4, divide, 0)
        part = jnp.zeros((128, 512), f32)
        for d in range(8):
            part = part + contract_last(every_cot[i, d], w_split[d, lanes_of(to, 512), :])
        for q in range(4):
            part_out[to, q] = part[:, q * 128 : (q + 1) * 128].astype(bf16)

    def share_output(k):
        to = turn(y, k)
        send(part_out.at[to], part_y.at[y], py_send, py_recv.at[y], col=to * 4 + z)

    for n in (0, 1):
        take_out[n].wait()
        from_output(n + 1)
    pl.semaphore_wait(barrier, 66)

    keep = pltpu.make_async_copy(emb.at[me], own_emb.at[r, :, c], emb_recv)
    keep.start()

    def give(k, _):
        peer = lax.rem(me + 1 + lax.rem(k + 40, 63), 64)
        send(
            emb.at[peer], own_emb.at[r, :, c], emb_send, emb_recv,
            col=peer // 4, row=lax.rem(peer, 4),
        )
        return 0

    lax.fori_loop(1, 64, give, 0)
    share_output(1)
    share_output(2)
    take_out[2].wait()
    from_output(3)
    share_output(3)
    take_out[3].wait()
    from_output(0)
    part_y[y] = part_out[y]
    take_proj.wait()
    take_bias.wait()
    lanes = lax.broadcasted_iota(jnp.int32, (32, 128), 1)
    ranks = lax.broadcasted_iota(jnp.int32, (32, 128), 0)
    repeat = (lax.rem(lanes, 32) == ranks).astype(f32).astype(bf16)
    wide = contract_first(proj[...], repeat).astype(bf16)
    block = lax.broadcasted_iota(jnp.int32, (128, 128), 1) // 32
    order = ordering(256, 32)

    def sample(s):
        return jnp.concatenate([own_emb[q, s].reshape(128, 128) for q in range(4)], axis=1)

    arrived(own_emb, emb_recv)
    for s in range(2):
        own = sample(s)
        high, low = split(dot(own, wide))
        both = contract_first(own, jnp.concatenate([high, low], axis=1))
        folds[...] = both[:, :128] + both[:, 128:]
        inter = jnp.zeros((128, 128), f32)
        for j in range(4):
            inter = jnp.where(block == j, folds[pl.ds(j, 128, stride=4), :], inter)
        scale = lax.rsqrt(whole_sum(inter * inter) / (512 * 32) + epsilon)
        norm = inter * scale
        normed[s] = norm
        inv[s] = jnp.broadcast_to(scale, (8, 128))
        for q in range(4):
            to_row[q, s] = norm[q * 32 : (q + 1) * 32].astype(bf16)
    raw[c, r] = to_row[r]
    plane = z * 4 + r

    def scatter(k, _):
        peer = lax.rem(plane + 1 + lax.rem(k + 8, 15), 16)
        to_z = peer // 4
        to_r = lax.rem(peer, 4)
        send(to_row.at[to_r], raw.at[c, r], near_send, raw_recv.at[c], col=y * 4 + to_z, row=to_r)
        return 0

    lax.fori_loop(1, 16, scatter, 0)

    for k in others:
        f = turn(y, k)
        arrived(part_y.at[f], py_recv.at[f])
    for q in range(4):
        part_z_out[q] = four([part_y[f, q].astype(f32) for f in range(4)]).astype(bf16)
    part_z[z] = part_z_out[z]
    for k in others:
        to = turn(z, k)
        send(part_z_out.at[to], part_z.at[z], pz_send, pz_recv.at[z], col=y * 4 + to)

    arrived(raw.at[c, three], raw_recv.at[c])
    for k in others:
        send(raw.at[c], raw.at[c], far_send, raw_recv.at[c], col=turn(y, k) * 4 + z)
    for m in (1, 3, 2):
        slot = y * 4 + turn(z, m)
        arrived(raw.at[slot], raw_recv.at[slot])
        for k in others:
            send(raw.at[slot], raw.at[slot], far_send, raw_recv.at[slot], col=turn(y, k) * 4 + z)
    send(every_cot.at[i], every_cot.at[i], cot_send, cot_recv.at[i], batch=sibling)
    send(every_cot.at[i], every_cot.at[i], cot_send, cot_recv.at[i], batch=across)

    def lay(slot):
        rows = dot(order, raw[slot].reshape(256, 128))
        gathered[:, slot] = rows.reshape(32, 8, 128).astype(bf16)

    for q in range(4):
        lay(y * 4 + q)
    for k in others:
        f = turn(z, k)
        arrived(part_z.at[f], pz_recv.at[f])
    part_x[r] = four([part_z[f].astype(f32) for f in range(4)])
    for k in others:
        send(part_x.at[r], part_x.at[r], px_send, px_recv.at[r], row=turn(r, k))
    take_in.wait()
    for e in range(32):
        w_turned[e] = jnp.transpose(w_in[e])
    for k in range(4):
        for m in others:
            slot = turn(y, m) * 4 + turn(z, k)
            arrived(raw.at[slot], raw_recv.at[slot])
            lay(slot)
    pre = jnp.zeros((128, 128), f32)
    for e in range(32):
        pre = pre + dot(gathered[e].reshape(128, 128), w_in[e])
    pre_x[r] = pre
    for k in others:
        send(pre_x.at[r], pre_x.at[r], pre_send, pre_recv.at[r], row=turn(r, k))
    for k in others:
        to = turn(i, k)
        send(gathered.at[pl.ds(8 * to, 8)], acts.at[i], acts_send, acts_recv.at[i], batch=to)
    mine = pltpu.make_async_copy(gathered.at[pl.ds(8 * i, 8)], acts.at[i], own_sem)
    mine.start()
    for k in others:
        f = turn(r, k)
        arrived(part_x.at[f], px_recv.at[f])
    d_hidden = four(part_x)
    for k in others:
        f = turn(r, k)
        arrived(pre_x.at[f], pre_recv.at[f])
    preact = four(pre_x) + bias[...]
    sig = 1.0 / (1.0 + jnp.exp(-preact))
    hidden[...] = (preact * sig).astype(bf16)
    d_value = d_hidden * sig * (1.0 + preact * (1.0 - sig))
    d_pre_b[...] = d_value.astype(bf16)
    bias_all[i] = jnp.broadcast_to(jnp.sum(d_value, axis=0, keepdims=True), (8, 128))

    for k in others:
        send(hidden, hidden_all.at[:, lanes_of(c)], h_send, h_recv.at[c], col=y * 4 + turn(z, k))
    for n, (first, size) in enumerate(pieces):
        for e in range(first, first + size):
            part = dot(d_pre_b[...], w_turned[e])
            d_act[e] = part.reshape(16, 8, 128).astype(bf16)
        for k in others:
            to = turn(y, k)
            send(
                d_act.at[pl.ds(first, size), pl.ds(4 * to, 4)],
                d_y.at[y, pl.ds(first, size)],
                dy_send, dy_recv.at[n, y], col=to * 4 + z,
            )
    for k in others:
        send(hidden, hidden_all.at[:, lanes_of(c)], h_send, h_recv.at[c], col=turn(y, k) * 4 + z)
    hidden_all[:, lanes_of(c)] = hidden[...]
    d_all[i] = d_pre_b[...]
    for k in others:
        to = turn(i, k)
        send(d_pre_b, d_all.at[i], all_send, all_recv.at[i], batch=to)
        send(bias_all.at[i], bias_all.at[i], bias_send, bias_recv.at[i], batch=to)
    for m in others:
        slot = y * 4 + turn(z, m)
        place = hidden_all.at[:, lanes_of(slot)]
        arrived(place, h_recv.at[slot])
        for k in others:
            send(place, place, h_send, h_recv.at[slot], col=turn(y, k) * 4 + z)
    arrived(every_cot.at[across], cot_recv.at[across])
    send(every_cot.at[across], every_cot.at[across], cot_send, cot_recv.at[across], batch=sibling)
    for n, (first, size) in enumerate(pieces):
        d_z_out, d_z = z_out[n], z_in[n]
        undo = ordering(8 * size, size)
        span = pl.ds(first, size)
        d_y[y, span] = d_act[span, pl.ds(4 * y, 4)]
        for k in others:
            f = turn(y, k)
            arrived(d_y.at[f, span], dy_recv.at[n, f])
        for q in range(4):
            part = four([d_y[f, span, q].astype(f32) for f in range(4)])
            rows = contract_first(undo, part.reshape(8 * size, 128).astype(bf16))
            for g in range(4):
                d_z_out[q * 4 + g] = (
                    rows[g * 2 * size : (g + 1) * 2 * size].reshape(2, size, 128).astype(bf16)
                )
        d_z[plane] = d_z_out[plane]

        def hand(k, _):
            peer = lax.rem(plane + 1 + lax.rem(k + 8, 15), 16)
            send(
                d_z_out.at[peer], d_z.at[plane], dz_send.at[n], dz_recv.at[n],
                col=y * 4 + peer // 4, row=lax.rem(peer, 4),
            )
            return 0

        lax.fori_loop(1, 16, hand, 0)
    for m in others:
        for k in range(4):
            slot = turn(y, m) * 4 + k
            arrived(hidden_all.at[:, lanes_of(slot)], h_recv.at[slot])
    own_hidden[i] = hidden_all[:, lanes_of(i, 512)]
    mine.wait()
    for k in others:
        f = turn(i, k)
        arrived(d_all.at[f], all_recv.at[f])
        arrived(acts.at[f], acts_recv.at[f])
    for e in range(8):
        part = four([contract_first(acts[f, e].reshape(128, 128), d_all[f]) for f in range(4)])
        grad_in[i, e] = part.astype(bf16)
    send(grad_in.at[i], grad_in.at[i], in_send, in_recv.at[i], batch=sibling)
    send(grad_in.at[i], grad_in.at[i], in_send, in_recv.at[i], batch=across)
    grad_wide[i] = grad_in[i].astype(f32)
    for n in range(len(pieces)):
        arrived(z_in[n].at[pl.ds(0, 15)], dz_recv.at[n])
    for k in others:
        to = turn(i, k)
        send(
            hidden_all.at[:, lanes_of(to, 512)], own_hidden.at[i], oh_send, oh_recv.at[i],
            batch=to,
        )
    for s in range(2):
        grad = jnp.concatenate(
            [
                four([d_z[q * 4 + g, s].astype(f32) for q in range(4)])
                for g in range(4)
                for d_z in z_in
            ],
            axis=0,
        )
        norm = normed[s]
        inner = whole_sum(grad * norm) / (512 * 32)
        d_inter = (inv[s, 0:1, :] * (grad - norm * inner)).astype(bf16).astype(f32)
        for j in range(4):
            folds[pl.ds(j, 128, stride=4), :] = jnp.where(block == j, d_inter, 0.0)
        own = sample(s)
        fold = dot(own, folds[...].astype(bf16))
        fold = fold + pltpu.roll(fold, 32, 1)
        fold = fold + pltpu.roll(fold, 64, 1)
        high, low = split(jnp.transpose(fold)[:32])
        both = dot(jnp.concatenate([high, low], axis=0), own)
        for q in range(4):
            part = both[:32, q * 128 : (q + 1) * 128] + both[32:, q * 128 : (q + 1) * 128]
            if s == 0:
                proj_out[q] = part
            else:
                proj_out[q] += part
    flat = y * 4 + r
    proj_x[flat] = proj_out[r]

    def hand_on(k, _):
        peer = lax.rem(flat + 1 + lax.rem(k + 8, 15), 16)
        to_r = lax.rem(peer, 4)
        send(
            proj_out.at[to_r], proj_x.at[flat], gx_send, gx_recv,
            col=peer // 4 * 4 + z, row=to_r,
        )
        return 0

    lax.fori_loop(1, 16, hand_on, 0)
    for d in range(8):
        stage[pl.ds(d, 128, stride=8), :] = dot(hidden_all[...], w_split[d])
    mixed[...] = stage[...].reshape(128, 8, 128).astype(bf16)
    arrived(proj_x.at[pl.ds(0, 15)], gx_recv)
    proj_z[z] = four([four([proj_x[q * 4 + g] for g in range(4)]) for q in range(4)])
    for k in others:
        send(proj_z.at[z], proj_z.at[z], gz_send, gz_recv.at[z], col=y * 4 + turn(z, k))
    for k in others:
        f = turn(z, k)
        arrived(proj_z.at[f], gz_recv.at[f])
    proj_b[i] = four(proj_z)
    for k in others:
        send(proj_b.at[i], proj_b.at[i], gb_send, gb_recv.at[i], batch=turn(i, k))
    arrived(grad_in.at[across], in_recv.at[across])
    send(grad_in.at[across], grad_in.at[across], in_send, in_recv.at[across], batch=sibling)
    grad_wide[across] = grad_in[across].astype(f32)
    arrived(grad_in.at[sibling], in_recv.at[sibling])
    grad_wide[sibling] = grad_in[sibling].astype(f32)
    for k in others:
        f = turn(i, k)
        arrived(own_hidden.at[f], oh_recv.at[f])
    arrived(every_cot.at[sibling], cot_recv.at[sibling])
    arrived(every_cot.at[diagonal], cot_recv.at[diagonal])
    for f in range(4):
        hidden_t[:, f * 128 : (f + 1) * 128] = jnp.transpose(own_hidden[f])

    def outer(d):
        cots = jnp.concatenate([every_cot[f, d] for f in range(4)], axis=0)
        grad_out[pl.ds(d, 512, stride=8), :] = dot(hidden_t[...], cots)

    for d in range(4):
        outer(d)
    for d in range(4, 8):
        outer(d)
    for k in others:
        f = turn(i, k)
        arrived(bias_all.at[f], bias_recv.at[f])
    grad_bias[...] = four(bias_all)
    for k in others:
        f = turn(i, k)
        arrived(proj_b.at[f], gb_recv.at[f])
    grad_proj[...] = four(proj_b)
    arrived(grad_in.at[diagonal], in_recv.at[diagonal])
    grad_wide[diagonal] = grad_in[diagonal].astype(f32)
    arrived(emb.at[pl.ds(0, 63)], emb_send)
    arrived(every_cot.at[three], cot_send)
    arrived(part_y.at[three], py_send)
    arrived(part_z.at[three], pz_send)
    arrived(part_x.at[three], px_send)
    arrived(raw.at[pl.ds(0, 15), 0], near_send)
    arrived(raw.at[pl.ds(0, 12)], far_send)
    arrived(pre_x.at[three], pre_send)
    arrived(hidden_all.at[:, pl.ds(0, 15 * 128)], h_send)
    arrived(own_hidden.at[three], oh_send)
    arrived(d_act.at[:, pl.ds(0, 12)], dy_send)
    for n in range(len(pieces)):
        arrived(z_out[n].at[pl.ds(0, 15)], dz_send.at[n])
    arrived(acts.at[three], acts_send)
    arrived(d_all.at[three], all_send)
    arrived(grad_in.at[three], in_send)
    arrived(bias_all.at[three], bias_send)
    arrived(proj_x.at[pl.ds(0, 15)], gx_send)
    arrived(proj_z.at[three], gz_send)
    arrived(proj_b.at[three], gb_send)


def everything(emb, proj, w_in, bias, w_out, cot):
    out = jax.ShapeDtypeStruct
    pair = [DMA, DMA((4,))]
    count = len(pieces)
    far = pl.BlockSpec(memory_space=pltpu.HBM)
    near = pl.BlockSpec(memory_space=VMEM)
    return pl.pallas_call(
        kernel,
        out_shape=(
            out((128, 8, 128), bf16),
            out((4096, 128), f32),
            out((4, 8, 128, 128), f32),
            out((8, 128), f32),
            out((32, 128), f32),
        ),
        in_specs=[far] * 6,
        out_specs=[near] * 5,
        scratch_shapes=[
            VMEM((32, 512), bf16),
            VMEM((32, 128, 128), bf16),
            VMEM((32, 128, 128), bf16),
            VMEM((1, 128), f32),
            VMEM((2048, 8, 128), bf16),
            VMEM((128, 8, 128), bf16),
            VMEM((8, 2048, 128), bf16),
            VMEM((1024, 128), f32),
            VMEM((4, 8, 128, 128), bf16),
            VMEM((4, 2, 16, 8, 128), bf16),
            VMEM((512, 128), f32),
            VMEM((2, 128, 128), f32),
            VMEM((2, 8, 128), f32),
            VMEM((4, 4, 128, 128), bf16),
            VMEM((4, 4, 128, 128), bf16),
            VMEM((4, 128, 128), bf16),
            VMEM((4, 128, 128), bf16),
            VMEM((4, 128, 128), f32),
            VMEM((4, 2, 32, 128), bf16),
            VMEM((16, 4, 2, 32, 128), bf16),
            VMEM((32, 16, 8, 128), bf16),
            VMEM((4, 128, 128), f32),
            VMEM((128, 128), bf16),
            VMEM((128, 128), bf16),
            VMEM((32, 16, 8, 128), bf16),
            VMEM((4, 32, 4, 8, 128), bf16),
            tuple(VMEM((16, 2, size, 128), bf16) for _, size in pieces),
            tuple(VMEM((16, 2, size, 128), bf16) for _, size in pieces),
            VMEM((4, 8, 128, 128), bf16),
            VMEM((4, 8, 16, 8, 128), bf16),
            VMEM((4, 128, 128), bf16),
            VMEM((4, 8, 128), f32),
            VMEM((128, 2048), bf16),
            VMEM((4, 128, 512), bf16),
            VMEM((512, 512), bf16),
            VMEM((4, 32, 128), f32),
            VMEM((16, 32, 128), f32),
            VMEM((4, 32, 128), f32),
            VMEM((4, 32, 128), f32),
            DMA, DMA((4,)), DMA, DMA, DMA, DMA, DMA, *pair,
            *pair, *pair, *pair,
            DMA, DMA, DMA((16,)), *pair,
            DMA, DMA((16,)), *pair, DMA, DMA((count, 4)), DMA((count,)), DMA((count,)),
            *pair, *pair, *pair, *pair,
            DMA, DMA, *pair, *pair, DMA,
        ],
        compiler_params=pltpu.CompilerParams(
            collective_id=0, has_side_effects=True, vmem_limit_bytes=49 << 20
        ),
        name="block",
    )(*[pltpu.with_memory_space_constraint(a, pltpu.HBM) for a in (emb, proj, w_in, bias, w_out, cot)])


def finish_kernel(
    mixed, grad_out, grad_in, grad_bias, grad_proj,
    mixed_far, grad_out_far, grad_in_far, grad_bias_far, grad_proj_far,
    sems,
):
    copies = [
        pltpu.make_async_copy(grad_out, grad_out_far, sems.at[0]),
        pltpu.make_async_copy(grad_in, grad_in_far, sems.at[4]),
        pltpu.make_async_copy(mixed, mixed_far, sems.at[1]),
        pltpu.make_async_copy(grad_bias.at[pl.ds(0, 1)], grad_bias_far, sems.at[2]),
        pltpu.make_async_copy(grad_proj, grad_proj_far, sems.at[3]),
    ]
    for copy in copies:
        copy.start()
    for copy in copies:
        copy.wait()


def finish(mixed, grad_out, grad_in, grad_bias, grad_proj):
    near = pl.BlockSpec(memory_space=VMEM)
    far = pl.BlockSpec(memory_space=pltpu.HBM)
    return pl.pallas_call(
        finish_kernel,
        out_shape=(
            pltpu.HBM((128, 8, 128), bf16),
            pltpu.HBM((4096, 128), f32),
            pltpu.HBM((4, 8, 128, 128), f32),
            pltpu.HBM((1, 128), f32),
            pltpu.HBM((32, 128), f32),
        ),
        in_specs=[near] * 5,
        out_specs=[far] * 5,
        scratch_shapes=[DMA((5,))],
        compiler_params=pltpu.CompilerParams(vmem_limit_bytes=16 << 20),
        name="finish",
    )(mixed, grad_out, grad_in, grad_bias, grad_proj)


def local(embeddings, projection, w_in, bias, w_out, cotangent):
    results = everything(
        embeddings.reshape(64, 2, 8, 128), projection.T, w_in.reshape(32, 128, 128),
        bias.reshape(1, 128), w_out, cotangent,
    )
    mixed, grad_out, grad_in, grad_bias, grad_proj = finish(*results)
    return (
        mixed, grad_out.reshape(512, 8, 128), grad_in.reshape(4096, 128),
        grad_bias.reshape(128), grad_proj.T,
    )


def solution(mesh):
    placed = (
        P("batch", "col", "row"),
        P(),
        P("row", "col"),
        P("col"),
        P(None, "col", "row"),
        P("batch", "col", "row"),
    )
    return jax.shard_map(
        local,
        mesh=mesh,
        in_specs=placed,
        out_specs=(
            P("batch", "col", "row"),
            P("batch", "col", "row"),
            P("row", "col"),
            P("col"),
            P("row", None),
        ),
        check_vma=False,
    )
```

```python
import jax
import jax.numpy as jnp
from jax import lax
from jax.experimental import pallas as pl
from jax.experimental.pallas import tpu as pltpu
from jax.sharding import PartitionSpec as P

epsilon = 1e-06
bf16 = jnp.bfloat16
f32 = jnp.float32
MESH = pl.DeviceIdType.MESH
VMEM = pltpu.VMEM
DMA = pltpu.SemaphoreType.DMA
others = (2, 1, 3)
pieces = ((0, 16), (16, 16))


def contract_last(left, right):
    return lax.dot_general(left, right, (((1,), (1,)), ((), ())), preferred_element_type=f32)


def contract_first(left, right):
    return lax.dot_general(left, right, (((0,), (0,)), ((), ())), preferred_element_type=f32)


def dot(left, right):
    return jnp.dot(left, right, preferred_element_type=f32)


def send(src, dst, send_sem, recv_sem, **place):
    copy = pltpu.make_async_remote_copy(
        src_ref=src, dst_ref=dst, send_sem=send_sem, recv_sem=recv_sem,
        device_id=place, device_id_type=MESH,
    )
    copy.start()


def arrived(ref, sem):
    pltpu.make_async_copy(ref, ref, sem).wait()


def split(value):
    high = value.astype(bf16)
    return high, (value - high.astype(f32)).astype(bf16)


def four(parts):
    return (parts[0] + parts[1]) + (parts[2] + parts[3])


def turn(place, k):
    return lax.rem(place + k, 4)


def lanes_of(slot, size=128):
    return pl.ds(pl.multiple_of(slot * size, size), size)


def whole_sum(value):
    return jnp.sum(jnp.sum(value, axis=0, keepdims=True), axis=1, keepdims=True)


def ordering(size, high):
    at = lax.broadcasted_iota(jnp.int32, (size, size), 0)
    of = lax.broadcasted_iota(jnp.int32, (size, size), 1)
    source = lax.rem(at, 8) // 2 * (2 * high) + lax.rem(at, 2) * high + at // 8
    return (of == source).astype(f32).astype(bf16)


def kernel(
    emb, proj_far, w_in_far, bias_far, w_out_far, cot_far,
    mixed, grad_out, grad_in, grad_bias, grad_proj,
    proj, w_in, w_turned, bias, w_out, cot, w_split, stage, every_cot, own_emb, folds, normed, inv,
    part_out, part_y, part_z_out, part_z, part_x,
    to_row, raw, gathered, pre_x, hidden, d_pre_b,
    d_act, d_y, z_out, z_in, acts, d_all, bias_all, hidden_all, own_hidden, hidden_t,
    proj_out, proj_x, proj_z, proj_b,
    load_in, load_out, load_cot, load_proj, load_bias, emb_send, emb_recv, cot_send, cot_recv,
    py_send, py_recv, pz_send, pz_recv, px_send, px_recv,
    near_send, far_send, raw_recv, pre_send, pre_recv,
    h_send, h_recv, oh_send, oh_recv, dy_send, dy_recv, dz_send, dz_recv,
    acts_send, acts_recv, all_send, all_recv, in_send, in_recv, bias_send, bias_recv,
    gx_send, gx_recv, gz_send, gz_recv, gb_send, gb_recv, own_sem,
):
    i = lax.axis_index("batch")
    r = lax.axis_index("row")
    c = lax.axis_index("col")
    y = c // 4
    z = c - y * 4
    sibling = i + 1 - 2 * lax.rem(i, 2)
    across = turn(i, 2)
    diagonal = turn(sibling, 2)
    me = c * 4 + r
    three = pl.ds(0, 3)
    barrier = pltpu.get_barrier_semaphore()

    def greet(k, _):
        peer = lax.rem(me + 1 + lax.rem(k + 40, 63), 64)
        pl.semaphore_signal(
            barrier, inc=1, device_id={"col": peer // 4, "row": lax.rem(peer, 4)},
            device_id_type=MESH,
        )
        return 0

    lax.fori_loop(1, 64, greet, 0)
    for k in others:
        pl.semaphore_signal(barrier, inc=1, device_id={"batch": turn(i, k)}, device_id_type=MESH)
    take_cot = pltpu.make_async_copy(cot_far, cot, load_cot)
    take_cot.start()
    take_out = []
    for k in (1, 2, 3, 0):
        at = lanes_of(turn(y, k), 512)
        take_out.append(pltpu.make_async_copy(w_out_far.at[at], w_out.at[at], load_out.at[k]))
        take_out[-1].start()
    take_proj = pltpu.make_async_copy(proj_far, proj, load_proj)
    take_proj.start()
    take_bias = pltpu.make_async_copy(bias_far, bias, load_bias)
    take_bias.start()
    take_in = pltpu.make_async_copy(w_in_far, w_in, load_in)
    take_in.start()
    take_cot.wait()
    stage[...] = cot[...].astype(f32).reshape(1024, 128)
    for d in range(8):
        every_cot[i, d] = stage[pl.ds(d, 128, stride=8), :].astype(bf16)

    def from_output(k):
        to = turn(y, k)

        def divide(n, _):
            at = pl.multiple_of(to * 512 + n * 128, 128)
            stage[...] = w_out[pl.ds(at, 128)].astype(f32).reshape(1024, 128)
            for d in range(8):
                w_split[d, pl.ds(at, 128), :] = stage[pl.ds(d, 128, stride=8), :].astype(bf16)
            return 0

        lax.fori_loop(0, 4, divide, 0)
        part = jnp.zeros((128, 512), f32)
        for d in range(8):
            part = part + contract_last(every_cot[i, d], w_split[d, lanes_of(to, 512), :])
        for q in range(4):
            part_out[to, q] = part[:, q * 128 : (q + 1) * 128].astype(bf16)

    def share_output(k):
        to = turn(y, k)
        send(part_out.at[to], part_y.at[y], py_send, py_recv.at[y], col=to * 4 + z)

    for n in (0, 1):
        take_out[n].wait()
        from_output(n + 1)
    pl.semaphore_wait(barrier, 66)

    keep = pltpu.make_async_copy(emb.at[me], own_emb.at[r, :, c], emb_recv)
    keep.start()

    def give(k, _):
        peer = lax.rem(me + 1 + lax.rem(k + 40, 63), 64)
        send(
            emb.at[peer], own_emb.at[r, :, c], emb_send, emb_recv,
            col=peer // 4, row=lax.rem(peer, 4),
        )
        return 0

    lax.fori_loop(1, 64, give, 0)
    share_output(1)
    share_output(2)
    take_out[2].wait()
    from_output(3)
    share_output(3)
    take_out[3].wait()
    from_output(0)
    part_y[y] = part_out[y]
    take_proj.wait()
    take_bias.wait()
    lanes = lax.broadcasted_iota(jnp.int32, (32, 128), 1)
    ranks = lax.broadcasted_iota(jnp.int32, (32, 128), 0)
    repeat = (lax.rem(lanes, 32) == ranks).astype(f32).astype(bf16)
    wide = contract_first(proj[...], repeat).astype(bf16)
    block = lax.broadcasted_iota(jnp.int32, (128, 128), 1) // 32
    order = ordering(256, 32)

    def sample(s):
        return jnp.concatenate([own_emb[q, s].reshape(128, 128) for q in range(4)], axis=1)

    arrived(own_emb, emb_recv)
    for s in range(2):
        own = sample(s)
        high, low = split(dot(own, wide))
        both = contract_first(own, jnp.concatenate([high, low], axis=1))
        folds[...] = both[:, :128] + both[:, 128:]
        inter = jnp.zeros((128, 128), f32)
        for j in range(4):
            inter = jnp.where(block == j, folds[pl.ds(j, 128, stride=4), :], inter)
        scale = lax.rsqrt(whole_sum(inter * inter) / (512 * 32) + epsilon)
        norm = inter * scale
        normed[s] = norm
        inv[s] = jnp.broadcast_to(scale, (8, 128))
        for q in range(4):
            to_row[q, s] = norm[q * 32 : (q + 1) * 32].astype(bf16)
    raw[c, r] = to_row[r]
    plane = z * 4 + r

    def scatter(k, _):
        peer = lax.rem(plane + 1 + lax.rem(k + 8, 15), 16)
        to_z = peer // 4
        to_r = lax.rem(peer, 4)
        send(to_row.at[to_r], raw.at[c, r], near_send, raw_recv.at[c], col=y * 4 + to_z, row=to_r)
        return 0

    lax.fori_loop(1, 16, scatter, 0)

    for k in others:
        f = turn(y, k)
        arrived(part_y.at[f], py_recv.at[f])
    for q in range(4):
        part_z_out[q] = four([part_y[f, q].astype(f32) for f in range(4)]).astype(bf16)
    part_z[z] = part_z_out[z]
    for k in others:
        to = turn(z, k)
        send(part_z_out.at[to], part_z.at[z], pz_send, pz_recv.at[z], col=y * 4 + to)

    arrived(raw.at[c, three], raw_recv.at[c])
    for k in others:
        send(raw.at[c], raw.at[c], far_send, raw_recv.at[c], col=turn(y, k) * 4 + z)
    for m in (1, 3, 2):
        slot = y * 4 + turn(z, m)
        arrived(raw.at[slot], raw_recv.at[slot])
        for k in others:
            send(raw.at[slot], raw.at[slot], far_send, raw_recv.at[slot], col=turn(y, k) * 4 + z)
    send(every_cot.at[i], every_cot.at[i], cot_send, cot_recv.at[i], batch=sibling)
    send(every_cot.at[i], every_cot.at[i], cot_send, cot_recv.at[i], batch=across)

    def lay(slot):
        rows = dot(order, raw[slot].reshape(256, 128))
        gathered[:, slot] = rows.reshape(32, 8, 128).astype(bf16)

    for q in range(4):
        lay(y * 4 + q)
    for k in others:
        f = turn(z, k)
        arrived(part_z.at[f], pz_recv.at[f])
    part_x[r] = four([part_z[f].astype(f32) for f in range(4)])
    for k in others:
        send(part_x.at[r], part_x.at[r], px_send, px_recv.at[r], row=turn(r, k))
    take_in.wait()
    for e in range(32):
        w_turned[e] = jnp.transpose(w_in[e])
    for k in range(4):
        for m in others:
            slot = turn(y, m) * 4 + turn(z, k)
            arrived(raw.at[slot], raw_recv.at[slot])
            lay(slot)
    pre = jnp.zeros((128, 128), f32)
    for e in range(32):
        pre = pre + dot(gathered[e].reshape(128, 128), w_in[e])
    pre_x[r] = pre
    for k in others:
        send(pre_x.at[r], pre_x.at[r], pre_send, pre_recv.at[r], row=turn(r, k))
    for k in others:
        to = turn(i, k)
        send(gathered.at[pl.ds(8 * to, 8)], acts.at[i], acts_send, acts_recv.at[i], batch=to)
    mine = pltpu.make_async_copy(gathered.at[pl.ds(8 * i, 8)], acts.at[i], own_sem)
    mine.start()
    for k in others:
        f = turn(r, k)
        arrived(part_x.at[f], px_recv.at[f])
    d_hidden = four(part_x)
    for k in others:
        f = turn(r, k)
        arrived(pre_x.at[f], pre_recv.at[f])
    preact = four(pre_x) + bias[...]
    sig = 1.0 / (1.0 + jnp.exp(-preact))
    hidden[...] = (preact * sig).astype(bf16)
    d_value = d_hidden * sig * (1.0 + preact * (1.0 - sig))
    d_pre_b[...] = d_value.astype(bf16)
    bias_all[i] = jnp.broadcast_to(jnp.sum(d_value, axis=0, keepdims=True), (8, 128))

    for k in others:
        send(hidden, hidden_all.at[:, lanes_of(c)], h_send, h_recv.at[c], col=y * 4 + turn(z, k))
    for n, (first, size) in enumerate(pieces):
        for e in range(first, first + size):
            part = dot(d_pre_b[...], w_turned[e])
            d_act[e] = part.reshape(16, 8, 128).astype(bf16)
        for k in others:
            to = turn(y, k)
            send(
                d_act.at[pl.ds(first, size), pl.ds(4 * to, 4)],
                d_y.at[y, pl.ds(first, size)],
                dy_send, dy_recv.at[n, y], col=to * 4 + z,
            )
    for k in others:
        send(hidden, hidden_all.at[:, lanes_of(c)], h_send, h_recv.at[c], col=turn(y, k) * 4 + z)
    hidden_all[:, lanes_of(c)] = hidden[...]
    d_all[i] = d_pre_b[...]
    for k in others:
        to = turn(i, k)
        send(d_pre_b, d_all.at[i], all_send, all_recv.at[i], batch=to)
        send(bias_all.at[i], bias_all.at[i], bias_send, bias_recv.at[i], batch=to)
    for m in others:
        slot = y * 4 + turn(z, m)
        place = hidden_all.at[:, lanes_of(slot)]
        arrived(place, h_recv.at[slot])
        for k in others:
            send(place, place, h_send, h_recv.at[slot], col=turn(y, k) * 4 + z)
    arrived(every_cot.at[across], cot_recv.at[across])
    send(every_cot.at[across], every_cot.at[across], cot_send, cot_recv.at[across], batch=sibling)
    for n, (first, size) in enumerate(pieces):
        d_z_out, d_z = z_out[n], z_in[n]
        undo = ordering(8 * size, size)
        span = pl.ds(first, size)
        d_y[y, span] = d_act[span, pl.ds(4 * y, 4)]
        for k in others:
            f = turn(y, k)
            arrived(d_y.at[f, span], dy_recv.at[n, f])
        for q in range(4):
            part = four([d_y[f, span, q].astype(f32) for f in range(4)])
            rows = contract_first(undo, part.reshape(8 * size, 128).astype(bf16))
            for g in range(4):
                d_z_out[q * 4 + g] = (
                    rows[g * 2 * size : (g + 1) * 2 * size].reshape(2, size, 128).astype(bf16)
                )
        d_z[plane] = d_z_out[plane]

        def hand(k, _):
            peer = lax.rem(plane + 1 + lax.rem(k + 8, 15), 16)
            send(
                d_z_out.at[peer], d_z.at[plane], dz_send.at[n], dz_recv.at[n],
                col=y * 4 + peer // 4, row=lax.rem(peer, 4),
            )
            return 0

        lax.fori_loop(1, 16, hand, 0)
    for m in others:
        for k in range(4):
            slot = turn(y, m) * 4 + k
            arrived(hidden_all.at[:, lanes_of(slot)], h_recv.at[slot])
    own_hidden[i] = hidden_all[:, lanes_of(i, 512)]
    for d in range(8):
        stage[pl.ds(d, 128, stride=8), :] = dot(hidden_all[...], w_split[d])
    mixed[...] = stage[...].reshape(128, 8, 128).astype(bf16)
    mine.wait()
    for k in others:
        f = turn(i, k)
        arrived(d_all.at[f], all_recv.at[f])
        arrived(acts.at[f], acts_recv.at[f])
    for e in range(8):
        part = four([contract_first(acts[f, e].reshape(128, 128), d_all[f]) for f in range(4)])
        grad_in[i, e] = part.astype(bf16)
    send(grad_in.at[i], grad_in.at[i], in_send, in_recv.at[i], batch=sibling)
    send(grad_in.at[i], grad_in.at[i], in_send, in_recv.at[i], batch=across)
    for n in range(len(pieces)):
        arrived(z_in[n].at[pl.ds(0, 15)], dz_recv.at[n])
    for k in others:
        to = turn(i, k)
        send(
            hidden_all.at[:, lanes_of(to, 512)], own_hidden.at[i], oh_send, oh_recv.at[i],
            batch=to,
        )
    for s in range(2):
        grad = jnp.concatenate(
            [
                four([d_z[q * 4 + g, s].astype(f32) for q in range(4)])
                for g in range(4)
                for d_z in z_in
            ],
            axis=0,
        )
        norm = normed[s]
        inner = whole_sum(grad * norm) / (512 * 32)
        d_inter = (inv[s, 0:1, :] * (grad - norm * inner)).astype(bf16).astype(f32)
        for j in range(4):
            folds[pl.ds(j, 128, stride=4), :] = jnp.where(block == j, d_inter, 0.0)
        own = sample(s)
        fold = dot(own, folds[...].astype(bf16))
        fold = fold + pltpu.roll(fold, 32, 1)
        fold = fold + pltpu.roll(fold, 64, 1)
        high, low = split(jnp.transpose(fold)[:32])
        both = dot(jnp.concatenate([high, low], axis=0), own)
        for q in range(4):
            part = both[:32, q * 128 : (q + 1) * 128] + both[32:, q * 128 : (q + 1) * 128]
            if s == 0:
                proj_out[q] = part
            else:
                proj_out[q] += part
    flat = y * 4 + r
    proj_x[flat] = proj_out[r]

    def hand_on(k, _):
        peer = lax.rem(flat + 1 + lax.rem(k + 8, 15), 16)
        to_r = lax.rem(peer, 4)
        send(
            proj_out.at[to_r], proj_x.at[flat], gx_send, gx_recv,
            col=peer // 4 * 4 + z, row=to_r,
        )
        return 0

    lax.fori_loop(1, 16, hand_on, 0)
    arrived(proj_x.at[pl.ds(0, 15)], gx_recv)
    proj_z[z] = four([four([proj_x[q * 4 + g] for g in range(4)]) for q in range(4)])
    for k in others:
        send(proj_z.at[z], proj_z.at[z], gz_send, gz_recv.at[z], col=y * 4 + turn(z, k))
    for k in others:
        f = turn(z, k)
        arrived(proj_z.at[f], gz_recv.at[f])
    proj_b[i] = four(proj_z)
    for k in others:
        send(proj_b.at[i], proj_b.at[i], gb_send, gb_recv.at[i], batch=turn(i, k))
    arrived(grad_in.at[across], in_recv.at[across])
    send(grad_in.at[across], grad_in.at[across], in_send, in_recv.at[across], batch=sibling)
    for k in others:
        f = turn(i, k)
        arrived(own_hidden.at[f], oh_recv.at[f])
    arrived(every_cot.at[sibling], cot_recv.at[sibling])
    arrived(every_cot.at[diagonal], cot_recv.at[diagonal])
    for f in range(4):
        hidden_t[:, f * 128 : (f + 1) * 128] = jnp.transpose(own_hidden[f])

    def outer(d):
        cots = jnp.concatenate([every_cot[f, d] for f in range(4)], axis=0)
        grad_out[pl.ds(d, 512, stride=8), :] = dot(hidden_t[...], cots)

    for d in range(4):
        outer(d)
    for d in range(4, 8):
        outer(d)
    for k in others:
        f = turn(i, k)
        arrived(bias_all.at[f], bias_recv.at[f])
    grad_bias[...] = four(bias_all)
    for k in others:
        f = turn(i, k)
        arrived(proj_b.at[f], gb_recv.at[f])
    grad_proj[...] = four(proj_b)
    arrived(grad_in.at[sibling], in_recv.at[sibling])
    arrived(grad_in.at[diagonal], in_recv.at[diagonal])
    arrived(emb.at[pl.ds(0, 63)], emb_send)
    arrived(every_cot.at[three], cot_send)
    arrived(part_y.at[three], py_send)
    arrived(part_z.at[three], pz_send)
    arrived(part_x.at[three], px_send)
    arrived(raw.at[pl.ds(0, 15), 0], near_send)
    arrived(raw.at[pl.ds(0, 12)], far_send)
    arrived(pre_x.at[three], pre_send)
    arrived(hidden_all.at[:, pl.ds(0, 15 * 128)], h_send)
    arrived(own_hidden.at[three], oh_send)
    arrived(d_act.at[:, pl.ds(0, 12)], dy_send)
    for n in range(len(pieces)):
        arrived(z_out[n].at[pl.ds(0, 15)], dz_send.at[n])
    arrived(acts.at[three], acts_send)
    arrived(d_all.at[three], all_send)
    arrived(grad_in.at[three], in_send)
    arrived(bias_all.at[three], bias_send)
    arrived(proj_x.at[pl.ds(0, 15)], gx_send)
    arrived(proj_z.at[three], gz_send)
    arrived(proj_b.at[three], gb_send)


def everything(emb, proj, w_in, bias, w_out, cot):
    out = jax.ShapeDtypeStruct
    pair = [DMA, DMA((4,))]
    count = len(pieces)
    far = pl.BlockSpec(memory_space=pltpu.HBM)
    near = pl.BlockSpec(memory_space=VMEM)
    return pl.pallas_call(
        kernel,
        out_shape=(
            out((128, 8, 128), bf16),
            out((4096, 128), f32),
            out((4, 8, 128, 128), bf16),
            out((8, 128), f32),
            out((32, 128), f32),
        ),
        in_specs=[far] * 6,
        out_specs=[near] * 5,
        scratch_shapes=[
            VMEM((32, 512), bf16),
            VMEM((32, 128, 128), bf16),
            VMEM((32, 128, 128), bf16),
            VMEM((1, 128), f32),
            VMEM((2048, 8, 128), bf16),
            VMEM((128, 8, 128), bf16),
            VMEM((8, 2048, 128), bf16),
            VMEM((1024, 128), f32),
            VMEM((4, 8, 128, 128), bf16),
            VMEM((4, 2, 16, 8, 128), bf16),
            VMEM((512, 128), f32),
            VMEM((2, 128, 128), f32),
            VMEM((2, 8, 128), f32),
            VMEM((4, 4, 128, 128), bf16),
            VMEM((4, 4, 128, 128), bf16),
            VMEM((4, 128, 128), bf16),
            VMEM((4, 128, 128), bf16),
            VMEM((4, 128, 128), f32),
            VMEM((4, 2, 32, 128), bf16),
            VMEM((16, 4, 2, 32, 128), bf16),
            VMEM((32, 16, 8, 128), bf16),
            VMEM((4, 128, 128), f32),
            VMEM((128, 128), bf16),
            VMEM((128, 128), bf16),
            VMEM((32, 16, 8, 128), bf16),
            VMEM((4, 32, 4, 8, 128), bf16),
            tuple(VMEM((16, 2, size, 128), bf16) for _, size in pieces),
            tuple(VMEM((16, 2, size, 128), bf16) for _, size in pieces),
            VMEM((4, 8, 16, 8, 128), bf16),
            VMEM((4, 128, 128), bf16),
            VMEM((4, 8, 128), f32),
            VMEM((128, 2048), bf16),
            VMEM((4, 128, 512), bf16),
            VMEM((512, 512), bf16),
            VMEM((4, 32, 128), f32),
            VMEM((16, 32, 128), f32),
            VMEM((4, 32, 128), f32),
            VMEM((4, 32, 128), f32),
            DMA, DMA((4,)), DMA, DMA, DMA, DMA, DMA, *pair,
            *pair, *pair, *pair,
            DMA, DMA, DMA((16,)), *pair,
            DMA, DMA((16,)), *pair, DMA, DMA((count, 4)), DMA((count,)), DMA((count,)),
            *pair, *pair, *pair, *pair,
            DMA, DMA, *pair, *pair, DMA,
        ],
        compiler_params=pltpu.CompilerParams(
            collective_id=0, has_side_effects=True, vmem_limit_bytes=49 << 20
        ),
        name="block",
    )(*[pltpu.with_memory_space_constraint(a, pltpu.HBM) for a in (emb, proj, w_in, bias, w_out, cot)])


def finish_kernel(
    mixed, grad_out, grad_in, grad_bias, grad_proj,
    mixed_far, grad_out_far, grad_in_far, grad_bias_far, grad_proj_far,
    wide, sems,
):
    copies = [
        pltpu.make_async_copy(grad_out, grad_out_far, sems.at[0]),
        pltpu.make_async_copy(mixed, mixed_far, sems.at[1]),
        pltpu.make_async_copy(grad_bias.at[pl.ds(0, 1)], grad_bias_far, sems.at[2]),
        pltpu.make_async_copy(grad_proj, grad_proj_far, sems.at[3]),
    ]
    for copy in copies:
        copy.start()
    for f in range(4):
        wide[f] = grad_in[f].astype(f32)
        copies.append(pltpu.make_async_copy(wide.at[f], grad_in_far.at[f], sems.at[4 + f]))
        copies[-1].start()
    for copy in copies:
        copy.wait()


def finish(mixed, grad_out, grad_in, grad_bias, grad_proj):
    near = pl.BlockSpec(memory_space=VMEM)
    far = pl.BlockSpec(memory_space=pltpu.HBM)
    return pl.pallas_call(
        finish_kernel,
        out_shape=(
            pltpu.HBM((128, 8, 128), bf16),
            pltpu.HBM((4096, 128), f32),
            pltpu.HBM((4, 8, 128, 128), f32),
            pltpu.HBM((1, 128), f32),
            pltpu.HBM((32, 128), f32),
        ),
        in_specs=[near] * 5,
        out_specs=[far] * 5,
        scratch_shapes=[VMEM((4, 8, 128, 128), f32), DMA((8,))],
        compiler_params=pltpu.CompilerParams(vmem_limit_bytes=16 << 20),
        name="finish",
    )(mixed, grad_out, grad_in, grad_bias, grad_proj)


def local(embeddings, projection, w_in, bias, w_out, cotangent):
    results = everything(
        embeddings.reshape(64, 2, 8, 128), projection.T, w_in.reshape(32, 128, 128),
        bias.reshape(1, 128), w_out, cotangent,
    )
    mixed, grad_out, grad_in, grad_bias, grad_proj = finish(*results)
    return (
        mixed, grad_out.reshape(512, 8, 128), grad_in.reshape(4096, 128),
        grad_bias.reshape(128), grad_proj.T,
    )


def solution(mesh):
    placed = (
        P("batch", "col", "row"),
        P(),
        P("row", "col"),
        P("col"),
        P(None, "col", "row"),
        P("batch", "col", "row"),
    )
    return jax.shard_map(
        local,
        mesh=mesh,
        in_specs=placed,
        out_specs=(
            P("batch", "col", "row"),
            P("batch", "col", "row"),
            P("row", "col"),
            P("col"),
            P("row", None),
        ),
        check_vma=False,
    )
```
